128 devices in a mesh: row: 8 (over x_lo, y), col: 16 (over x_hi, z, core).
Axes of the slice: x: 4 (x_hi: 2, x_lo: 2; x = x_hi * 2 + x_lo), y: 4, z: 4, core: 2. Of those that a mesh axis runs over, the one named last changes fastest.
Arguments:
- features: bfloat16 [65536, 512], P(('row', 'col')), may hold values from -6 to 6
- tile_cols: int32 [8, 16, 32, 8], P('row', 'col'), may hold values from 0 to 63, as said below
- tile_masks: bfloat16 [8, 16, 32, 8, 128, 128], P('row', 'col'), may hold values from 0 to 1, as said below
- degree: int32 [65536], P(('row', 'col')), may hold values from 8 to 32
- owner_nodes: int32 [65536], P(('row', 'col')), may hold values from 0 to 65535, as said below
- owner_position: int32 [65536], P(('row', 'col')), may hold values from 0 to 65535, as said below
- self_weight: bfloat16 [512, 512], replicated, may hold values from -0.25 to 0.25
- neigh_weight: bfloat16 [512, 512], replicated, may hold values from -0.25 to 0.25
- cotangent: bfloat16 [65536, 512], P(('row', 'col')), may hold values from -6 to 6
Outputs:
- hidden: bfloat16 [65536, 512], P(('row', 'col'))
- grad_features: bfloat16 [65536, 512], P(('row', 'col'))
- grad_self: float32 [512, 512], replicated
- grad_neigh: float32 [512, 512], replicated
The draws below stay inside these ranges and needn't reach their ends.
Inputs may be any that keep to these rules, and one draw needn't show every extreme that they name: `tile_cols`: in each grid cell, the 8 entries of one tile row are different tile columns. `tile_masks`: entries are 0 or 1. `owner_nodes`: A permutation of the node numbers. For any two devices, the number of nodes of the first one's block that the second one holds in the owner layout is 0 or exactly 8. `owner_position`: the inverse permutation of owner_nodes.
All inputs are finite; a program needn't handle non-finite values.
Results may differ from the reference program's by a relative error of at most 0.013.
Values may be sent and summed in bfloat16 or wider, within the bound.
A program may use at most 128 MiB of HBM per device.

```python
import math
import jax
import jax.numpy as jnp
from jax import lax

F = 512
TILE = 128
ROWS_DEV = 512
TPR = 8
NODES = 65536
CAP = 8
TROWS = 32
TCOLS = 64
N_ROW = 8
N_COL = 16


def relay_tables(key):
    devices = NODES // ROWS_DEV
    relay_key = jax.random.fold_in(key, 17)
    key_list = jax.random.split(relay_key, 4)
    labels = jax.random.permutation(key_list[0], devices).astype(jnp.int32)
    inverse = jnp.zeros((devices,), jnp.int32).at[labels].set(jnp.arange(devices, dtype=jnp.int32))
    shifts = jax.random.permutation(key_list[1], devices)[:devices // 2].astype(jnp.int32)
    orders = jax.vmap(lambda one_key: jax.random.permutation(one_key, ROWS_DEV))(jax.random.split(key_list[2], devices)).astype(jnp.int32)
    placements = jax.vmap(lambda one_key: jax.random.permutation(one_key, ROWS_DEV))(jax.random.split(key_list[3], devices)).astype(jnp.int32)
    group_index = orders // CAP
    sources = jnp.arange(devices, dtype=jnp.int32)[:, None]
    owner_device = inverse[(labels[sources] + shifts[group_index]) % devices]
    position = owner_device * ROWS_DEV + placements[owner_device, orders]
    owner_position = position.reshape(-1).astype(jnp.int32)
    owner_nodes = jnp.zeros((NODES,), jnp.int32).at[owner_position].set(jnp.arange(NODES, dtype=jnp.int32))
    return (owner_nodes, owner_position)


def draw_owner_nodes(key, part):
    return relay_tables(key)[0]


def draw_owner_position(key, part):
    return relay_tables(key)[1]


def draw_tile_cols(key, part):
    cols_key = jax.random.fold_in(key, 11)
    key_list = jax.random.split(cols_key, N_ROW * N_COL * TROWS)
    picks = jax.vmap(lambda one_key: jax.random.permutation(one_key, TCOLS)[:TPR])(key_list)
    return picks.reshape(N_ROW, N_COL, TROWS, TPR).astype(jnp.int32)


def draw_tile_masks(key, part):
    mask_key = jax.random.fold_in(key, 13)
    key_pair = jax.random.split(mask_key, 2)
    shape_lead = (N_ROW, N_COL, TROWS, TPR, 1, 1)
    entries_row = float(TILE * TPR)
    expected = jax.random.uniform(key_pair[0], shape_lead, jnp.float32, 8.0, 32.0)
    density = jnp.minimum(expected / entries_row, 1.0)
    uniform_draw = jax.random.uniform(key_pair[1], (N_ROW, N_COL, TROWS, TPR, TILE, TILE), jnp.float32)
    return (uniform_draw < density).astype(jnp.float32).astype(jnp.bfloat16)


def place_ends(drawn, own_key, least, top_value):
    extent = drawn.shape
    index_at = [jax.random.randint(jax.random.fold_in(own_key, axis), (), 0, extent[axis]) for axis in range(len(extent))]
    drawn = drawn.at[tuple(index_at)].set(least)
    longest = extent.index(max(extent))
    index_at[longest] = (index_at[longest] + 1) % extent[longest]
    return drawn.at[tuple(index_at)].set(top_value)


def level_of(key, shape, cuts, low, top_value):
    level, own = 1.0, jax.random.fold_in(key, 6)
    for dim, blocks in cuts:
        steps = jnp.exp(jax.random.uniform(jax.random.fold_in(own, dim), (blocks,), jnp.float32, low / len(cuts), top_value / len(cuts)))
        level = level * jnp.repeat(steps, shape[dim] // blocks).reshape([-1 if axis == dim else 1 for axis in range(len(shape))])
    return level


def centred(own_key, dims, scale, limit, cuts=(), kind=jnp.bfloat16):
    array = scale * jax.random.normal(own_key, dims, jnp.float32)
    if cuts:
        array = array * level_of(own_key, dims, cuts, -0.22, 0.18)
    return jnp.clip(array, -limit, limit).astype(kind)


def setup_inputs(seed: int = 0) -> dict:
    streams_of = jax.random.split(jax.random.key(seed), 10)
    features = centred(streams_of[0], (NODES, F), 1.0, 6.0, ((0, 128),))
    tile_cols = draw_tile_cols(jax.random.fold_in(streams_of[9], 71), 0)
    tile_masks = draw_tile_masks(jax.random.fold_in(streams_of[9], 71), 0)
    degree = place_ends(jax.random.randint(streams_of[3], (NODES,), 8, 33), jax.random.fold_in(streams_of[3], 1), 8, 32).astype(jnp.int32)
    owner_nodes = draw_owner_nodes(jax.random.fold_in(streams_of[9], 71), 0)
    owner_position = draw_owner_position(jax.random.fold_in(streams_of[9], 71), 0)
    self_weight = centred(streams_of[6], (F, F), F ** -0.5, 0.25)
    neigh_weight = centred(streams_of[7], (F, F), F ** -0.5, 0.25)
    cotangent = centred(streams_of[8], (NODES, F), 1.0, 6.0, ((0, 128),))
    return {"features": features, "tile_cols": tile_cols, "tile_masks": tile_masks, "degree": degree, "owner_nodes": owner_nodes, "owner_position": owner_position, "self_weight": self_weight, "neigh_weight": neigh_weight, "cotangent": cotangent}


def forward_cell(pattern, columns, column_rows):
    row_tiles = column_rows.reshape(-1, TILE, F)
    chosen = row_tiles[columns]
    result = jnp.einsum('tkij,tkjf->tif', pattern.astype(jnp.float32), chosen.astype(jnp.float32), precision=lax.Precision.HIGHEST)
    return result.reshape(-1, F)

def backward_cell(pattern, columns, spread_rows):
    pieces = jnp.einsum('tkij,tif->tkjf', pattern.astype(jnp.float32), spread_rows.reshape(-1, TILE, F).astype(jnp.float32), precision=lax.Precision.HIGHEST)
    totals = jnp.zeros((TCOLS, TILE, F), jnp.float32).at[columns.reshape(-1)].add(pieces.reshape(-1, TILE, F))
    return totals.reshape(-1, F)

def rounded(values):
    return lax.optimization_barrier(values.astype(jnp.bfloat16)).astype(jnp.float32)

def reference(features, tile_cols, tile_masks, degree, owner_nodes, owner_position, self_weight, neigh_weight, cotangent):
    node_feats = features[owner_position]
    grid_feats = node_feats.reshape(N_ROW, N_COL * ROWS_DEV, F)

    def forward_column(col_index):

        def add_row(totals, row_index):
            partial_value = forward_cell(tile_masks[row_index, col_index], tile_cols[row_index, col_index], grid_feats[row_index])
            return (totals + rounded(partial_value), None)
        start_zero = jnp.zeros((N_ROW * ROWS_DEV, F), jnp.float32)
        return lax.scan(add_row, start_zero, jnp.arange(N_ROW, dtype=jnp.int32))[0]
    by_column = lax.map(forward_column, jnp.arange(N_COL, dtype=jnp.int32))
    summed_node = by_column.reshape(N_COL, N_ROW, ROWS_DEV, F).transpose(1, 0, 2, 3).reshape(NODES, F)
    summed = summed_node[owner_nodes]
    degrees = degree.astype(jnp.float32)[:, None]
    aggregate = (summed / degrees).astype(jnp.bfloat16)
    preact = jnp.dot(features, self_weight, preferred_element_type=jnp.float32) + jnp.dot(aggregate, neigh_weight, preferred_element_type=jnp.float32)
    hidden = jax.nn.silu(preact).astype(jnp.bfloat16)
    gate_value = jax.nn.sigmoid(preact)
    slopes = (cotangent.astype(jnp.float32) * gate_value * (1.0 + preact * (1.0 - gate_value))).astype(jnp.bfloat16)
    grad_scale = 1.0 / math.sqrt(NODES)
    grad_self = jnp.dot(features.T, slopes, preferred_element_type=jnp.float32) * grad_scale
    grad_neigh = jnp.dot(aggregate.T, slopes, preferred_element_type=jnp.float32) * grad_scale
    own_back = jnp.dot(slopes, self_weight.T, preferred_element_type=jnp.float32)
    spread = (jnp.dot(slopes, neigh_weight.T, preferred_element_type=jnp.float32) / degrees).astype(jnp.bfloat16)
    grid_spread = spread[owner_position].reshape(N_ROW, N_COL, ROWS_DEV, F)

    def backward_row(row_index):

        def add_col(totals, col_index):
            partial_value = backward_cell(tile_masks[row_index, col_index], tile_cols[row_index, col_index], grid_spread[:, col_index].reshape(-1, F))
            return (totals + rounded(partial_value), None)
        start_zero = jnp.zeros((N_COL * ROWS_DEV, F), jnp.float32)
        return lax.scan(add_col, start_zero, jnp.arange(N_COL, dtype=jnp.int32))[0]
    neigh_node = lax.map(backward_row, jnp.arange(N_ROW, dtype=jnp.int32)).reshape(NODES, F)
    grad_features = (own_back + neigh_node[owner_nodes]).astype(jnp.bfloat16)
    return (hidden, grad_features, grad_self, grad_neigh)
```

```python
import functools
import math

import jax
import jax.numpy as jnp
from jax import lax
from jax.experimental import pallas as pl
from jax.experimental.pallas import tpu as pltpu
from jax.sharding import PartitionSpec as P

F32 = jnp.float32
BF16 = jnp.bfloat16
VMEM_LIMIT = 60 * 1024 * 1024
ROW_T = (((0,), (0,)), ((), ()))
COL_T = (((1,), (1,)), ((), ()))


def rank_within(group_keys, order_keys):
    same_group = group_keys[:, None] == group_keys[None, :]
    earlier = order_keys[None, :] < order_keys[:, None]
    return jnp.sum(same_group & earlier, axis=1)


def params(**kw):
    return pltpu.CompilerParams(vmem_limit_bytes=VMEM_LIMIT, **kw)


def pack_kernel(flat_ref, data_ref, out_ref):
    step = pl.program_id(0)
    size = out_ref.shape[0]
    slot = lax.broadcasted_iota(jnp.int32, (size, flat_ref.shape[1]), 0) + step * size
    pick = jnp.where(slot == flat_ref[...], 1.0, 0.0).astype(BF16)
    out_ref[...] = jnp.dot(pick, data_ref[...], preferred_element_type=F32).astype(BF16)


def pack(flat, data, slots):
    rows, width = data.shape
    parts = 4
    return pl.pallas_call(
        pack_kernel,
        grid=(parts,),
        in_specs=[
            pl.BlockSpec((1, rows), lambda i: (0, 0)),
            pl.BlockSpec((rows, width), lambda i: (0, 0)),
        ],
        out_specs=pl.BlockSpec((slots // parts, width), lambda i: (i, 0)),
        out_shape=jax.ShapeDtypeStruct((slots, width), BF16),
        name="pack",
    )(flat.reshape(1, rows), data)


def unpack_kernel(flat_ref, data_ref, out_ref):
    size = out_ref.shape[0]
    slot = lax.broadcasted_iota(jnp.int32, (size, data_ref.shape[0]), 1)
    pick = jnp.where(slot == flat_ref[...], 1.0, 0.0).astype(BF16)
    out_ref[...] = jnp.dot(pick, data_ref[...], preferred_element_type=F32).astype(BF16)


def unpack(flat, data):
    slots, width = data.shape
    rows = flat.shape[0]
    parts = 4
    return pl.pallas_call(
        unpack_kernel,
        grid=(parts,),
        in_specs=[
            pl.BlockSpec((rows // parts, 1), lambda i: (i, 0)),
            pl.BlockSpec((slots, width), lambda i: (0, 0)),
        ],
        out_specs=pl.BlockSpec((rows // parts, width), lambda i: (i, 0)),
        out_shape=jax.ShapeDtypeStruct((rows, width), BF16),
        name="unpack",
    )(flat.reshape(rows, 1), data)


def gather_product_kernel(cols_ref, mask_ref, x_ref, out_ref):
    row = pl.program_id(0)
    breadth, tile = mask_ref.shape[1], mask_ref.shape[2]
    left = jnp.concatenate([mask_ref[0, k] for k in range(breadth)], axis=1)
    right = jnp.concatenate(
        [x_ref[pl.ds(pl.multiple_of(cols_ref[row, k] * tile, tile), tile), :] for k in range(breadth)], axis=0
    )
    out_ref[...] = jnp.dot(left, right, preferred_element_type=F32).astype(BF16)


def gather_product(columns, pattern, x):
    trows, breadth, tile, _ = pattern.shape
    width = x.shape[1]
    return pl.pallas_call(
        gather_product_kernel,
        grid_spec=pltpu.PrefetchScalarGridSpec(
            num_scalar_prefetch=1,
            grid=(trows,),
            in_specs=[
                pl.BlockSpec((1, breadth, tile, tile), lambda i, c: (i, 0, 0, 0)),
                pl.BlockSpec(x.shape, lambda i, c: (0, 0), pipeline_mode=pl.Buffered(1)),
            ],
            out_specs=pl.BlockSpec((tile, width), lambda i, c: (i, 0)),
        ),
        out_shape=jax.ShapeDtypeStruct((trows * tile, width), BF16),
        compiler_params=params(),
        name="gather_product",
    )(columns, pattern, x)


def scatter_product_kernel(cols_ref, mask_ref, s_ref, out_ref, total):
    row = pl.program_id(0)
    breadth, tile = mask_ref.shape[1], mask_ref.shape[2]

    @pl.when(row == 0)
    def _():
        total[...] = jnp.zeros_like(total)

    for k in range(breadth):
        piece = lax.dot_general(mask_ref[0, k], s_ref[...], ROW_T, preferred_element_type=F32)
        at = pl.ds(pl.multiple_of(cols_ref[row, k] * tile, tile), tile)
        total[at, :] += piece

    @pl.when(row == pl.num_programs(0) - 1)
    def _():
        out_ref[...] = total[...].astype(BF16)


def scatter_product(columns, pattern, spread, total_rows):
    trows, breadth, tile, _ = pattern.shape
    width = spread.shape[1]
    return pl.pallas_call(
        scatter_product_kernel,
        grid_spec=pltpu.PrefetchScalarGridSpec(
            num_scalar_prefetch=1,
            grid=(trows,),
            in_specs=[
                pl.BlockSpec((1, breadth, tile, tile), lambda i, c: (i, 0, 0, 0)),
                pl.BlockSpec((tile, width), lambda i, c: (i, 0)),
            ],
            out_specs=pl.BlockSpec((total_rows, width), lambda i, c: (0, 0), pipeline_mode=pl.Buffered(1)),
            scratch_shapes=[pltpu.VMEM((total_rows, width), F32)],
        ),
        out_shape=jax.ShapeDtypeStruct((total_rows, width), BF16),
        compiler_params=params(),
        name="scatter_product",
    )(columns, pattern, spread)


def dense_kernel(
    part_ref, x_ref, extra_ref, ws_ref, wn_ref, hidden_ref, own_ref, spread_ref, gs_ref, gn_ref
):
    step = pl.program_id(0)
    width = x_ref.shape[1]
    x = x_ref[...]
    degrees = extra_ref[:, pl.ds(width, 1)].astype(F32)
    cot = extra_ref[:, pl.ds(0, width)].astype(F32)
    summed = part_ref[0].astype(F32)
    for r in range(1, part_ref.shape[0]):
        summed = summed + part_ref[r].astype(F32)
    aggregate = (summed / degrees).astype(BF16)
    preact = jnp.dot(x, ws_ref[...], preferred_element_type=F32) + jnp.dot(
        aggregate, wn_ref[...], preferred_element_type=F32
    )
    gate = jax.nn.sigmoid(preact)
    hidden_ref[...] = (preact * gate).astype(BF16)
    slopes = (cot * gate * (1.0 + preact * (1.0 - gate))).astype(BF16)
    gs = lax.dot_general(x, slopes, ROW_T, preferred_element_type=F32)
    gn = lax.dot_general(aggregate, slopes, ROW_T, preferred_element_type=F32)

    @pl.when(step == 0)
    def _():
        gs_ref[...] = gs
        gn_ref[...] = gn

    @pl.when(step > 0)
    def _():
        gs_ref[...] += gs
        gn_ref[...] += gn

    own_ref[...] = lax.dot_general(slopes, ws_ref[...], COL_T, preferred_element_type=F32)
    spread_ref[...] = (
        lax.dot_general(slopes, wn_ref[...], COL_T, preferred_element_type=F32) / degrees
    ).astype(BF16)


def dense(parts, x, extra, ws, wn):
    rows, width = x.shape
    step = 128
    whole = lambda i: (0, 0)
    rowwise = lambda i: (i, 0)
    return pl.pallas_call(
        dense_kernel,
        grid=(rows // step,),
        in_specs=[
            pl.BlockSpec((parts.shape[0], step, width), lambda i: (0, i, 0)),
            pl.BlockSpec((step, width), rowwise),
            pl.BlockSpec((step, extra.shape[1]), rowwise),
            pl.BlockSpec((width, width), whole),
            pl.BlockSpec((width, width), whole),
        ],
        out_specs=[
            pl.BlockSpec((step, width), rowwise),
            pl.BlockSpec((step, width), rowwise),
            pl.BlockSpec((step, width), rowwise),
            pl.BlockSpec((width, width), whole),
            pl.BlockSpec((width, width), whole),
        ],
        out_shape=[
            jax.ShapeDtypeStruct((rows, width), BF16),
            jax.ShapeDtypeStruct((rows, width), F32),
            jax.ShapeDtypeStruct((rows, width), BF16),
            jax.ShapeDtypeStruct((width, width), F32),
            jax.ShapeDtypeStruct((width, width), F32),
        ],
        compiler_params=params(),
        name="dense",
    )(parts, x, extra, ws, wn)


def swap_all(data, axes):
    return lax.all_to_all(data, axes, split_axis=0, concat_axis=0, tiled=True)


def on_device(
    features, tile_cols, tile_masks, degree, owner_nodes, owner_position, self_weight, neigh_weight, cotangent
):
    rows, width = features.shape
    n_row, n_col = lax.axis_size("row"), lax.axis_size("col")
    devices = n_row * n_col
    slot_count = 2 * rows // devices
    slots = devices * slot_count
    pattern, columns = tile_masks[0, 0], tile_cols[0, 0]
    own_dest = owner_nodes // rows
    own_flat = own_dest * slot_count + rank_within(own_dest, jnp.arange(rows, dtype=jnp.int32))
    node_source = owner_position // rows
    node_flat = node_source * slot_count + rank_within(node_source, owner_position)

    both = ("row", "col")
    degree_cols = jnp.broadcast_to(degree.astype(BF16)[:, None], (rows, 128))
    node_x = unpack(node_flat, swap_all(pack(own_flat, features, slots), both))
    extra = jnp.concatenate([cotangent, degree_cols], axis=1)
    node_extra = unpack(node_flat, swap_all(pack(own_flat, extra, slots), both))
    column_x = lax.all_gather(node_x, "col", axis=0, tiled=True)
    partial_rows = gather_product(columns, pattern, column_x)
    parts = swap_all(partial_rows.reshape(n_row, rows, width), "row")
    hidden, own_back, spread, grad_self, grad_neigh = dense(parts, node_x, node_extra, self_weight, neigh_weight)
    grid_spread = lax.all_gather(spread, "row", axis=0, tiled=True)
    back = scatter_product(columns, pattern, grid_spread, n_col * rows)
    node_back = lax.psum_scatter(back, "col", scatter_dimension=0, tiled=True)
    grad_node = (own_back + node_back.astype(F32)).astype(BF16)
    hidden_out = unpack(own_flat, swap_all(pack(node_flat, hidden, slots), both))
    grad_out = unpack(own_flat, swap_all(pack(node_flat, grad_node, slots), both))
    sums = lax.psum((grad_self, grad_neigh), both)
    grad_scale = 1.0 / math.sqrt(rows * devices)
    return hidden_out, grad_out, sums[0] * grad_scale, sums[1] * grad_scale


def solution(mesh):
    both = P(("row", "col"))
    wide = P(("row", "col"), None)
    placed = (
        wide,
        P("row", "col", None, None),
        P("row", "col", None, None, None, None),
        both,
        both,
        both,
        P(),
        P(),
        wide,
    )
    return jax.shard_map(
        on_device, mesh=mesh, in_specs=placed, out_specs=(wide, wide, P(), P()), check_vma=False
    )
```

```python
import math

import jax
import jax.numpy as jnp
from jax import lax
from jax.experimental import pallas as pl
from jax.experimental.pallas import tpu as pltpu
from jax.sharding import PartitionSpec as P

F32 = jnp.float32
BF16 = jnp.bfloat16
MESH = pl.DeviceIdType.MESH
VMEM_LIMIT = 60 * 1024 * 1024
ROW_T = (((0,), (0,)), ((), ()))
COL_T = (((1,), (1,)), ((), ()))


def rank_within(group_keys, order_keys):
    same_group = group_keys[:, None] == group_keys[None, :]
    earlier = order_keys[None, :] < order_keys[:, None]
    return jnp.sum(same_group & earlier, axis=1)


def params(**kw):
    return pltpu.CompilerParams(vmem_limit_bytes=VMEM_LIMIT, **kw)


def pack_kernel(flat_ref, data_ref, out_ref):
    step = pl.program_id(0)
    size = out_ref.shape[0]
    slot = lax.broadcasted_iota(jnp.int32, (size, flat_ref.shape[1]), 0) + step * size
    pick = jnp.where(slot == flat_ref[...], 1.0, 0.0).astype(BF16)
    out_ref[...] = jnp.dot(pick, data_ref[...], preferred_element_type=F32).astype(BF16)


def pack(flat, data, slots):
    rows, width = data.shape
    parts = 4
    return pl.pallas_call(
        pack_kernel,
        grid=(parts,),
        in_specs=[
            pl.BlockSpec((1, rows), lambda i: (0, 0)),
            pl.BlockSpec((rows, width), lambda i: (0, 0)),
        ],
        out_specs=pl.BlockSpec((slots // parts, width), lambda i: (i, 0)),
        out_shape=jax.ShapeDtypeStruct((slots, width), BF16),
        name="pack",
    )(flat.reshape(1, rows), data)


def unpack_kernel(flat_ref, data_ref, out_ref):
    size = out_ref.shape[0]
    slot = lax.broadcasted_iota(jnp.int32, (size, data_ref.shape[0]), 1)
    pick = jnp.where(slot == flat_ref[...], 1.0, 0.0).astype(BF16)
    out_ref[...] = jnp.dot(pick, data_ref[...], preferred_element_type=F32).astype(BF16)


def unpack(flat, data):
    slots, width = data.shape
    rows = flat.shape[0]
    parts = 4
    return pl.pallas_call(
        unpack_kernel,
        grid=(parts,),
        in_specs=[
            pl.BlockSpec((rows // parts, 1), lambda i: (i, 0)),
            pl.BlockSpec((slots, width), lambda i: (0, 0)),
        ],
        out_specs=pl.BlockSpec((rows // parts, width), lambda i: (i, 0)),
        out_shape=jax.ShapeDtypeStruct((rows, width), BF16),
        name="unpack",
    )(flat.reshape(rows, 1), data)


def unpack_tiles_kernel(flat_ref, data_ref, out_ref):
    size = out_ref.shape[2]
    slot = lax.broadcasted_iota(jnp.int32, (size, data_ref.shape[0]), 1)
    pick = jnp.where(slot == flat_ref[...], 1.0, 0.0).astype(BF16)
    rows = jnp.dot(pick, data_ref[...], preferred_element_type=F32).astype(BF16)
    for c in range(4):
        out_ref[c, 0] = rows[:, c * 128 : (c + 1) * 128]


def unpack_tiles(flat, data):
    slots, width = data.shape
    rows = flat.shape[0]
    return pl.pallas_call(
        unpack_tiles_kernel,
        grid=(4,),
        in_specs=[
            pl.BlockSpec((rows // 4, 1), lambda i: (i, 0)),
            pl.BlockSpec((slots, width), lambda i: (0, 0)),
        ],
        out_specs=pl.BlockSpec((4, 1, 128, 128), lambda i: (0, i, 0, 0)),
        out_shape=jax.ShapeDtypeStruct((4, 4, 128, 128), BF16),
        name="unpack_tiles",
    )(flat.reshape(rows, 1), data)

def place():
    r, c = lax.axis_index("row"), lax.axis_index("col")
    return r // 4, r % 4, c // 8, (c // 2) % 4, c % 2


def at_device(xl, y, xh, z, k):
    return (xl * 4 + y, xh * 8 + z * 2 + k)


def meet(peers):
    barrier = pltpu.get_barrier_semaphore()
    for peer in peers:
        pl.semaphore_signal(barrier, inc=1, device_id=peer, device_id_type=MESH)
    pl.semaphore_wait(barrier, len(peers))


def all_peers():
    xl, y, xh, z, k = place()
    peers = [
        at_device(1 - xl, y, xh, z, k),
        at_device(xl, y, 1 - xh, z, k),
        at_device(xl, y, xh, z, 1 - k),
    ]
    for d in (1, 2, 3):
        peers.append(at_device(xl, (y + d) % 4, xh, z, k))
        peers.append(at_device(xl, y, xh, (z + d) % 4, k))
    return peers


class Copies:
    def __init__(self, send, recv):
        self.send, self.recv, self.used, self.started = send, recv, 0, []

    def remote(self, src, dst, device):
        i, self.used = self.used, self.used + 1
        copy = pltpu.make_async_remote_copy(
            src_ref=src, dst_ref=dst, send_sem=self.send.at[i], recv_sem=self.recv.at[i],
            device_id=device, device_id_type=MESH,
        )
        copy.start()
        self.started.append(copy)
        return copy

    def local(self, src, dst):
        i, self.used = self.used, self.used + 1
        copy = pltpu.make_async_copy(src, dst, self.recv.at[i])
        copy.start()
        return copy

    def finish(self):
        for copy in self.started:
            copy.wait_send()


FAR_FIRST = (2, 1, 3)


def forward_kernel(cols_ref, x_ref, mask_hbm, out_ref, mask, *rest):
    held, part, near, cross, crossed, (send, recv) = (
        rest[0:4], rest[4:8], rest[8:12], rest[12:16], rest[16:20], rest[20:22]
    )
    xl, y, xh, z, k = place()
    copies = Copies(send, recv)
    mask_copy = copies.local(mask_hbm, mask)
    meet(all_peers())
    tiles = lambda slot: pl.ds(slot * 4, 4)
    mine, pair = k * 8 + xh * 4 + z, k * 8 + (1 - xh) * 4 + z
    gathered, over, swap, row_copies, cross_copy = [[] for _ in range(4)], {}, {}, {}, {}

    def own(c):
        gathered[c].append(copies.local(x_ref.at[c], held[c].at[tiles(mine)]))
        over[c] = copies.remote(x_ref.at[c], held[c].at[tiles(mine)], at_device(xl, y, 1 - xh, z, k))
        for d in FAR_FIRST:
            to = at_device(xl, y, xh, (z + d) % 4, k)
            gathered[c].append(copies.remote(x_ref.at[c], held[c].at[tiles(mine)], to))

    def onward(c):
        over[c].wait_recv()
        for d in FAR_FIRST:
            to = at_device(xl, y, xh, (z + d) % 4, k)
            gathered[c].append(copies.remote(held[c].at[tiles(pair)], held[c].at[tiles(pair)], to))

    def swap_cores(c):
        gathered[c][0].wait()
        for copy in gathered[c][1:]:
            copy.wait_recv()
        half = held[c].at[pl.ds(k * 32, 32)]
        swap[c] = copies.remote(half, half, at_device(xl, y, xh, z, 1 - k))

    def product(c):
        swap[c].wait_recv()
        row_copies[c] = []
        for d in FAR_FIRST + (0,):
            to_y = (y + d) % 4

            def one(q, carry):
                t = (q // 4) * 16 + to_y * 4 + q % 4
                left = jnp.concatenate([mask[t * 8 + j] for j in range(8)], axis=1)
                right = jnp.concatenate([held[c][cols_ref[t * 8 + j]] for j in range(8)], axis=0)
                part[c][to_y * 8 + q] = jnp.dot(left, right, preferred_element_type=F32).astype(BF16)
                return carry

            lax.fori_loop(0, 8, one, 0)
            if d:
                i = FAR_FIRST.index(d)
                row_copies[c].append(
                    copies.remote(
                        part[c].at[pl.ds(to_y * 8, 8)], near[c].at[pl.ds(i * 8, 8)], at_device(xl, to_y, xh, z, k)
                    )
                )

    def row_sum(c, side, i):
        total = part[c][y * 8 + side * 4 + i].astype(F32)
        for n in range(3):
            total = total + near[c][n * 8 + side * 4 + i].astype(F32)
        return total

    def sum_rows(c):
        for copy in row_copies[c]:
            copy.wait_recv()

        def one(i, carry):
            cross[c][i] = row_sum(c, 1 - xl, i).astype(BF16)
            return carry

        lax.fori_loop(0, 4, one, 0)
        cross_copy[c] = copies.remote(cross[c], crossed[c], at_device(1 - xl, y, xh, z, k))

    def sum_cross(c):
        cross_copy[c].wait_recv()

        def one(i, carry):
            out_ref[c, i] = row_sum(c, xl, i) + crossed[c][i].astype(F32)
            return carry

        lax.fori_loop(0, 4, one, 0)

    own(0)
    onward(0)
    own(1)
    onward(1)
    swap_cores(0)
    own(2)
    mask_copy.wait()
    product(0)
    onward(2)
    swap_cores(1)
    own(3)
    product(1)
    onward(3)
    swap_cores(2)
    sum_rows(0)
    product(2)
    swap_cores(3)
    sum_rows(1)
    sum_cross(0)
    product(3)
    sum_rows(2)
    sum_cross(1)
    sum_rows(3)
    sum_cross(2)
    sum_cross(3)
    copies.finish()


def remote_params(ident):
    return params(collective_id=ident, has_side_effects=True)


SMEM_SPEC = pl.BlockSpec(memory_space=pltpu.SMEM)
VMEM_SPEC = pl.BlockSpec(memory_space=pltpu.VMEM)
ANY_SPEC = pl.BlockSpec(memory_space=pl.ANY)


def tile_buffer(count):
    return pltpu.VMEM((count, 128, 128), BF16)


def forward_exchange(cols, x, masks):
    return pl.pallas_call(
        forward_kernel,
        in_specs=[SMEM_SPEC, VMEM_SPEC, ANY_SPEC],
        out_specs=VMEM_SPEC,
        out_shape=jax.ShapeDtypeStruct(x.shape, F32),
        scratch_shapes=[tile_buffer(256)]
        + [tile_buffer(64)] * 4
        + [tile_buffer(32)] * 4
        + [tile_buffer(24)] * 4
        + [tile_buffer(4)] * 8
        + [pltpu.SemaphoreType.DMA((64,)), pltpu.SemaphoreType.DMA((64,))],
        compiler_params=remote_params(0),
        name="forward_exchange",
    )(cols, x, masks)


def backward_kernel(pick_ref, from_ref, keep_ref, last_ref, some_ref, s_ref, mask_hbm, out_ref, mask, chain, *rest):
    held, block, traded, paired, near, cross, crossed, (send, recv) = (
        rest[0:4], rest[4:8], rest[8:12], rest[12:16], rest[16:20], rest[20:24], rest[24:28], rest[28:30]
    )
    xl, y, xh, z, k = place()
    copies = Copies(send, recv)
    mask_copy = copies.local(mask_hbm, mask)
    meet(all_peers())
    tiles = lambda slot: pl.ds(slot * 4, 4)
    mine, pair = xl * 4 + y, (1 - xl) * 4 + y
    gathered, over, trade, col_copies, cross_copy = [[] for _ in range(4)], {}, {}, {}, {}

    def own(c):
        gathered[c].append(copies.local(s_ref.at[c], held[c].at[tiles(mine)]))
        over[c] = copies.remote(s_ref.at[c], held[c].at[tiles(mine)], at_device(1 - xl, y, xh, z, k))
        for d in FAR_FIRST:
            to = at_device(xl, (y + d) % 4, xh, z, k)
            gathered[c].append(copies.remote(s_ref.at[c], held[c].at[tiles(mine)], to))

    def onward(c):
        over[c].wait_recv()
        for d in FAR_FIRST:
            to = at_device(xl, (y + d) % 4, xh, z, k)
            gathered[c].append(copies.remote(held[c].at[tiles(pair)], held[c].at[tiles(pair)], to))

    def product(c):
        gathered[c][0].wait()
        for copy in gathered[c][1:]:
            copy.wait_recv()

        def one(g, total):
            for u in range(8):
                e = g * 8 + u
                piece = jnp.dot(held[c][from_ref[e]], mask[pick_ref[e]], preferred_element_type=F32)
                total = total * keep_ref[e] + piece
                chain[e] = total.astype(BF16)
            return total

        lax.fori_loop(0, 32, one, jnp.zeros((128, 128), F32))

        def settle(p, carry):
            block[c][p] = (chain[last_ref[p]].astype(F32) * some_ref[p]).astype(BF16)
            return carry

        lax.fori_loop(0, 64, settle, 0)
        trade[c] = copies.remote(
            block[c].at[pl.ds((1 - k) * 32, 32)], traded[c], at_device(xl, y, xh, z, 1 - k)
        )

    def sum_cores(c):
        trade[c].wait_recv()

        def one(i, carry):
            paired[c][i] = (block[c][k * 32 + i].astype(F32) + traded[c][i].astype(F32)).astype(BF16)
            return carry

        lax.fori_loop(0, 32, one, 0)
        col_copies[c] = []
        for i, d in enumerate(FAR_FIRST):
            to_z = (z + d) % 4
            col_copies[c].append(
                copies.remote(
                    paired[c].at[pl.ds(to_z * 8, 8)], near[c].at[pl.ds(i * 8, 8)], at_device(xl, y, xh, to_z, k)
                )
            )

    def col_sum(c, side, i):
        total = paired[c][z * 8 + side * 4 + i].astype(F32)
        for n in range(3):
            total = total + near[c][n * 8 + side * 4 + i].astype(F32)
        return total

    def sum_cols(c):
        for copy in col_copies[c]:
            copy.wait_recv()

        def one(i, carry):
            cross[c][i] = col_sum(c, 1 - xh, i).astype(BF16)
            return carry

        lax.fori_loop(0, 4, one, 0)
        cross_copy[c] = copies.remote(cross[c], crossed[c], at_device(xl, y, 1 - xh, z, k))

    def sum_cross(c):
        cross_copy[c].wait_recv()

        def one(i, carry):
            out_ref[c, i] = col_sum(c, xh, i) + crossed[c][i].astype(F32)
            return carry

        lax.fori_loop(0, 4, one, 0)

    own(0)
    onward(0)
    own(1)
    onward(1)
    own(2)
    mask_copy.wait()
    product(0)
    onward(2)
    own(3)
    sum_cores(0)
    product(1)
    onward(3)
    sum_cores(1)
    sum_cols(0)
    product(2)
    sum_cores(2)
    sum_cols(1)
    sum_cross(0)
    product(3)
    sum_cores(3)
    sum_cols(2)
    sum_cross(1)
    sum_cols(3)
    sum_cross(2)
    sum_cross(3)
    copies.finish()


def backward_exchange(tables, s, masks):
    return pl.pallas_call(
        backward_kernel,
        in_specs=[SMEM_SPEC] * 5 + [VMEM_SPEC, ANY_SPEC],
        out_specs=VMEM_SPEC,
        out_shape=jax.ShapeDtypeStruct(s.shape, F32),
        scratch_shapes=[tile_buffer(256), tile_buffer(256)]
        + [tile_buffer(32)] * 4
        + [tile_buffer(64)] * 4
        + [tile_buffer(32)] * 8
        + [tile_buffer(24)] * 4
        + [tile_buffer(4)] * 8
        + [pltpu.SemaphoreType.DMA((64,)), pltpu.SemaphoreType.DMA((64,))],
        compiler_params=remote_params(1),
        name="backward_exchange",
    )(*tables, s, masks)


def column_order(columns):
    flat = columns.reshape(-1)
    count = flat.shape[0]
    block = flat // 4
    xh, z, k = block // 8, (block // 2) % 4, block % 2
    held_tile = (k * 8 + xh * 4 + z) * 4 + flat % 4
    back_tile = (k * 8 + z * 2 + xh) * 4 + flat % 4
    entry = jnp.arange(count, dtype=jnp.int32)
    key = back_tile * count + entry
    rank = jnp.sum((key[None, :] < key[:, None]).astype(jnp.int32), axis=1)
    hit = rank[None, :] == entry[:, None]
    pick = jnp.sum(jnp.where(hit, entry[None, :], 0), axis=1)
    sorted_tile = jnp.sum(jnp.where(hit, back_tile[None, :], 0), axis=1)
    before = jnp.concatenate([jnp.full((1,), -1, jnp.int32), sorted_tile[:-1]])
    keep = (sorted_tile == before).astype(F32)
    spot = jnp.arange(64, dtype=jnp.int32)
    upto = jnp.sum((back_tile[None, :] <= spot[:, None]).astype(jnp.int32), axis=1)
    some = jnp.any(back_tile[None, :] == spot[:, None], axis=1).astype(F32)
    last = jnp.maximum(upto - 1, 0)
    return held_tile, (pick, pick // 8, keep, last, some)


def dense_kernel(
    sum_ref, x_ref, extra_ref, ws_ref, wn_ref, hidden_ref, own_ref, spread_ref, gs_ref, gn_ref
):
    step = pl.program_id(0)
    width = hidden_ref.shape[1]
    x = jnp.concatenate([x_ref[c, 0] for c in range(4)], axis=1)
    degrees = extra_ref[:, pl.ds(width, 1)].astype(F32)
    cot = extra_ref[:, pl.ds(0, width)].astype(F32)
    summed = jnp.concatenate([sum_ref[c, 0] for c in range(4)], axis=1)
    aggregate = (summed / degrees).astype(BF16)
    preact = jnp.dot(x, ws_ref[...], preferred_element_type=F32) + jnp.dot(
        aggregate, wn_ref[...], preferred_element_type=F32
    )
    gate = jax.nn.sigmoid(preact)
    hidden_ref[...] = (preact * gate).astype(BF16)
    slopes = (cot * gate * (1.0 + preact * (1.0 - gate))).astype(BF16)
    gs = lax.dot_general(x, slopes, ROW_T, preferred_element_type=F32)
    gn = lax.dot_general(aggregate, slopes, ROW_T, preferred_element_type=F32)

    @pl.when(step == 0)
    def _():
        gs_ref[...] = gs
        gn_ref[...] = gn

    @pl.when(step > 0)
    def _():
        gs_ref[...] += gs
        gn_ref[...] += gn

    own_ref[...] = lax.dot_general(slopes, ws_ref[...], COL_T, preferred_element_type=F32)
    spread = lax.dot_general(slopes, wn_ref[...], COL_T, preferred_element_type=F32) / degrees
    for c in range(4):
        spread_ref[c, 0] = spread[:, c * 128 : (c + 1) * 128].T.astype(BF16)


def dense(summed, x, extra, ws, wn):
    rows, width = extra.shape[0], ws.shape[0]
    step = 128
    whole = lambda i: (0, 0)
    rowwise = lambda i: (i, 0)
    tiled = pl.BlockSpec((4, 1, step, 128), lambda i: (0, i, 0, 0))
    return pl.pallas_call(
        dense_kernel,
        grid=(rows // step,),
        in_specs=[
            tiled,
            tiled,
            pl.BlockSpec((step, extra.shape[1]), rowwise),
            pl.BlockSpec((width, width), whole),
            pl.BlockSpec((width, width), whole),
        ],
        out_specs=[
            pl.BlockSpec((step, width), rowwise),
            pl.BlockSpec((step, width), rowwise),
            tiled,
            pl.BlockSpec((width, width), whole),
            pl.BlockSpec((width, width), whole),
        ],
        out_shape=[
            jax.ShapeDtypeStruct((rows, width), BF16),
            jax.ShapeDtypeStruct((rows, width), F32),
            jax.ShapeDtypeStruct(x.shape, BF16),
            jax.ShapeDtypeStruct((width, width), F32),
            jax.ShapeDtypeStruct((width, width), F32),
        ],
        compiler_params=params(),
        name="dense",
    )(summed, x, extra, ws, wn)


def join_kernel(own_ref, back_ref, out_ref):
    back = jnp.concatenate([back_ref[c, 0].T for c in range(4)], axis=1)
    out_ref[...] = (own_ref[...] + back).astype(BF16)


def join(own_back, back):
    rows, width = own_back.shape
    return pl.pallas_call(
        join_kernel,
        grid=(rows // 128,),
        in_specs=[
            pl.BlockSpec((128, width), lambda i: (i, 0)),
            pl.BlockSpec((4, 1, 128, 128), lambda i: (0, i, 0, 0)),
        ],
        out_specs=pl.BlockSpec((128, width), lambda i: (i, 0)),
        out_shape=jax.ShapeDtypeStruct((rows, width), BF16),
        name="join",
    )(own_back, back)


def swap_all(data, axes):
    return lax.all_to_all(data, axes, split_axis=0, concat_axis=0, tiled=True)


def on_device(
    features, tile_cols, tile_masks, degree, owner_nodes, owner_position, self_weight, neigh_weight, cotangent
):
    rows, width = features.shape
    n_row, n_col = lax.axis_size("row"), lax.axis_size("col")
    devices = n_row * n_col
    slot_count = 2 * rows // devices
    slots = devices * slot_count
    masks = tile_masks.reshape(256, 128, 128)
    own_dest = owner_nodes // rows
    own_flat = own_dest * slot_count + rank_within(own_dest, jnp.arange(rows, dtype=jnp.int32))
    node_source = owner_position // rows
    node_flat = node_source * slot_count + rank_within(node_source, owner_position)
    cols, tables = column_order(tile_cols[0, 0])

    both = ("row", "col")
    degree_cols = jnp.broadcast_to(degree.astype(BF16)[:, None], (rows, 128))
    node_x = unpack_tiles(node_flat, swap_all(pack(own_flat, features, slots), both))
    extra = jnp.concatenate([cotangent, degree_cols], axis=1)
    node_extra = unpack(node_flat, swap_all(pack(own_flat, extra, slots), both))
    summed = forward_exchange(cols, node_x, masks)
    hidden, own_back, spread, grad_self, grad_neigh = dense(summed, node_x, node_extra, self_weight, neigh_weight)
    sums = lax.psum((grad_self, grad_neigh), both)
    back = backward_exchange(tables, spread, masks)
    grad_node = join(own_back, back)
    hidden_out = unpack(own_flat, swap_all(pack(node_flat, hidden, slots), both))
    grad_out = unpack(own_flat, swap_all(pack(node_flat, grad_node, slots), both))
    grad_scale = 1.0 / math.sqrt(rows * devices)
    return hidden_out, grad_out, sums[0] * grad_scale, sums[1] * grad_scale


def solution(mesh):
    both = P(("row", "col"))
    wide = P(("row", "col"), None)
    placed = (
        wide,
        P("row", "col", None, None),
        P("row", "col", None, None, None, None),
        both,
        both,
        both,
        P(),
        P(),
        wide,
    )
    return jax.shard_map(
        on_device, mesh=mesh, in_specs=placed, out_specs=(wide, wide, P(), P()), check_vma=False
    )
```

```python
import functools
import math

import jax
import jax.numpy as jnp
from jax import lax
from jax.experimental import pallas as pl
from jax.experimental.pallas import tpu as pltpu
from jax.sharding import PartitionSpec as P

F32 = jnp.float32
BF16 = jnp.bfloat16
MESH = pl.DeviceIdType.MESH
VMEM_LIMIT = 60 * 1024 * 1024
ROW_T = (((0,), (0,)), ((), ()))
COL_T = (((1,), (1,)), ((), ()))


def rank_within(group_keys, order_keys):
    same_group = group_keys[:, None] == group_keys[None, :]
    earlier = order_keys[None, :] < order_keys[:, None]
    return jnp.sum(same_group & earlier, axis=1)


def params(**kw):
    return pltpu.CompilerParams(vmem_limit_bytes=VMEM_LIMIT, **kw)


def pack_kernel(flat_ref, data_ref, out_ref):
    step = pl.program_id(0)
    size = out_ref.shape[0]
    slot = lax.broadcasted_iota(jnp.int32, (size, flat_ref.shape[1]), 0) + step * size
    pick = jnp.where(slot == flat_ref[...], 1.0, 0.0).astype(BF16)
    out_ref[...] = jnp.dot(pick, data_ref[...], preferred_element_type=F32).astype(BF16)


def pack(flat, data, slots):
    rows, width = data.shape
    parts = 4
    return pl.pallas_call(
        pack_kernel,
        grid=(parts,),
        in_specs=[
            pl.BlockSpec((1, rows), lambda i: (0, 0)),
            pl.BlockSpec((rows, width), lambda i: (0, 0)),
        ],
        out_specs=pl.BlockSpec((slots // parts, width), lambda i: (i, 0)),
        out_shape=jax.ShapeDtypeStruct((slots, width), BF16),
        name="pack",
    )(flat.reshape(1, rows), data)


def unpack_kernel(flat_ref, data_ref, out_ref):
    size = out_ref.shape[0]
    slot = lax.broadcasted_iota(jnp.int32, (size, data_ref.shape[0]), 1)
    pick = jnp.where(slot == flat_ref[...], 1.0, 0.0).astype(BF16)
    out_ref[...] = jnp.dot(pick, data_ref[...], preferred_element_type=F32).astype(BF16)


def unpack(flat, data):
    slots, width = data.shape
    rows = flat.shape[0]
    parts = 4
    return pl.pallas_call(
        unpack_kernel,
        grid=(parts,),
        in_specs=[
            pl.BlockSpec((rows // parts, 1), lambda i: (i, 0)),
            pl.BlockSpec((slots, width), lambda i: (0, 0)),
        ],
        out_specs=pl.BlockSpec((rows // parts, width), lambda i: (i, 0)),
        out_shape=jax.ShapeDtypeStruct((rows, width), BF16),
        name="unpack",
    )(flat.reshape(rows, 1), data)


def unpack_tiles_kernel(flat_ref, data_ref, out_ref):
    size = out_ref.shape[2]
    slot = lax.broadcasted_iota(jnp.int32, (size, data_ref.shape[0]), 1)
    pick = jnp.where(slot == flat_ref[...], 1.0, 0.0).astype(BF16)
    rows = jnp.dot(pick, data_ref[...], preferred_element_type=F32).astype(BF16)
    for c in range(4):
        out_ref[c, 0] = rows[:, c * 128 : (c + 1) * 128]


def unpack_tiles(flat, data):
    slots, width = data.shape
    rows = flat.shape[0]
    return pl.pallas_call(
        unpack_tiles_kernel,
        grid=(4,),
        in_specs=[
            pl.BlockSpec((rows // 4, 1), lambda i: (i, 0)),
            pl.BlockSpec((slots, width), lambda i: (0, 0)),
        ],
        out_specs=pl.BlockSpec((4, 1, 128, 128), lambda i: (0, i, 0, 0)),
        out_shape=jax.ShapeDtypeStruct((4, 4, 128, 128), BF16),
        name="unpack_tiles",
    )(flat.reshape(rows, 1), data)

def place():
    r, c = lax.axis_index("row"), lax.axis_index("col")
    return r // 4, r % 4, c // 8, (c // 2) % 4, c % 2


def at_device(xl, y, xh, z, k):
    return (xl * 4 + y, xh * 8 + z * 2 + k)


def meet(peers):
    barrier = pltpu.get_barrier_semaphore()
    for peer in peers:
        pl.semaphore_signal(barrier, inc=1, device_id=peer, device_id_type=MESH)
    pl.semaphore_wait(barrier, len(peers))


def all_peers():
    xl, y, xh, z, k = place()
    peers = [
        at_device(1 - xl, y, xh, z, k),
        at_device(xl, y, 1 - xh, z, k),
        at_device(1 - xl, y, 1 - xh, z, k),
        at_device(xl, y, xh, z, 1 - k),
    ]
    for d in (1, 2, 3):
        peers.append(at_device(xl, (y + d) % 4, xh, z, k))
        peers.append(at_device(xl, y, xh, (z + d) % 4, k))
    return peers


class Copies:
    def __init__(self, send, recv):
        self.send, self.recv, self.used, self.started = send, recv, 0, []

    def remote(self, src, dst, device):
        i, self.used = self.used, self.used + 1
        copy = pltpu.make_async_remote_copy(
            src_ref=src, dst_ref=dst, send_sem=self.send.at[i], recv_sem=self.recv.at[i],
            device_id=device, device_id_type=MESH,
        )
        copy.start()
        self.started.append(copy)
        return copy

    def local(self, src, dst):
        i, self.used = self.used, self.used + 1
        copy = pltpu.make_async_copy(src, dst, self.recv.at[i])
        copy.start()
        return copy

    def finish(self):
        for copy in self.started:
            copy.wait_send()


FAR_FIRST = (2, 1, 3)


def forward_kernel(cols_ref, x_ref, mask_hbm, out_ref, mask, *rest):
    held, part, near, cross, crossed, (send, recv) = (
        rest[0:4], rest[4:8], rest[8:12], rest[12:16], rest[16:20], rest[20:22]
    )
    xl, y, xh, z, k = place()
    copies = Copies(send, recv)
    mask_copy = copies.local(mask_hbm, mask)
    meet(all_peers())
    tiles = lambda slot: pl.ds(slot * 4, 4)
    mine, pair = k * 8 + xh * 4 + z, k * 8 + (1 - xh) * 4 + z
    gathered, over, swap, row_copies, cross_copy = [[] for _ in range(4)], {}, {}, {}, {}

    def own(c):
        gathered[c].append(copies.local(x_ref.at[c], held[c].at[tiles(mine)]))
        over[c] = copies.remote(x_ref.at[c], held[c].at[tiles(mine)], at_device(xl, y, 1 - xh, z, k))
        for d in FAR_FIRST:
            to = at_device(xl, y, xh, (z + d) % 4, k)
            gathered[c].append(copies.remote(x_ref.at[c], held[c].at[tiles(mine)], to))

    def onward(c):
        over[c].wait_recv()
        for d in FAR_FIRST:
            to = at_device(xl, y, xh, (z + d) % 4, k)
            gathered[c].append(copies.remote(held[c].at[tiles(pair)], held[c].at[tiles(pair)], to))

    def swap_cores(c):
        gathered[c][0].wait()
        for copy in gathered[c][1:]:
            copy.wait_recv()
        half = held[c].at[pl.ds(k * 32, 32)]
        swap[c] = copies.remote(half, half, at_device(xl, y, xh, z, 1 - k))

    def product(c):
        swap[c].wait_recv()
        row_copies[c] = []
        for d in FAR_FIRST + (0,):
            to_y = (y + d) % 4

            def one(q, carry):
                t = (q // 4) * 16 + to_y * 4 + q % 4
                left = jnp.concatenate([mask[t * 8 + j] for j in range(8)], axis=1)
                right = jnp.concatenate([held[c][cols_ref[t * 8 + j]] for j in range(8)], axis=0)
                part[c][to_y * 8 + q] = jnp.dot(left, right, preferred_element_type=F32).astype(BF16)
                return carry

            lax.fori_loop(0, 8, one, 0)
            if d:
                i = FAR_FIRST.index(d)
                row_copies[c].append(
                    copies.remote(
                        part[c].at[pl.ds(to_y * 8, 8)], near[c].at[pl.ds(i * 8, 8)], at_device(xl, to_y, xh, z, k)
                    )
                )

    def row_sum(c, side, i):
        total = part[c][y * 8 + side * 4 + i].astype(F32)
        for n in range(3):
            total = total + near[c][n * 8 + side * 4 + i].astype(F32)
        return total

    def sum_rows(c):
        for copy in row_copies[c]:
            copy.wait_recv()

        def one(i, carry):
            cross[c][i] = row_sum(c, 1 - xl, i).astype(BF16)
            return carry

        lax.fori_loop(0, 4, one, 0)
        cross_copy[c] = copies.remote(cross[c], crossed[c], at_device(1 - xl, y, xh, z, k))

    def sum_cross(c):
        cross_copy[c].wait_recv()

        def one(i, carry):
            out_ref[c, i] = row_sum(c, xl, i) + crossed[c][i].astype(F32)
            return carry

        lax.fori_loop(0, 4, one, 0)

    own(0)
    onward(0)
    own(1)
    onward(1)
    swap_cores(0)
    own(2)
    mask_copy.wait()
    product(0)
    onward(2)
    swap_cores(1)
    own(3)
    product(1)
    onward(3)
    swap_cores(2)
    sum_rows(0)
    product(2)
    swap_cores(3)
    sum_rows(1)
    sum_cross(0)
    product(3)
    sum_rows(2)
    sum_cross(1)
    sum_rows(3)
    sum_cross(2)
    sum_cross(3)
    copies.finish()


def remote_params(ident):
    return params(collective_id=ident, has_side_effects=True)


SMEM_SPEC = pl.BlockSpec(memory_space=pltpu.SMEM)
VMEM_SPEC = pl.BlockSpec(memory_space=pltpu.VMEM)
ANY_SPEC = pl.BlockSpec(memory_space=pl.ANY)


def tile_buffer(count):
    return pltpu.VMEM((count, 128, 128), BF16)


def forward_exchange(cols, x, masks):
    return pl.pallas_call(
        forward_kernel,
        in_specs=[SMEM_SPEC, VMEM_SPEC, ANY_SPEC],
        out_specs=VMEM_SPEC,
        out_shape=jax.ShapeDtypeStruct(x.shape, F32),
        scratch_shapes=[tile_buffer(256)]
        + [tile_buffer(64)] * 4
        + [tile_buffer(32)] * 4
        + [tile_buffer(24)] * 4
        + [tile_buffer(4)] * 8
        + [pltpu.SemaphoreType.DMA((64,)), pltpu.SemaphoreType.DMA((64,))],
        compiler_params=remote_params(0),
        name="forward_exchange",
    )(cols, x, masks)


def backward_kernel(scale, pick_ref, from_ref, keep_ref, last_ref, some_ref, s_ref, g_ref, mask_hbm, out_ref, sum_ref, mask, chain, *rest):
    held, block, traded, paired, near, cross, crossed, (send, recv) = (
        rest[0:4], rest[4:8], rest[8:12], rest[12:16], rest[16:20], rest[20:24], rest[24:28], rest[28:30]
    )
    g_core, g_traded, g_half, g_quarter, g_part, g_eighth, g_piece = rest[30:37]
    xl, y, xh, z, k = place()
    copies = Copies(send, recv)
    mask_copy = copies.local(mask_hbm, mask)
    meet(all_peers())
    tiles = lambda slot: pl.ds(slot * 4, 4)
    mine, pair = xl * 4 + y, (1 - xl) * 4 + y
    gathered, over, trade, col_copies, cross_copy = [[] for _ in range(4)], {}, {}, {}, {}

    def own(c):
        gathered[c].append(copies.local(s_ref.at[c], held[c].at[tiles(mine)]))
        over[c] = copies.remote(s_ref.at[c], held[c].at[tiles(mine)], at_device(1 - xl, y, xh, z, k))
        for d in FAR_FIRST:
            to = at_device(xl, (y + d) % 4, xh, z, k)
            gathered[c].append(copies.remote(s_ref.at[c], held[c].at[tiles(mine)], to))

    def onward(c):
        over[c].wait_recv()
        for d in FAR_FIRST:
            to = at_device(xl, (y + d) % 4, xh, z, k)
            gathered[c].append(copies.remote(held[c].at[tiles(pair)], held[c].at[tiles(pair)], to))

    def product(c, between):
        gathered[c][0].wait()
        for copy in gathered[c][1:]:
            copy.wait_recv()

        def one(g, total):
            for u in range(8):
                e = g * 8 + u
                piece = jnp.dot(held[c][from_ref[e]], mask[pick_ref[e]], preferred_element_type=F32)
                total = total * keep_ref[e] + piece
                chain[e] = total.astype(BF16)
            return total

        half = lax.fori_loop(0, 16, one, jnp.zeros((128, 128), F32))
        between()
        lax.fori_loop(16, 32, one, half)

        def settle(p, carry):
            block[c][p] = (chain[last_ref[p]].astype(F32) * some_ref[p]).astype(BF16)
            return carry

        lax.fori_loop(0, 64, settle, 0)
        trade[c] = copies.remote(
            block[c].at[pl.ds((1 - k) * 32, 32)], traded[c], at_device(xl, y, xh, z, 1 - k)
        )

    def sum_cores(c):
        trade[c].wait_recv()

        def one(i, carry):
            paired[c][i] = (block[c][k * 32 + i].astype(F32) + traded[c][i].astype(F32)).astype(BF16)
            return carry

        lax.fori_loop(0, 32, one, 0)
        col_copies[c] = []
        for i, d in enumerate(FAR_FIRST):
            to_z = (z + d) % 4
            col_copies[c].append(
                copies.remote(
                    paired[c].at[pl.ds(to_z * 8, 8)], near[c].at[pl.ds(i * 8, 8)], at_device(xl, y, xh, to_z, k)
                )
            )

    def col_sum(c, side, i):
        total = paired[c][z * 8 + side * 4 + i].astype(F32)
        for n in range(3):
            total = total + near[c][n * 8 + side * 4 + i].astype(F32)
        return total

    def sum_cols(c):
        for copy in col_copies[c]:
            copy.wait_recv()

        def one(i, carry):
            cross[c][i] = col_sum(c, 1 - xh, i).astype(BF16)
            return carry

        lax.fori_loop(0, 4, one, 0)
        cross_copy[c] = copies.remote(cross[c], crossed[c], at_device(xl, y, 1 - xh, z, k))

    def sum_cross(c):
        cross_copy[c].wait_recv()

        def one(i, carry):
            out_ref[c, i] = col_sum(c, xh, i) + crossed[c][i].astype(F32)
            return carry

        lax.fori_loop(0, 4, one, 0)

    width = g_ref.shape[1]
    quarter_at = k * 512 + z * 128
    part_at = quarter_at + y * 32
    x_index = xl * 2 + xh
    piece_at = part_at + x_index * 8
    x_others = [((xl + a) % 2, (xh + b) % 2) for a, b in ((1, 1), (0, 1), (1, 0))]
    level = {}

    def blocks(count, size, body):
        def one(i, carry):
            body(pl.ds(pl.multiple_of(i * size, size), size), i * size)
            return carry

        lax.fori_loop(0, count, one, 0)

    def rows_of(base, offset, size):
        return pl.ds(pl.multiple_of(base + offset, size), size)

    def grad_core():
        def body(at, offset):
            g_core[at] = g_ref[rows_of((1 - k) * 512, offset, 64)].astype(BF16)

        blocks(8, 64, body)
        level["core"] = copies.remote(g_core, g_traded, at_device(xl, y, xh, z, 1 - k))

    def grad_z():
        level["core"].wait_recv()

        def body(at, offset):
            g_half[at] = (g_ref[rows_of(k * 512, offset, 64)] + g_traded[at].astype(F32)).astype(BF16)

        blocks(8, 64, body)
        level["z"] = []
        for i, d in enumerate(FAR_FIRST):
            to_z = (z + d) % 4
            level["z"].append(
                copies.remote(g_half.at[rows_of(0, to_z * 128, 128)], g_quarter.at[i], at_device(xl, y, xh, to_z, k))
            )

    def grad_y():
        for copy in level["z"]:
            copy.wait_recv()

        def body(at, offset):
            total = g_ref[rows_of(quarter_at, offset, 32)] + g_traded[rows_of(z * 128, offset, 32)].astype(F32)
            for i in range(3):
                total = total + g_quarter[i, at].astype(F32)
            g_part[0, at] = total

        blocks(4, 32, body)
        level["y"] = []
        for i, d in enumerate(FAR_FIRST):
            to_y = (y + d) % 4
            level["y"].append(
                copies.remote(g_part.at[0, rows_of(0, to_y * 32, 32)], g_eighth.at[i], at_device(xl, to_y, xh, z, k))
            )

    def grad_x():
        for copy in level["y"]:
            copy.wait_recv()
        total = g_part[0, rows_of(0, y * 32, 32)]
        for i in range(3):
            total = total + g_eighth[i]
        g_eighth_sum = g_piece.at[0]
        g_eighth_sum[...] = total
        level["x"] = []
        for i, (a, b) in enumerate(x_others):
            at = rows_of(0, (a * 2 + b) * 8, 8)
            level["x"].append(copies.remote(g_eighth_sum.at[at], g_piece.at[1, pl.ds(i * 8, 8)], at_device(a, y, b, z, k)))

    def grad_total():
        for copy in level["x"]:
            copy.wait_recv()
        total = g_piece[0, rows_of(0, x_index * 8, 8)]
        for i in range(3):
            total = total + g_piece[1, pl.ds(i * 8, 8)]
        at = rows_of(piece_at, 0, 8)
        sum_ref[at] = total * scale
        level["to_x"] = [copies.remote(sum_ref.at[at], sum_ref.at[at], at_device(a, y, b, z, k)) for a, b in x_others]

    def grad_to_y():
        for copy in level["to_x"]:
            copy.wait_recv()
        at = rows_of(part_at, 0, 32)
        level["to_y"] = [
            copies.remote(sum_ref.at[at], sum_ref.at[at], at_device(xl, (y + d) % 4, xh, z, k)) for d in FAR_FIRST
        ]

    def grad_to_z():
        for copy in level["to_y"]:
            copy.wait_recv()
        at = rows_of(quarter_at, 0, 128)
        level["to_z"] = [
            copies.remote(sum_ref.at[at], sum_ref.at[at], at_device(xl, y, xh, (z + d) % 4, k)) for d in FAR_FIRST
        ]

    def grad_to_core():
        for copy in level["to_z"]:
            copy.wait_recv()
        at = rows_of(k * 512, 0, 512)
        level["to_core"] = copies.remote(sum_ref.at[at], sum_ref.at[at], at_device(xl, y, xh, z, 1 - k))

    own(0)
    grad_core()
    onward(0)
    own(1)
    onward(1)
    grad_z()
    own(2)
    mask_copy.wait()
    product(0, grad_y)
    onward(2)
    own(3)
    sum_cores(0)
    grad_x()
    product(1, grad_total)
    onward(3)
    sum_cores(1)
    grad_to_y()
    sum_cols(0)
    product(2, grad_to_z)
    sum_cores(2)
    sum_cols(1)
    grad_to_core()
    sum_cross(0)
    product(3, lambda: None)
    sum_cores(3)
    sum_cols(2)
    sum_cross(1)
    sum_cols(3)
    sum_cross(2)
    sum_cross(3)
    level["to_core"].wait_recv()
    copies.finish()


def backward_exchange(tables, s, grads, masks, scale):
    return pl.pallas_call(
        functools.partial(backward_kernel, scale),
        in_specs=[SMEM_SPEC] * 5 + [VMEM_SPEC, VMEM_SPEC, ANY_SPEC],
        out_specs=[VMEM_SPEC, VMEM_SPEC],
        out_shape=[jax.ShapeDtypeStruct(s.shape, F32), jax.ShapeDtypeStruct(grads.shape, F32)],
        scratch_shapes=[tile_buffer(256), tile_buffer(256)]
        + [tile_buffer(32)] * 4
        + [tile_buffer(64)] * 4
        + [tile_buffer(32)] * 8
        + [tile_buffer(24)] * 4
        + [tile_buffer(4)] * 8
        + [pltpu.SemaphoreType.DMA((96,)), pltpu.SemaphoreType.DMA((96,))]
        + [pltpu.VMEM((512, 512), BF16)] * 3
        + [pltpu.VMEM((3, 128, 512), BF16), pltpu.VMEM((1, 128, 512), F32)]
        + [pltpu.VMEM((3, 32, 512), F32), pltpu.VMEM((2, 32, 512), F32)],
        compiler_params=remote_params(1),
        name="backward_exchange",
    )(*tables, s, grads, masks)


def column_order(columns):
    flat = columns.reshape(-1)
    count = flat.shape[0]
    block = flat // 4
    xh, z, k = block // 8, (block // 2) % 4, block % 2
    held_tile = (k * 8 + xh * 4 + z) * 4 + flat % 4
    back_tile = (k * 8 + z * 2 + xh) * 4 + flat % 4
    entry = jnp.arange(count, dtype=jnp.int32)
    key = back_tile * count + entry
    rank = jnp.sum((key[None, :] < key[:, None]).astype(jnp.int32), axis=1)
    hit = rank[None, :] == entry[:, None]
    pick = jnp.sum(jnp.where(hit, entry[None, :], 0), axis=1)
    sorted_tile = jnp.sum(jnp.where(hit, back_tile[None, :], 0), axis=1)
    before = jnp.concatenate([jnp.full((1,), -1, jnp.int32), sorted_tile[:-1]])
    keep = (sorted_tile == before).astype(F32)
    spot = jnp.arange(64, dtype=jnp.int32)
    upto = jnp.sum((back_tile[None, :] <= spot[:, None]).astype(jnp.int32), axis=1)
    some = jnp.any(back_tile[None, :] == spot[:, None], axis=1).astype(F32)
    last = jnp.maximum(upto - 1, 0)
    return held_tile, (pick, pick // 8, keep, last, some)


def dense_kernel(
    sum_ref, x_ref, extra_ref, ws_ref, wn_ref, hidden_ref, own_ref, spread_ref, grads_ref
):
    step = pl.program_id(0)
    width = hidden_ref.shape[1]
    x = jnp.concatenate([x_ref[c, 0] for c in range(4)], axis=1)
    degrees = extra_ref[:, pl.ds(width, 1)].astype(F32)
    cot = extra_ref[:, pl.ds(0, width)].astype(F32)
    summed = jnp.concatenate([sum_ref[c, 0] for c in range(4)], axis=1)
    aggregate = (summed / degrees).astype(BF16)
    preact = jnp.dot(x, ws_ref[...], preferred_element_type=F32) + jnp.dot(
        aggregate, wn_ref[...], preferred_element_type=F32
    )
    gate = jax.nn.sigmoid(preact)
    hidden_ref[...] = (preact * gate).astype(BF16)
    slopes = (cot * gate * (1.0 + preact * (1.0 - gate))).astype(BF16)
    gs = lax.dot_general(x, slopes, ROW_T, preferred_element_type=F32)
    gn = lax.dot_general(aggregate, slopes, ROW_T, preferred_element_type=F32)

    @pl.when(step == 0)
    def _():
        grads_ref[pl.ds(0, width)] = gs
        grads_ref[pl.ds(width, width)] = gn

    @pl.when(step > 0)
    def _():
        grads_ref[pl.ds(0, width)] += gs
        grads_ref[pl.ds(width, width)] += gn

    own_ref[...] = lax.dot_general(slopes, ws_ref[...], COL_T, preferred_element_type=F32)
    spread = lax.dot_general(slopes, wn_ref[...], COL_T, preferred_element_type=F32) / degrees
    for c in range(4):
        spread_ref[c, 0] = spread[:, c * 128 : (c + 1) * 128].T.astype(BF16)


def dense(summed, x, extra, ws, wn):
    rows, width = extra.shape[0], ws.shape[0]
    step = 128
    whole = lambda i: (0, 0)
    rowwise = lambda i: (i, 0)
    tiled = pl.BlockSpec((4, 1, step, 128), lambda i: (0, i, 0, 0))
    return pl.pallas_call(
        dense_kernel,
        grid=(rows // step,),
        in_specs=[
            tiled,
            tiled,
            pl.BlockSpec((step, extra.shape[1]), rowwise),
            pl.BlockSpec((width, width), whole),
            pl.BlockSpec((width, width), whole),
        ],
        out_specs=[
            pl.BlockSpec((step, width), rowwise),
            pl.BlockSpec((step, width), rowwise),
            tiled,
            pl.BlockSpec((2 * width, width), whole),
        ],
        out_shape=[
            jax.ShapeDtypeStruct((rows, width), BF16),
            jax.ShapeDtypeStruct((rows, width), F32),
            jax.ShapeDtypeStruct(x.shape, BF16),
            jax.ShapeDtypeStruct((2 * width, width), F32),
        ],
        compiler_params=params(),
        name="dense",
    )(summed, x, extra, ws, wn)


def join_kernel(own_ref, back_ref, out_ref):
    back = jnp.concatenate([back_ref[c, 0].T for c in range(4)], axis=1)
    out_ref[...] = (own_ref[...] + back).astype(BF16)


def join(own_back, back):
    rows, width = own_back.shape
    return pl.pallas_call(
        join_kernel,
        grid=(rows // 128,),
        in_specs=[
            pl.BlockSpec((128, width), lambda i: (i, 0)),
            pl.BlockSpec((4, 1, 128, 128), lambda i: (0, i, 0, 0)),
        ],
        out_specs=pl.BlockSpec((128, width), lambda i: (i, 0)),
        out_shape=jax.ShapeDtypeStruct((rows, width), BF16),
        name="join",
    )(own_back, back)


def swap_all(data, axes):
    return lax.all_to_all(data, axes, split_axis=0, concat_axis=0, tiled=True)


def on_device(
    features, tile_cols, tile_masks, degree, owner_nodes, owner_position, self_weight, neigh_weight, cotangent
):
    rows, width = features.shape
    n_row, n_col = lax.axis_size("row"), lax.axis_size("col")
    devices = n_row * n_col
    slot_count = 2 * rows // devices
    slots = devices * slot_count
    masks = tile_masks.reshape(256, 128, 128)
    own_dest = owner_nodes // rows
    own_flat = own_dest * slot_count + rank_within(own_dest, jnp.arange(rows, dtype=jnp.int32))
    node_source = owner_position // rows
    node_flat = node_source * slot_count + rank_within(node_source, owner_position)
    cols, tables = column_order(tile_cols[0, 0])

    both = ("row", "col")
    degree_cols = jnp.broadcast_to(degree.astype(BF16)[:, None], (rows, 128))
    node_x = unpack_tiles(node_flat, swap_all(pack(own_flat, features, slots), both))
    extra = jnp.concatenate([cotangent, degree_cols], axis=1)
    node_extra = unpack(node_flat, swap_all(pack(own_flat, extra, slots), both))
    summed = forward_exchange(cols, node_x, masks)
    hidden, own_back, spread, grads = dense(summed, node_x, node_extra, self_weight, neigh_weight)
    grad_scale = 1.0 / math.sqrt(rows * devices)
    back, sums = backward_exchange(tables, spread, grads, masks, grad_scale)
    grad_node = join(own_back, back)
    hidden_out = unpack(own_flat, swap_all(pack(node_flat, hidden, slots), both))
    grad_out = unpack(own_flat, swap_all(pack(node_flat, grad_node, slots), both))
    return hidden_out, grad_out, sums[:width], sums[width:]


def solution(mesh):
    both = P(("row", "col"))
    wide = P(("row", "col"), None)
    placed = (
        wide,
        P("row", "col", None, None),
        P("row", "col", None, None, None, None),
        both,
        both,
        both,
        P(),
        P(),
        wide,
    )
    return jax.shard_map(
        on_device, mesh=mesh, in_specs=placed, out_specs=(wide, wide, P(), P()), check_vma=False
    )
```

```python
import functools
import math

import jax
import jax.numpy as jnp
from jax import lax
from jax.experimental import pallas as pl
from jax.experimental.pallas import tpu as pltpu
from jax.sharding import PartitionSpec as P

F32 = jnp.float32
DEVICES = 128
BF16 = jnp.bfloat16
MESH = pl.DeviceIdType.MESH
VMEM_LIMIT = 60 * 1024 * 1024
ROW_T = (((0,), (0,)), ((), ()))
COL_T = (((1,), (1,)), ((), ()))


def rank_within(group_keys, order_keys):
    same_group = group_keys[:, None] == group_keys[None, :]
    earlier = order_keys[None, :] < order_keys[:, None]
    return jnp.sum(same_group & earlier, axis=1)


def params(**kw):
    return pltpu.CompilerParams(vmem_limit_bytes=VMEM_LIMIT, **kw)


def place():
    r, c = lax.axis_index("row"), lax.axis_index("col")
    return r // 4, r % 4, c // 8, (c // 2) % 4, c % 2


def at_device(xl, y, xh, z, k):
    return (xl * 4 + y, xh * 8 + z * 2 + k)


def device_number():
    return lax.axis_index("row") * 16 + lax.axis_index("col")


def greet():
    barrier, me = pltpu.get_barrier_semaphore(), device_number()

    def one(step, carry):
        peer = (me + step) % DEVICES
        pl.semaphore_signal(barrier, inc=1, device_id=(peer // 16, peer % 16), device_id_type=MESH)
        return carry

    lax.fori_loop(1, DEVICES, one, 0)


def meet():
    pl.semaphore_wait(pltpu.get_barrier_semaphore(), DEVICES - 1)


class Relay:
    def __init__(self, outbox, inbox, sems):
        self.outbox, self.inbox, self.sems = outbox, inbox, sems
        self.width = outbox.shape[2]

    def pack(self, spread_out, data, first):
        def one(i, carry):
            rows = jnp.dot(
                spread_out[pl.ds(pl.multiple_of(i * 128, 128), 128)],
                data[:, pl.ds(first, self.width)],
                preferred_element_type=F32,
            )
            self.outbox[pl.ds(i * 16, 16)] = rows.reshape(16, 8, self.width).astype(BF16)
            return carry

        lax.fori_loop(0, 8, one, 0)

    def whole(self):
        slots = pl.ds(0, DEVICES - 1)
        peer = (device_number() + 1) % DEVICES
        return pltpu.make_async_remote_copy(
            src_ref=self.outbox.at[slots], dst_ref=self.inbox.at[slots], send_sem=self.sems.at[0],
            recv_sem=self.sems.at[1], device_id=(peer // 16, peer % 16), device_id_type=MESH,
        )

    def kept(self):
        me = device_number()
        return pltpu.make_async_copy(self.outbox.at[me], self.inbox.at[me], self.sems.at[2])

    def start(self):
        me = device_number()
        self.kept().start()

        def one(step, carry):
            peer = (me + step) % DEVICES
            pltpu.make_async_remote_copy(
                src_ref=self.outbox.at[peer], dst_ref=self.inbox.at[me], send_sem=self.sems.at[0],
                recv_sem=self.sems.at[1], device_id=(peer // 16, peer % 16), device_id_type=MESH,
            ).start()
            return carry

        lax.fori_loop(1, DEVICES, one, 0)

    def collect(self, flat):
        self.kept().wait()
        self.whole().wait_recv()

        def one(i, carry):
            rows = self.inbox[pl.ds(i * 16, 16)].astype(F32).reshape(128, self.width)
            flat[pl.ds(pl.multiple_of(i * 128, 128), 128), pl.ds(0, self.width)] = rows.astype(BF16)
            return carry

        lax.fori_loop(0, 8, one, 0)

    def finish(self):
        self.whole().wait_send()


def pick_rows(table, flat_row):
    def one(i, carry):
        slot = lax.broadcasted_iota(jnp.int32, (128, table.shape[1]), 0) + i * 128
        table[pl.ds(pl.multiple_of(i * 128, 128), 128)] = jnp.where(slot == flat_row[...], 1.0, 0.0).astype(BF16)
        return carry

    lax.fori_loop(0, table.shape[0] // 128, one, 0)


def pick_slots(table, flat_col):
    def one(i, carry):
        at = pl.ds(pl.multiple_of(i * 128, 128), 128)
        slot = lax.broadcasted_iota(jnp.int32, (128, table.shape[1]), 1)
        table[at] = jnp.where(slot == flat_col[at], 1.0, 0.0).astype(BF16)
        return carry

    lax.fori_loop(0, table.shape[0] // 128, one, 0)


def each_block(count, body):
    def one(i, carry):
        body(i, pl.ds(pl.multiple_of(i * 128, 128), 128))
        return carry

    lax.fori_loop(0, count, one, 0)


class Copies:
    def __init__(self, send, recv):
        self.send, self.recv, self.used, self.started = send, recv, 0, []

    def remote(self, src, dst, device):
        i, self.used = self.used, self.used + 1
        copy = pltpu.make_async_remote_copy(
            src_ref=src, dst_ref=dst, send_sem=self.send.at[i], recv_sem=self.recv.at[i],
            device_id=device, device_id_type=MESH,
        )
        copy.start()
        self.started.append(copy)
        return copy

    def local(self, src, dst):
        i, self.used = self.used, self.used + 1
        copy = pltpu.make_async_copy(src, dst, self.recv.at[i])
        copy.start()
        return copy

    def finish(self):
        for copy in self.started:
            copy.wait_send()


FAR_FIRST = (2, 1, 3)


def forward_kernel(
    cols_ref, own_row, node_col, features, extra, mask_hbm, out_ref, x_ref, node_extra, mask, *rest
):
    held, part, near, cross, crossed, (send, recv) = (
        rest[0:4], rest[4:8], rest[8:12], rest[12:16], rest[16:20], rest[20:22]
    )
    xl, y, xh, z, k = place()
    copies = Copies(send, recv)
    mask_copy = copies.local(mask_hbm, mask)
    packing, unpacking, flat, flat_extra = rest[22:26]
    relays = [Relay(rest[26], rest[27], rest[28]), Relay(rest[29], rest[30], rest[31])]
    extra_relay = Relay(rest[32], rest[33], rest[34])
    greet()
    pick_rows(packing, own_row)
    relays[0].pack(packing, features, 0)
    meet()
    relays[0].start()
    relays[1].pack(packing, features, 256)
    relays[1].start()
    pick_slots(unpacking, node_col)
    extra_relay.pack(packing, extra, 0)

    def unpack(c):
        if c % 2 == 0:
            relays[c // 2].collect(flat)

        def one(i, at):
            rows = jnp.dot(unpacking[at], flat[:, pl.ds(c % 2 * 128, 128)], preferred_element_type=F32)
            x_ref[c, i] = rows.astype(BF16)

        each_block(4, one)

    def unpack_extra():
        extra_relay.collect(flat_extra)

        def one(i, at):
            node_extra[at] = jnp.dot(unpacking[at], flat_extra[...], preferred_element_type=F32).astype(BF16)

        each_block(4, one)

    tiles = lambda slot: pl.ds(slot * 4, 4)
    mine, pair = k * 8 + xh * 4 + z, k * 8 + (1 - xh) * 4 + z
    gathered, over, swap, row_copies, cross_copy = [[] for _ in range(4)], {}, {}, {}, {}

    def own(c):
        gathered[c].append(copies.local(x_ref.at[c], held[c].at[tiles(mine)]))
        over[c] = copies.remote(x_ref.at[c], held[c].at[tiles(mine)], at_device(xl, y, 1 - xh, z, k))
        for d in FAR_FIRST:
            to = at_device(xl, y, xh, (z + d) % 4, k)
            gathered[c].append(copies.remote(x_ref.at[c], held[c].at[tiles(mine)], to))

    def onward(c):
        over[c].wait_recv()
        for d in FAR_FIRST:
            to = at_device(xl, y, xh, (z + d) % 4, k)
            gathered[c].append(copies.remote(held[c].at[tiles(pair)], held[c].at[tiles(pair)], to))

    def swap_cores(c):
        gathered[c][0].wait()
        for copy in gathered[c][1:]:
            copy.wait_recv()
        half = held[c].at[pl.ds(k * 32, 32)]
        swap[c] = copies.remote(half, half, at_device(xl, y, xh, z, 1 - k))

    def product(c):
        swap[c].wait_recv()
        row_copies[c] = []
        for d in FAR_FIRST + (0,):
            to_y = (y + d) % 4

            def one(q, carry):
                t = (q // 4) * 16 + to_y * 4 + q % 4
                left = jnp.concatenate([mask[t * 8 + j] for j in range(8)], axis=1)
                right = jnp.concatenate([held[c][cols_ref[t * 8 + j]] for j in range(8)], axis=0)
                part[c][to_y * 8 + q] = jnp.dot(left, right, preferred_element_type=F32).astype(BF16)
                return carry

            lax.fori_loop(0, 8, one, 0)
            if d:
                i = FAR_FIRST.index(d)
                row_copies[c].append(
                    copies.remote(
                        part[c].at[pl.ds(to_y * 8, 8)], near[c].at[pl.ds(i * 8, 8)], at_device(xl, to_y, xh, z, k)
                    )
                )

    def row_sum(c, side, i):
        total = part[c][y * 8 + side * 4 + i].astype(F32)
        for n in range(3):
            total = total + near[c][n * 8 + side * 4 + i].astype(F32)
        return total

    def sum_rows(c):
        for copy in row_copies[c]:
            copy.wait_recv()

        def one(i, carry):
            cross[c][i] = row_sum(c, 1 - xl, i).astype(BF16)
            return carry

        lax.fori_loop(0, 4, one, 0)
        cross_copy[c] = copies.remote(cross[c], crossed[c], at_device(1 - xl, y, xh, z, k))

    def sum_cross(c):
        cross_copy[c].wait_recv()

        def one(i, carry):
            out_ref[c, i] = row_sum(c, xl, i) + crossed[c][i].astype(F32)
            return carry

        lax.fori_loop(0, 4, one, 0)

    unpack(0)
    own(0)
    unpack(1)
    onward(0)
    own(1)
    unpack(2)
    onward(1)
    swap_cores(0)
    own(2)
    unpack(3)
    mask_copy.wait()
    product(0)
    onward(2)
    swap_cores(1)
    own(3)
    product(1)
    onward(3)
    swap_cores(2)
    extra_relay.start()
    sum_rows(0)
    product(2)
    swap_cores(3)
    sum_rows(1)
    sum_cross(0)
    product(3)
    sum_rows(2)
    sum_cross(1)
    unpack_extra()
    sum_rows(3)
    sum_cross(2)
    sum_cross(3)
    copies.finish()
    for relay in relays + [extra_relay]:
        relay.finish()


def remote_params(ident):
    return params(collective_id=ident, has_side_effects=True)


SMEM_SPEC = pl.BlockSpec(memory_space=pltpu.SMEM)
VMEM_SPEC = pl.BlockSpec(memory_space=pltpu.VMEM)
ANY_SPEC = pl.BlockSpec(memory_space=pl.ANY)


def tile_buffer(count):
    return pltpu.VMEM((count, 128, 128), BF16)


def boxes(width):
    return [
        pltpu.VMEM((DEVICES, 8, width), BF16),
        pltpu.VMEM((DEVICES, 8, width), BF16),
        pltpu.SemaphoreType.DMA((3,)),
    ]


def forward_exchange(cols, own_row, node_col, features, extra, masks):
    rows, width = features.shape
    slots, wide = DEVICES * 8, extra.shape[1]
    tiled = (4, 4, 128, 128)
    return pl.pallas_call(
        forward_kernel,
        in_specs=[SMEM_SPEC] + [VMEM_SPEC] * 4 + [ANY_SPEC],
        out_specs=[VMEM_SPEC] * 3,
        out_shape=[
            jax.ShapeDtypeStruct(tiled, F32),
            jax.ShapeDtypeStruct(tiled, BF16),
            jax.ShapeDtypeStruct((rows, wide), BF16),
        ],
        scratch_shapes=[tile_buffer(256)]
        + [tile_buffer(64)] * 4
        + [tile_buffer(32)] * 4
        + [tile_buffer(24)] * 4
        + [tile_buffer(4)] * 8
        + [pltpu.SemaphoreType.DMA((64,)), pltpu.SemaphoreType.DMA((64,))]
        + [pltpu.VMEM((slots, rows), BF16), pltpu.VMEM((rows, slots), BF16)]
        + [pltpu.VMEM((slots, width // 2), BF16), pltpu.VMEM((slots, wide), BF16)]
        + boxes(width // 2) * 2
        + boxes(wide),
        compiler_params=remote_params(0),
        name="forward_exchange",
    )(cols, own_row, node_col, features, extra, masks)


def backward_kernel(
    scale, pick_ref, from_ref, keep_ref, last_ref, some_ref, node_row, own_col, hidden, own_back, s_ref, g_ref, mask_hbm,
    hidden_out, grad_out, sum_ref, mask, chain, *rest
):
    held, block, traded, near, cross, crossed, (send, recv) = (
        rest[0:4], rest[4:8], rest[8:12], rest[12:16], rest[16:20], rest[20:24], rest[24:26]
    )
    g_core, g_traded, g_half, g_quarter, g_part, g_eighth, g_piece = rest[26:33]
    xl, y, xh, z, k = place()
    copies = Copies(send, recv)
    mask_copy = copies.local(mask_hbm, mask)
    packing, unpacking, flat, joined = rest[33:37]
    hidden_relay = Relay(rest[37], rest[38], rest[39])
    relays = [Relay(rest[i], rest[i + 1], rest[i + 2]) for i in (40, 43, 46)]
    greet()
    pick_rows(packing, node_row)
    pick_slots(unpacking, own_col)
    hidden_relay.pack(packing, hidden, 0)
    meet()
    tiles = lambda slot: pl.ds(slot * 4, 4)
    mine, pair = xl * 4 + y, (1 - xl) * 4 + y
    gathered, over, trade, col_copies, cross_copy = [[] for _ in range(4)], {}, {}, {}, {}

    def own(c):
        gathered[c].append(copies.local(s_ref.at[c], held[c].at[tiles(mine)]))
        over[c] = copies.remote(s_ref.at[c], held[c].at[tiles(mine)], at_device(1 - xl, y, xh, z, k))
        for d in FAR_FIRST:
            to = at_device(xl, (y + d) % 4, xh, z, k)
            gathered[c].append(copies.remote(s_ref.at[c], held[c].at[tiles(mine)], to))

    def onward(c):
        over[c].wait_recv()
        for d in FAR_FIRST:
            to = at_device(xl, (y + d) % 4, xh, z, k)
            gathered[c].append(copies.remote(held[c].at[tiles(pair)], held[c].at[tiles(pair)], to))

    def product(c, between):
        gathered[c][0].wait()
        for copy in gathered[c][1:]:
            copy.wait_recv()

        def one(g, total):
            for u in range(8):
                e = g * 8 + u
                piece = jnp.dot(held[c][from_ref[e]], mask[pick_ref[e]], preferred_element_type=F32)
                total = total * keep_ref[e] + piece
                chain[e] = total.astype(BF16)
            return total

        half = lax.fori_loop(0, 16, one, jnp.zeros((128, 128), F32))
        between()
        lax.fori_loop(16, 32, one, half)

        def settle(p, carry):
            block[c][p] = (chain[last_ref[p]].astype(F32) * some_ref[p]).astype(BF16)
            return carry

        lax.fori_loop(0, 64, settle, 0)
        trade[c] = copies.remote(
            block[c].at[pl.ds((1 - k) * 32, 32)], traded[c], at_device(xl, y, xh, z, 1 - k)
        )

    def sum_cores(c):
        trade[c].wait_recv()

        def one(i, carry):
            block[c][k * 32 + i] = (block[c][k * 32 + i].astype(F32) + traded[c][i].astype(F32)).astype(BF16)
            return carry

        lax.fori_loop(0, 32, one, 0)
        col_copies[c] = []
        for i, d in enumerate(FAR_FIRST):
            to_z = (z + d) % 4
            col_copies[c].append(
                copies.remote(
                    block[c].at[pl.ds(k * 32 + to_z * 8, 8)], near[c].at[pl.ds(i * 8, 8)], at_device(xl, y, xh, to_z, k)
                )
            )

    def col_sum(c, side, i):
        total = block[c][k * 32 + z * 8 + side * 4 + i].astype(F32)
        for n in range(3):
            total = total + near[c][n * 8 + side * 4 + i].astype(F32)
        return total

    def sum_cols(c):
        for copy in col_copies[c]:
            copy.wait_recv()

        def one(i, carry):
            cross[c][i] = col_sum(c, 1 - xh, i).astype(BF16)
            return carry

        lax.fori_loop(0, 4, one, 0)
        cross_copy[c] = copies.remote(cross[c], crossed[c], at_device(xl, y, 1 - xh, z, k))

    def sum_cross(c):
        cross_copy[c].wait_recv()

        def one(i, carry):
            back = col_sum(c, xh, i) + crossed[c][i].astype(F32)
            at = (pl.ds(pl.multiple_of(i * 128, 128), 128), pl.ds(c * 128, 128))
            joined[at] = (own_back[at] + back.T).astype(BF16)
            return carry

        lax.fori_loop(0, 4, one, 0)

    width = g_ref.shape[1]
    quarter_at = k * 512 + z * 128
    part_at = quarter_at + y * 32
    x_index = xl * 2 + xh
    piece_at = part_at + x_index * 8
    x_others = [((xl + a) % 2, (xh + b) % 2) for a, b in ((1, 1), (0, 1), (1, 0))]
    level = {}

    def blocks(count, size, body):
        def one(i, carry):
            body(pl.ds(pl.multiple_of(i * size, size), size), i * size)
            return carry

        lax.fori_loop(0, count, one, 0)

    def rows_of(base, offset, size):
        return pl.ds(pl.multiple_of(base + offset, size), size)

    def grad_core():
        def body(at, offset):
            g_core[at] = g_ref[rows_of((1 - k) * 512, offset, 64)].astype(BF16)

        blocks(8, 64, body)
        level["core"] = copies.remote(g_core, g_traded, at_device(xl, y, xh, z, 1 - k))

    def grad_z():
        level["core"].wait_recv()

        def body(at, offset):
            g_half[at] = (g_ref[rows_of(k * 512, offset, 64)] + g_traded[at].astype(F32)).astype(BF16)

        blocks(8, 64, body)
        level["z"] = []
        for i, d in enumerate(FAR_FIRST):
            to_z = (z + d) % 4
            level["z"].append(
                copies.remote(g_half.at[rows_of(0, to_z * 128, 128)], g_quarter.at[i], at_device(xl, y, xh, to_z, k))
            )

    def grad_y():
        for copy in level["z"]:
            copy.wait_recv()

        def body(at, offset):
            total = g_ref[rows_of(quarter_at, offset, 32)] + g_traded[rows_of(z * 128, offset, 32)].astype(F32)
            for i in range(3):
                total = total + g_quarter[i, at].astype(F32)
            g_part[0, at] = total

        blocks(4, 32, body)
        level["y"] = []
        for i, d in enumerate(FAR_FIRST):
            to_y = (y + d) % 4
            level["y"].append(
                copies.remote(g_part.at[0, rows_of(0, to_y * 32, 32)], g_eighth.at[i], at_device(xl, to_y, xh, z, k))
            )

    def grad_x():
        for copy in level["y"]:
            copy.wait_recv()
        total = g_part[0, rows_of(0, y * 32, 32)]
        for i in range(3):
            total = total + g_eighth[i]
        g_eighth_sum = g_piece.at[0]
        g_eighth_sum[...] = total
        level["x"] = []
        for i, (a, b) in enumerate(x_others):
            at = rows_of(0, (a * 2 + b) * 8, 8)
            level["x"].append(copies.remote(g_eighth_sum.at[at], g_piece.at[1, pl.ds(i * 8, 8)], at_device(a, y, b, z, k)))

    def grad_total():
        for copy in level["x"]:
            copy.wait_recv()
        total = g_piece[0, rows_of(0, x_index * 8, 8)]
        for i in range(3):
            total = total + g_piece[1, pl.ds(i * 8, 8)]
        at = rows_of(piece_at, 0, 8)
        sum_ref[at] = total * scale
        level["to_x"] = [copies.remote(sum_ref.at[at], sum_ref.at[at], at_device(a, y, b, z, k)) for a, b in x_others]

    def grad_to_y():
        for copy in level["to_x"]:
            copy.wait_recv()
        at = rows_of(part_at, 0, 32)
        level["to_y"] = [
            copies.remote(sum_ref.at[at], sum_ref.at[at], at_device(xl, (y + d) % 4, xh, z, k)) for d in FAR_FIRST
        ]

    def grad_to_z():
        for copy in level["to_y"]:
            copy.wait_recv()
        at = rows_of(quarter_at, 0, 128)
        level["to_z"] = [
            copies.remote(sum_ref.at[at], sum_ref.at[at], at_device(xl, y, xh, (z + d) % 4, k)) for d in FAR_FIRST
        ]

    def grad_to_core():
        for copy in level["to_z"]:
            copy.wait_recv()
        at = rows_of(k * 512, 0, 512)
        level["to_core"] = copies.remote(sum_ref.at[at], sum_ref.at[at], at_device(xl, y, xh, z, 1 - k))

    def take(relay, out, first):
        relay.collect(flat)

        def one(i, at):
            rows = jnp.dot(unpacking[at], flat[:, pl.ds(0, relay.width)], preferred_element_type=F32)
            out[at, pl.ds(first, relay.width)] = rows.astype(BF16)

        each_block(4, one)

    def send_first():
        sum_cross(1)
        relays[0].pack(packing, joined, 0)
        relays[0].start()

    own(0)
    grad_core()
    onward(0)
    own(1)
    onward(1)
    grad_z()
    own(2)
    mask_copy.wait()
    product(0, grad_y)
    onward(2)
    own(3)
    sum_cores(0)
    grad_x()
    product(1, grad_total)
    onward(3)
    hidden_relay.start()
    sum_cores(1)
    grad_to_y()
    sum_cols(0)
    product(2, grad_to_z)
    sum_cores(2)
    sum_cols(1)
    grad_to_core()
    sum_cross(0)
    product(3, send_first)
    sum_cores(3)
    sum_cols(2)
    take(hidden_relay, hidden_out, 0)
    sum_cross(2)
    relays[1].pack(packing, joined, 256)
    relays[1].start()
    sum_cols(3)
    sum_cross(3)
    relays[2].pack(packing, joined, 384)
    relays[2].start()
    take(relays[0], grad_out, 0)
    take(relays[1], grad_out, 256)
    take(relays[2], grad_out, 384)
    level["to_core"].wait_recv()
    copies.finish()
    for relay in relays + [hidden_relay]:
        relay.finish()


def backward_exchange(tables, node_row, own_col, hidden, own_back, s, grads, masks, scale):
    rows, width = hidden.shape
    slots = DEVICES * 8
    return pl.pallas_call(
        functools.partial(backward_kernel, scale),
        in_specs=[SMEM_SPEC] * 5 + [VMEM_SPEC] * 6 + [ANY_SPEC],
        out_specs=[VMEM_SPEC] * 3,
        out_shape=[
            jax.ShapeDtypeStruct((rows, width), BF16),
            jax.ShapeDtypeStruct((rows, width), BF16),
            jax.ShapeDtypeStruct(grads.shape, F32),
        ],
        scratch_shapes=[tile_buffer(256), tile_buffer(256)]
        + [tile_buffer(32)] * 4
        + [tile_buffer(64)] * 4
        + [tile_buffer(32)] * 4
        + [tile_buffer(24)] * 4
        + [tile_buffer(4)] * 8
        + [pltpu.SemaphoreType.DMA((96,)), pltpu.SemaphoreType.DMA((96,))]
        + [pltpu.VMEM((512, 512), BF16)] * 3
        + [pltpu.VMEM((3, 128, 512), BF16), pltpu.VMEM((1, 128, 512), F32)]
        + [pltpu.VMEM((3, 32, 512), F32), pltpu.VMEM((2, 32, 512), F32)]
        + [pltpu.VMEM((slots, rows), BF16), pltpu.VMEM((rows, slots), BF16)]
        + [pltpu.VMEM((slots, width), BF16), pltpu.VMEM((rows, width), BF16)]
        + boxes(width)
        + boxes(width // 2)
        + boxes(width // 4) * 2,
        compiler_params=remote_params(1),
        name="backward_exchange",
    )(*tables, node_row, own_col, hidden, own_back, s, grads, masks)


def column_order(columns):
    flat = columns.reshape(-1)
    count = flat.shape[0]
    block = flat // 4
    xh, z, k = block // 8, (block // 2) % 4, block % 2
    held_tile = (k * 8 + xh * 4 + z) * 4 + flat % 4
    back_tile = (k * 8 + z * 2 + xh) * 4 + flat % 4
    entry = jnp.arange(count, dtype=jnp.int32)
    key = back_tile * count + entry
    rank = jnp.sum((key[None, :] < key[:, None]).astype(jnp.int32), axis=1)
    hit = rank[None, :] == entry[:, None]
    pick = jnp.sum(jnp.where(hit, entry[None, :], 0), axis=1)
    sorted_tile = jnp.sum(jnp.where(hit, back_tile[None, :], 0), axis=1)
    before = jnp.concatenate([jnp.full((1,), -1, jnp.int32), sorted_tile[:-1]])
    keep = (sorted_tile == before).astype(F32)
    spot = jnp.arange(64, dtype=jnp.int32)
    upto = jnp.sum((back_tile[None, :] <= spot[:, None]).astype(jnp.int32), axis=1)
    some = jnp.any(back_tile[None, :] == spot[:, None], axis=1).astype(F32)
    last = jnp.maximum(upto - 1, 0)
    return held_tile, (pick, pick // 8, keep, last, some)


def dense_kernel(
    sum_ref, x_ref, extra_ref, ws_ref, wn_ref, hidden_ref, own_ref, spread_ref, grads_ref
):
    step = pl.program_id(0)
    width = hidden_ref.shape[1]
    x = jnp.concatenate([x_ref[c, 0] for c in range(4)], axis=1)
    degrees = extra_ref[:, pl.ds(width, 1)].astype(F32)
    cot = extra_ref[:, pl.ds(0, width)].astype(F32)
    summed = jnp.concatenate([sum_ref[c, 0] for c in range(4)], axis=1)
    aggregate = (summed / degrees).astype(BF16)
    preact = jnp.dot(x, ws_ref[...], preferred_element_type=F32) + jnp.dot(
        aggregate, wn_ref[...], preferred_element_type=F32
    )
    gate = jax.nn.sigmoid(preact)
    hidden_ref[...] = (preact * gate).astype(BF16)
    slopes = (cot * gate * (1.0 + preact * (1.0 - gate))).astype(BF16)
    gs = lax.dot_general(x, slopes, ROW_T, preferred_element_type=F32)
    gn = lax.dot_general(aggregate, slopes, ROW_T, preferred_element_type=F32)

    @pl.when(step == 0)
    def _():
        grads_ref[pl.ds(0, width)] = gs
        grads_ref[pl.ds(width, width)] = gn

    @pl.when(step > 0)
    def _():
        grads_ref[pl.ds(0, width)] += gs
        grads_ref[pl.ds(width, width)] += gn

    own_ref[...] = lax.dot_general(slopes, ws_ref[...], COL_T, preferred_element_type=F32)
    spread = lax.dot_general(slopes, wn_ref[...], COL_T, preferred_element_type=F32) / degrees
    for c in range(4):
        spread_ref[c, 0] = spread[:, c * 128 : (c + 1) * 128].T.astype(BF16)


def dense(summed, x, extra, ws, wn):
    rows, width = extra.shape[0], ws.shape[0]
    step = 128
    whole = lambda i: (0, 0)
    rowwise = lambda i: (i, 0)
    tiled = pl.BlockSpec((4, 1, step, 128), lambda i: (0, i, 0, 0))
    return pl.pallas_call(
        dense_kernel,
        grid=(rows // step,),
        in_specs=[
            tiled,
            tiled,
            pl.BlockSpec((step, extra.shape[1]), rowwise),
            pl.BlockSpec((width, width), whole),
            pl.BlockSpec((width, width), whole),
        ],
        out_specs=[
            pl.BlockSpec((step, width), rowwise),
            pl.BlockSpec((step, width), rowwise),
            tiled,
            pl.BlockSpec((2 * width, width), whole),
        ],
        out_shape=[
            jax.ShapeDtypeStruct((rows, width), BF16),
            jax.ShapeDtypeStruct((rows, width), F32),
            jax.ShapeDtypeStruct(x.shape, BF16),
            jax.ShapeDtypeStruct((2 * width, width), F32),
        ],
        compiler_params=params(),
        name="dense",
    )(summed, x, extra, ws, wn)


def on_device(
    features, tile_cols, tile_masks, degree, owner_nodes, owner_position, self_weight, neigh_weight, cotangent
):
    rows, width = features.shape
    n_row, n_col = lax.axis_size("row"), lax.axis_size("col")
    devices = n_row * n_col
    slot_count = 2 * rows // devices
    masks = tile_masks.reshape(256, 128, 128)
    own_dest = owner_nodes // rows
    own_flat = own_dest * slot_count + rank_within(own_dest, jnp.arange(rows, dtype=jnp.int32))
    node_source = owner_position // rows
    node_flat = node_source * slot_count + rank_within(node_source, owner_position)
    cols, tables = column_order(tile_cols[0, 0])

    degree_cols = jnp.broadcast_to(degree.astype(BF16)[:, None], (rows, 128))
    extra = jnp.concatenate([cotangent, degree_cols], axis=1)
    own_row, own_col = own_flat.reshape(1, rows), own_flat.reshape(rows, 1)
    node_row, node_col = node_flat.reshape(1, rows), node_flat.reshape(rows, 1)
    summed, node_x, node_extra = forward_exchange(cols, own_row, node_col, features, extra, masks)
    hidden, own_back, spread, grads = dense(summed, node_x, node_extra, self_weight, neigh_weight)
    grad_scale = 1.0 / math.sqrt(rows * devices)
    hidden_out, grad_out, sums = backward_exchange(
        tables, node_row, own_col, hidden, own_back, spread, grads, masks, grad_scale
    )
    return hidden_out, grad_out, sums[:width], sums[width:]


def solution(mesh):
    both = P(("row", "col"))
    wide = P(("row", "col"), None)
    placed = (
        wide,
        P("row", "col", None, None),
        P("row", "col", None, None, None, None),
        both,
        both,
        both,
        P(),
        P(),
        wide,
    )
    return jax.shard_map(
        on_device, mesh=mesh, in_specs=placed, out_specs=(wide, wide, P(), P()), check_vma=False
    )
```

```python
import functools
import math

import jax
import jax.numpy as jnp
from jax import lax
from jax.experimental import pallas as pl
from jax.experimental.pallas import tpu as pltpu
from jax.sharding import PartitionSpec as P

F32 = jnp.float32
DEVICES = 128
BF16 = jnp.bfloat16
MESH = pl.DeviceIdType.MESH
VMEM_LIMIT = 60 * 1024 * 1024
ROW_T = (((0,), (0,)), ((), ()))
COL_T = (((1,), (1,)), ((), ()))


def params(**kw):
    return pltpu.CompilerParams(vmem_limit_bytes=VMEM_LIMIT, **kw)


def place():
    r, c = lax.axis_index("row"), lax.axis_index("col")
    return r // 4, r % 4, c // 8, (c // 2) % 4, c % 2


def at_device(xl, y, xh, z, k):
    return (xl * 4 + y, xh * 8 + z * 2 + k)


def device_number():
    return lax.axis_index("row") * 16 + lax.axis_index("col")


def greet():
    barrier, me = pltpu.get_barrier_semaphore(), device_number()

    def one(step, carry):
        peer = (me + step) % DEVICES
        pl.semaphore_signal(barrier, inc=1, device_id=(peer // 16, peer % 16), device_id_type=MESH)
        return carry

    lax.fori_loop(1, DEVICES, one, 0)


def meet():
    pl.semaphore_wait(pltpu.get_barrier_semaphore(), DEVICES - 1)


class Relay:
    def __init__(self, outbox, inbox, sems):
        self.outbox, self.inbox, self.sems = outbox, inbox, sems
        self.width = outbox.shape[2]

    def pack(self, spread_out, data, first):
        def one(i, carry):
            rows = jnp.dot(
                spread_out[pl.ds(pl.multiple_of(i * 128, 128), 128)],
                data[:, pl.ds(first, self.width)],
                preferred_element_type=F32,
            )
            self.outbox[pl.ds(i * 16, 16)] = rows.reshape(16, 8, self.width).astype(BF16)
            return carry

        lax.fori_loop(0, 8, one, 0)

    def whole(self):
        slots = pl.ds(0, DEVICES - 1)
        peer = (device_number() + 1) % DEVICES
        return pltpu.make_async_remote_copy(
            src_ref=self.outbox.at[slots], dst_ref=self.inbox.at[slots], send_sem=self.sems.at[0],
            recv_sem=self.sems.at[1], device_id=(peer // 16, peer % 16), device_id_type=MESH,
        )

    def kept(self):
        me = device_number()
        return pltpu.make_async_copy(self.outbox.at[me], self.inbox.at[me], self.sems.at[2])

    def start(self):
        me = device_number()
        self.kept().start()

        def one(step, carry):
            peer = (me + step) % DEVICES
            pltpu.make_async_remote_copy(
                src_ref=self.outbox.at[peer], dst_ref=self.inbox.at[me], send_sem=self.sems.at[0],
                recv_sem=self.sems.at[1], device_id=(peer // 16, peer % 16), device_id_type=MESH,
            ).start()
            return carry

        lax.fori_loop(1, DEVICES, one, 0)

    def collect(self, flat):
        self.kept().wait()
        self.whole().wait_recv()

        def one(i, carry):
            rows = self.inbox[pl.ds(i * 16, 16)].astype(F32).reshape(128, self.width)
            flat[pl.ds(pl.multiple_of(i * 128, 128), 128), pl.ds(0, self.width)] = rows.astype(BF16)
            return carry

        lax.fori_loop(0, 8, one, 0)

    def finish(self):
        self.whole().wait_send()


def pick_rows(table, flat_row):
    def one(i, carry):
        slot = lax.broadcasted_iota(jnp.int32, (128, table.shape[1]), 0) + i * 128
        table[pl.ds(pl.multiple_of(i * 128, 128), 128)] = jnp.where(slot == flat_row, 1.0, 0.0).astype(BF16)
        return carry

    lax.fori_loop(0, table.shape[0] // 128, one, 0)


def pick_slots(table, flat_col):
    def one(i, carry):
        at = pl.ds(pl.multiple_of(i * 128, 128), 128)
        slot = lax.broadcasted_iota(jnp.int32, (128, table.shape[1]), 1)
        table[at] = jnp.where(slot == flat_col[at], 1.0, 0.0).astype(BF16)
        return carry

    lax.fori_loop(0, table.shape[0] // 128, one, 0)


def upright(row):
    return jnp.broadcast_to(row, (128, row.shape[1])).T


def rank_row(group, order, side):
    count = group.shape[1]
    side[0, pl.ds(0, count)] = upright(group)
    side[1, pl.ds(0, count)] = upright(order)

    def one(i, total):
        at = pl.ds(pl.multiple_of(i * 128, 128), 128)
        before = (side[0, at, pl.ds(0, 1)] == group) & (side[1, at, pl.ds(0, 1)] < order)
        return total + jnp.sum(jnp.where(before, 1, 0), axis=0, keepdims=True)

    return lax.fori_loop(0, count // 128, one, jnp.zeros((1, count), jnp.int32))


def column_tables(cols, tables):
    count = cols.shape[1]
    block = cols // 4
    tile = ((block % 2) * 8 + ((block // 2) % 4) * 2 + block // 8) * 4 + cols % 4
    entry = lax.broadcasted_iota(jnp.int32, (1, count), 1)
    key = tile * count + entry
    rank = jnp.sum(jnp.where(upright(key)[:, :1] < key, 1, 0), axis=0, keepdims=True)
    place_of, tile_of = upright(rank)[:, :1], upright(tile)[:, :1]
    source = lax.broadcasted_iota(jnp.int32, (count, count), 0)
    spot = lax.broadcasted_iota(jnp.int32, (count, count), 1)
    add = lambda values: jnp.sum(values, axis=0, keepdims=True)
    pick = add(jnp.where(place_of == spot, source, 0))
    here = add(jnp.where(place_of == spot, tile_of, 0))
    before = add(jnp.where(place_of == spot - 1, tile_of + 1, 0)) - 1
    tables[0:1] = pick
    tables[1:2] = pick // 8
    tables[2:3] = jnp.where(here == before, 1, 0)
    tables[3:4] = jnp.maximum(add(jnp.where(tile_of <= spot, 1, 0)) - 1, 0)
    tables[4:5] = jnp.minimum(add(jnp.where(tile_of == spot, 1, 0)), 1)
    tables[5:8] = jnp.zeros((3, count), jnp.int32)


def each_block(count, body):
    def one(i, carry):
        body(i, pl.ds(pl.multiple_of(i * 128, 128), 128))
        return carry

    lax.fori_loop(0, count, one, 0)


class Copies:
    def __init__(self, send, recv):
        self.send, self.recv, self.used, self.started = send, recv, 0, []

    def remote(self, src, dst, device):
        i, self.used = self.used, self.used + 1
        copy = pltpu.make_async_remote_copy(
            src_ref=src, dst_ref=dst, send_sem=self.send.at[i], recv_sem=self.recv.at[i],
            device_id=device, device_id_type=MESH,
        )
        copy.start()
        self.started.append(copy)
        return copy

    def local(self, src, dst):
        i, self.used = self.used, self.used + 1
        copy = pltpu.make_async_copy(src, dst, self.recv.at[i])
        copy.start()
        return copy

    def finish(self):
        for copy in self.started:
            copy.wait_send()


FAR_FIRST = (2, 1, 3)


def held_tile(col):
    block = lax.shift_right_logical(col, 2)
    half = (block & 1) * 8 + lax.shift_right_logical(block, 3) * 4 + (lax.shift_right_logical(block, 1) & 3)
    return half * 4 + (col & 3)


def forward_kernel(
    cols_ref, cols_row, nodes, position, degree, features, cotangent, mask_hbm,
    out_ref, x_ref, node_extra, own_col, node_row, tables, mask, *rest
):
    held, part, near, cross, crossed, (send, recv) = (
        rest[0:4], rest[4:8], rest[8:12], rest[12:16], rest[16:20], rest[20:22]
    )
    xl, y, xh, z, k = place()
    copies = Copies(send, recv)
    mask_copy = copies.local(mask_hbm, mask)
    packing, unpacking, flat, flat_extra = rest[22:26]
    relays = [Relay(rest[26], rest[27], rest[28]), Relay(rest[29], rest[30], rest[31])]
    extra_relay = Relay(rest[32], rest[33], rest[34])
    extra, side, node_col = rest[35:38]
    width = features.shape[1]
    greet()
    lane = lax.broadcasted_iota(jnp.int32, nodes.shape, 1)
    dest = nodes[...] // width
    own_row = dest * 8 + rank_row(dest, lane, side)
    pick_rows(packing, own_row)
    relays[0].pack(packing, features, 0)
    meet()
    relays[0].start()
    relays[1].pack(packing, features, 256)
    relays[1].start()
    source = position[...] // width
    node_slot = source * 8 + rank_row(source, position[...], side)
    node_row[...] = node_slot
    node_col[...] = upright(node_slot)[:, :1]
    pick_slots(unpacking, node_col)
    own_col[...] = upright(own_row)[:, :1]
    column_tables(cols_row[...], tables)
    extra[:, pl.ds(0, width)] = cotangent[...]
    extra[:, pl.ds(width, 128)] = upright(degree[...]).astype(F32).astype(BF16)
    extra_relay.pack(packing, extra, 0)

    def unpack(c):
        if c % 2 == 0:
            relays[c // 2].collect(flat)

        def one(i, at):
            rows = jnp.dot(unpacking[at], flat[:, pl.ds(c % 2 * 128, 128)], preferred_element_type=F32)
            x_ref[c, i] = rows.astype(BF16)

        each_block(4, one)

    def unpack_extra():
        extra_relay.collect(flat_extra)

        def one(i, at):
            node_extra[at] = jnp.dot(unpacking[at], flat_extra[...], preferred_element_type=F32).astype(BF16)

        each_block(4, one)

    tiles = lambda slot: pl.ds(slot * 4, 4)
    mine, pair = k * 8 + xh * 4 + z, k * 8 + (1 - xh) * 4 + z
    gathered, over, swap, row_copies, cross_copy = [[] for _ in range(4)], {}, {}, {}, {}

    def own(c):
        gathered[c].append(copies.local(x_ref.at[c], held[c].at[tiles(mine)]))
        over[c] = copies.remote(x_ref.at[c], held[c].at[tiles(mine)], at_device(xl, y, 1 - xh, z, k))
        for d in FAR_FIRST:
            to = at_device(xl, y, xh, (z + d) % 4, k)
            gathered[c].append(copies.remote(x_ref.at[c], held[c].at[tiles(mine)], to))

    def onward(c):
        over[c].wait_recv()
        for d in FAR_FIRST:
            to = at_device(xl, y, xh, (z + d) % 4, k)
            gathered[c].append(copies.remote(held[c].at[tiles(pair)], held[c].at[tiles(pair)], to))

    def swap_cores(c):
        gathered[c][0].wait()
        for copy in gathered[c][1:]:
            copy.wait_recv()
        half = held[c].at[pl.ds(k * 32, 32)]
        swap[c] = copies.remote(half, half, at_device(xl, y, xh, z, 1 - k))

    def product(c):
        swap[c].wait_recv()
        row_copies[c] = []
        for d in FAR_FIRST + (0,):
            to_y = (y + d) % 4

            def one(q, carry):
                t = (q // 4) * 16 + to_y * 4 + q % 4
                left = jnp.concatenate([mask[t * 8 + j] for j in range(8)], axis=1)
                right = jnp.concatenate([held[c][held_tile(cols_ref[t * 8 + j])] for j in range(8)], axis=0)
                part[c][to_y * 8 + q] = jnp.dot(left, right, preferred_element_type=F32).astype(BF16)
                return carry

            lax.fori_loop(0, 8, one, 0)
            if d:
                i = FAR_FIRST.index(d)
                row_copies[c].append(
                    copies.remote(
                        part[c].at[pl.ds(to_y * 8, 8)], near[c].at[pl.ds(i * 8, 8)], at_device(xl, to_y, xh, z, k)
                    )
                )

    def row_sum(c, side, i):
        total = part[c][y * 8 + side * 4 + i].astype(F32)
        for n in range(3):
            total = total + near[c][n * 8 + side * 4 + i].astype(F32)
        return total

    def sum_rows(c):
        for copy in row_copies[c]:
            copy.wait_recv()

        def one(i, carry):
            cross[c][i] = row_sum(c, 1 - xl, i).astype(BF16)
            return carry

        lax.fori_loop(0, 4, one, 0)
        cross_copy[c] = copies.remote(cross[c], crossed[c], at_device(1 - xl, y, xh, z, k))

    def sum_cross(c):
        cross_copy[c].wait_recv()

        def one(i, carry):
            out_ref[c, i] = row_sum(c, xl, i) + crossed[c][i].astype(F32)
            return carry

        lax.fori_loop(0, 4, one, 0)

    unpack(0)
    own(0)
    unpack(1)
    onward(0)
    own(1)
    unpack(2)
    onward(1)
    swap_cores(0)
    own(2)
    unpack(3)
    mask_copy.wait()
    product(0)
    onward(2)
    swap_cores(1)
    own(3)
    product(1)
    onward(3)
    swap_cores(2)
    extra_relay.start()
    sum_rows(0)
    product(2)
    swap_cores(3)
    sum_rows(1)
    sum_cross(0)
    product(3)
    sum_rows(2)
    sum_cross(1)
    unpack_extra()
    sum_rows(3)
    sum_cross(2)
    sum_cross(3)
    copies.finish()
    for relay in relays + [extra_relay]:
        relay.finish()


def remote_params(ident):
    return params(collective_id=ident, has_side_effects=True)


SMEM_SPEC = pl.BlockSpec(memory_space=pltpu.SMEM)
VMEM_SPEC = pl.BlockSpec(memory_space=pltpu.VMEM)
ANY_SPEC = pl.BlockSpec(memory_space=pl.ANY)


def tile_buffer(count):
    return pltpu.VMEM((count, 128, 128), BF16)


def boxes(width):
    return [
        pltpu.VMEM((DEVICES, 8, width), BF16),
        pltpu.VMEM((DEVICES, 8, width), BF16),
        pltpu.SemaphoreType.DMA((3,)),
    ]


def forward_exchange(cols, nodes, position, degree, features, cotangent, masks):
    rows, width = features.shape
    slots, wide = DEVICES * 8, width + 128
    tiled = (4, 4, 128, 128)
    count = cols.shape[0]
    as_row = lambda values: values.reshape(1, -1)
    return pl.pallas_call(
        forward_kernel,
        in_specs=[SMEM_SPEC] + [VMEM_SPEC] * 6 + [ANY_SPEC],
        out_specs=[VMEM_SPEC] * 6,
        out_shape=[
            jax.ShapeDtypeStruct(tiled, F32),
            jax.ShapeDtypeStruct(tiled, BF16),
            jax.ShapeDtypeStruct((rows, wide), BF16),
            jax.ShapeDtypeStruct((rows, 1), jnp.int32),
            jax.ShapeDtypeStruct((1, rows), jnp.int32),
            jax.ShapeDtypeStruct((8, count), jnp.int32),
        ],
        scratch_shapes=[tile_buffer(256)]
        + [tile_buffer(64)] * 4
        + [tile_buffer(32)] * 4
        + [tile_buffer(24)] * 4
        + [tile_buffer(4)] * 8
        + [pltpu.SemaphoreType.DMA((64,)), pltpu.SemaphoreType.DMA((64,))]
        + [pltpu.VMEM((slots, rows), BF16), pltpu.VMEM((rows, slots), BF16)]
        + [pltpu.VMEM((slots, width // 2), BF16), pltpu.VMEM((slots, wide), BF16)]
        + boxes(width // 2) * 2
        + boxes(wide)
        + [pltpu.VMEM((rows, wide), BF16), pltpu.VMEM((2, rows, 128), jnp.int32), pltpu.VMEM((rows, 1), jnp.int32)],
        compiler_params=remote_params(0),
        name="forward_exchange",
    )(cols, as_row(cols), as_row(nodes), as_row(position), as_row(degree), features, cotangent, masks)


def backward_kernel(
    scale, tables, node_row, own_col, hidden, own_back, s_ref, g_ref, mask_hbm,
    hidden_out, grad_out, sum_ref, mask, chain, *rest
):
    held, block, traded, near, cross, crossed, (send, recv) = (
        rest[0:4], rest[4:8], rest[8:12], rest[12:16], rest[16:20], rest[20:24], rest[24:26]
    )
    g_core, g_traded, g_half, g_quarter, g_part, g_eighth, g_piece = rest[26:33]
    xl, y, xh, z, k = place()
    copies = Copies(send, recv)
    mask_copy = copies.local(mask_hbm, mask)
    packing, unpacking, flat, joined = rest[33:37]
    hidden_relay = Relay(rest[37], rest[38], rest[39])
    relays = [Relay(rest[i], rest[i + 1], rest[i + 2]) for i in (40, 43, 46)]
    greet()
    pick_rows(packing, node_row[...])
    pick_slots(unpacking, own_col)
    hidden_relay.pack(packing, hidden, 0)
    meet()
    tiles = lambda slot: pl.ds(slot * 4, 4)
    mine, pair = xl * 4 + y, (1 - xl) * 4 + y
    gathered, over, trade, col_copies, cross_copy = [[] for _ in range(4)], {}, {}, {}, {}

    def own(c):
        gathered[c].append(copies.local(s_ref.at[c], held[c].at[tiles(mine)]))
        over[c] = copies.remote(s_ref.at[c], held[c].at[tiles(mine)], at_device(1 - xl, y, xh, z, k))
        for d in FAR_FIRST:
            to = at_device(xl, (y + d) % 4, xh, z, k)
            gathered[c].append(copies.remote(s_ref.at[c], held[c].at[tiles(mine)], to))

    def onward(c):
        over[c].wait_recv()
        for d in FAR_FIRST:
            to = at_device(xl, (y + d) % 4, xh, z, k)
            gathered[c].append(copies.remote(held[c].at[tiles(pair)], held[c].at[tiles(pair)], to))

    def product(c, between):
        gathered[c][0].wait()
        for copy in gathered[c][1:]:
            copy.wait_recv()

        def one(g, total):
            for u in range(8):
                e = g * 8 + u
                piece = jnp.dot(held[c][tables[1, e]], mask[tables[0, e]], preferred_element_type=F32)
                total = total * tables[2, e].astype(F32) + piece
                chain[e] = total.astype(BF16)
            return total

        half = lax.fori_loop(0, 16, one, jnp.zeros((128, 128), F32))
        between()
        lax.fori_loop(16, 32, one, half)

        def settle(p, carry):
            block[c][p] = (chain[tables[3, p]].astype(F32) * tables[4, p].astype(F32)).astype(BF16)
            return carry

        lax.fori_loop(0, 64, settle, 0)
        trade[c] = copies.remote(
            block[c].at[pl.ds((1 - k) * 32, 32)], traded[c], at_device(xl, y, xh, z, 1 - k)
        )

    def sum_cores(c):
        trade[c].wait_recv()

        def one(i, carry):
            block[c][k * 32 + i] = (block[c][k * 32 + i].astype(F32) + traded[c][i].astype(F32)).astype(BF16)
            return carry

        lax.fori_loop(0, 32, one, 0)
        col_copies[c] = []
        for i, d in enumerate(FAR_FIRST):
            to_z = (z + d) % 4
            col_copies[c].append(
                copies.remote(
                    block[c].at[pl.ds(k * 32 + to_z * 8, 8)], near[c].at[pl.ds(i * 8, 8)], at_device(xl, y, xh, to_z, k)
                )
            )

    def col_sum(c, side, i):
        total = block[c][k * 32 + z * 8 + side * 4 + i].astype(F32)
        for n in range(3):
            total = total + near[c][n * 8 + side * 4 + i].astype(F32)
        return total

    def sum_cols(c):
        for copy in col_copies[c]:
            copy.wait_recv()

        def one(i, carry):
            cross[c][i] = col_sum(c, 1 - xh, i).astype(BF16)
            return carry

        lax.fori_loop(0, 4, one, 0)
        cross_copy[c] = copies.remote(cross[c], crossed[c], at_device(xl, y, 1 - xh, z, k))

    def sum_cross(c):
        cross_copy[c].wait_recv()

        def one(i, carry):
            back = col_sum(c, xh, i) + crossed[c][i].astype(F32)
            at = (pl.ds(pl.multiple_of(i * 128, 128), 128), pl.ds(c * 128, 128))
            joined[at] = (own_back[at] + back.T).astype(BF16)
            return carry

        lax.fori_loop(0, 4, one, 0)

    width = g_ref.shape[1]
    quarter_at = k * 512 + z * 128
    x_index = xl * 2 + xh
    x_others = [((xl + a) % 2, (xh + b) % 2) for a, b in ((1, 1), (0, 1), (1, 0))]
    level = {}

    def blocks(count, size, body):
        def one(i, carry):
            body(pl.ds(pl.multiple_of(i * size, size), size), i * size)
            return carry

        lax.fori_loop(0, count, one, 0)

    def rows_of(base, offset, size):
        return pl.ds(pl.multiple_of(base + offset, size), size)

    def grad_core():
        def body(at, offset):
            g_core[at] = g_ref[rows_of((1 - k) * 512, offset, 64)].astype(BF16)

        blocks(8, 64, body)
        level["core"] = copies.remote(g_core, g_traded, at_device(xl, y, xh, z, 1 - k))

    def grad_z():
        level["core"].wait_recv()

        def body(at, offset):
            g_half[at] = (g_ref[rows_of(k * 512, offset, 64)] + g_traded[at].astype(F32)).astype(BF16)

        blocks(8, 64, body)
        level["z"] = []
        for i, d in enumerate(FAR_FIRST):
            to_z = (z + d) % 4
            level["z"].append(
                copies.remote(g_half.at[rows_of(0, to_z * 128, 128)], g_quarter.at[i], at_device(xl, y, xh, to_z, k))
            )

    def grad_y():
        for copy in level["z"]:
            copy.wait_recv()

        def body(at, offset):
            total = g_ref[rows_of(quarter_at, offset, 32)] + g_traded[rows_of(z * 128, offset, 32)].astype(F32)
            for i in range(3):
                total = total + g_quarter[i, at].astype(F32)
            g_part[0, at] = total

        blocks(4, 32, body)
        level["y"] = []
        for i, d in enumerate(FAR_FIRST):
            to_y = (y + d) % 4
            level["y"].append(
                copies.remote(g_part.at[0, rows_of(0, to_y * 32, 32)], g_eighth.at[i], at_device(xl, to_y, xh, z, k))
            )

    def grad_x():
        for copy in level["y"]:
            copy.wait_recv()
        total = g_part[0, rows_of(0, y * 32, 32)]
        for i in range(3):
            total = total + g_eighth[i]
        g_eighth_sum = g_piece.at[0]
        g_eighth_sum[...] = total
        level["x"] = []
        for i, (a, b) in enumerate(x_others):
            at = rows_of(0, (a * 2 + b) * 8, 8)
            level["x"].append(copies.remote(g_eighth_sum.at[at], g_piece.at[1, pl.ds(i * 8, 8)], at_device(a, y, b, z, k)))

    def grad_total():
        for copy in level["x"]:
            copy.wait_recv()
        total = g_piece[0, rows_of(0, x_index * 8, 8)]
        for i in range(3):
            total = total + g_piece[1, pl.ds(i * 8, 8)]
        at = (k, z, y, rows_of(0, x_index * 8, 8))
        sum_ref[at] = total * scale
        level["to_x"] = [copies.remote(sum_ref.at[at], sum_ref.at[at], at_device(a, y, b, z, k)) for a, b in x_others]

    def grad_to_z():
        for copy in level["to_x"]:
            copy.wait_recv()
        at = sum_ref.at[k, z, y]
        level["to_z"] = [copies.remote(at, at, at_device(xl, y, xh, (z + d) % 4, k)) for d in FAR_FIRST]

    def grad_to_y():
        for copy in level["to_z"]:
            copy.wait_recv()
        at = sum_ref.at[k, :, y]
        level["to_y"] = [copies.remote(at, at, at_device(xl, (y + d) % 4, xh, z, k)) for d in FAR_FIRST]

    def grad_to_core():
        for copy in level["to_y"]:
            copy.wait_recv()
        level["to_core"] = copies.remote(sum_ref.at[k], sum_ref.at[k], at_device(xl, y, xh, z, 1 - k))

    def take(relay, out, first):
        relay.collect(flat)

        def one(i, at):
            rows = jnp.dot(unpacking[at], flat[:, pl.ds(0, relay.width)], preferred_element_type=F32)
            out[at, pl.ds(first, relay.width)] = rows.astype(BF16)

        each_block(4, one)

    def send_first():
        sum_cross(1)
        relays[0].pack(packing, joined, 0)
        relays[0].start()

    own(0)
    grad_core()
    onward(0)
    own(1)
    onward(1)
    grad_z()
    own(2)
    mask_copy.wait()
    product(0, grad_y)
    onward(2)
    own(3)
    sum_cores(0)
    grad_x()
    product(1, grad_total)
    onward(3)
    hidden_relay.start()
    sum_cores(1)
    grad_to_z()
    sum_cols(0)
    product(2, grad_to_y)
    sum_cores(2)
    sum_cols(1)
    grad_to_core()
    sum_cross(0)
    product(3, send_first)
    sum_cores(3)
    sum_cols(2)
    take(hidden_relay, hidden_out, 0)
    sum_cross(2)
    relays[1].pack(packing, joined, 256)
    relays[1].start()
    sum_cols(3)
    sum_cross(3)
    relays[2].pack(packing, joined, 384)
    relays[2].start()
    take(relays[0], grad_out, 0)
    take(relays[1], grad_out, 256)
    take(relays[2], grad_out, 384)
    level["to_core"].wait_recv()
    copies.finish()
    for relay in relays + [hidden_relay]:
        relay.finish()


def backward_exchange(tables, node_row, own_col, hidden, own_back, s, grads, masks, scale):
    rows, width = hidden.shape
    slots = DEVICES * 8
    return pl.pallas_call(
        functools.partial(backward_kernel, scale),
        in_specs=[SMEM_SPEC] + [VMEM_SPEC] * 6 + [ANY_SPEC],
        out_specs=[VMEM_SPEC] * 3,
        out_shape=[
            jax.ShapeDtypeStruct((rows, width), BF16),
            jax.ShapeDtypeStruct((rows, width), BF16),
            jax.ShapeDtypeStruct((2, 4, 4, 32, width), F32),
        ],
        scratch_shapes=[tile_buffer(256), tile_buffer(256)]
        + [tile_buffer(32)] * 4
        + [tile_buffer(64)] * 4
        + [tile_buffer(32)] * 4
        + [tile_buffer(24)] * 4
        + [tile_buffer(4)] * 8
        + [pltpu.SemaphoreType.DMA((96,)), pltpu.SemaphoreType.DMA((96,))]
        + [pltpu.VMEM((512, 512), BF16)] * 3
        + [pltpu.VMEM((3, 128, 512), BF16), pltpu.VMEM((1, 128, 512), F32)]
        + [pltpu.VMEM((3, 32, 512), F32), pltpu.VMEM((2, 32, 512), F32)]
        + [pltpu.VMEM((slots, rows), BF16), pltpu.VMEM((rows, slots), BF16)]
        + [pltpu.VMEM((slots, width), BF16), pltpu.VMEM((rows, width), BF16)]
        + boxes(width)
        + boxes(width // 2)
        + boxes(width // 4) * 2,
        compiler_params=remote_params(1),
        name="backward_exchange",
    )(tables, node_row, own_col, hidden, own_back, s, grads, masks)


def dense_kernel(
    sum_ref, x_ref, extra_ref, ws_ref, wn_ref, hidden_ref, own_ref, spread_ref, grads_ref
):
    step = pl.program_id(0)
    width = hidden_ref.shape[1]
    x = jnp.concatenate([x_ref[c, 0] for c in range(4)], axis=1)
    degrees = extra_ref[:, pl.ds(width, 1)].astype(F32)
    cot = extra_ref[:, pl.ds(0, width)].astype(F32)
    summed = jnp.concatenate([sum_ref[c, 0] for c in range(4)], axis=1)
    aggregate = (summed / degrees).astype(BF16)
    preact = jnp.dot(x, ws_ref[...], preferred_element_type=F32) + jnp.dot(
        aggregate, wn_ref[...], preferred_element_type=F32
    )
    gate = jax.nn.sigmoid(preact)
    hidden_ref[...] = (preact * gate).astype(BF16)
    slopes = (cot * gate * (1.0 + preact * (1.0 - gate))).astype(BF16)
    gs = lax.dot_general(x, slopes, ROW_T, preferred_element_type=F32)
    gn = lax.dot_general(aggregate, slopes, ROW_T, preferred_element_type=F32)

    @pl.when(step == 0)
    def _():
        grads_ref[pl.ds(0, width)] = gs
        grads_ref[pl.ds(width, width)] = gn

    @pl.when(step > 0)
    def _():
        grads_ref[pl.ds(0, width)] += gs
        grads_ref[pl.ds(width, width)] += gn

    own_ref[...] = lax.dot_general(slopes, ws_ref[...], COL_T, preferred_element_type=F32)
    spread = lax.dot_general(slopes, wn_ref[...], COL_T, preferred_element_type=F32) / degrees
    for c in range(4):
        spread_ref[c, 0] = spread[:, c * 128 : (c + 1) * 128].T.astype(BF16)


def dense(summed, x, extra, ws, wn):
    rows, width = extra.shape[0], ws.shape[0]
    step = 128
    whole = lambda i: (0, 0)
    rowwise = lambda i: (i, 0)
    tiled = pl.BlockSpec((4, 1, step, 128), lambda i: (0, i, 0, 0))
    return pl.pallas_call(
        dense_kernel,
        grid=(rows // step,),
        in_specs=[
            tiled,
            tiled,
            pl.BlockSpec((step, extra.shape[1]), rowwise),
            pl.BlockSpec((width, width), whole),
            pl.BlockSpec((width, width), whole),
        ],
        out_specs=[
            pl.BlockSpec((step, width), rowwise),
            pl.BlockSpec((step, width), rowwise),
            tiled,
            pl.BlockSpec((2 * width, width), whole),
        ],
        out_shape=[
            jax.ShapeDtypeStruct((rows, width), BF16),
            jax.ShapeDtypeStruct((rows, width), F32),
            jax.ShapeDtypeStruct(x.shape, BF16),
            jax.ShapeDtypeStruct((2 * width, width), F32),
        ],
        compiler_params=params(),
        name="dense",
    )(summed, x, extra, ws, wn)


def on_device(
    features, tile_cols, tile_masks, degree, owner_nodes, owner_position, self_weight, neigh_weight, cotangent
):
    rows, width = features.shape
    masks = tile_masks.reshape(-1, *tile_masks.shape[-2:])
    summed, node_x, node_extra, own_col, node_row, tables = forward_exchange(
        tile_cols.reshape(-1), owner_nodes, owner_position, degree, features, cotangent, masks
    )
    hidden, own_back, spread, grads = dense(summed, node_x, node_extra, self_weight, neigh_weight)
    grad_scale = 1.0 / math.sqrt(rows * DEVICES)
    hidden_out, grad_out, sums = backward_exchange(
        tables, node_row, own_col, hidden, own_back, spread, grads, masks, grad_scale
    )
    sums = sums.reshape(2, width, width)
    return hidden_out, grad_out, sums[0], sums[1]


def solution(mesh):
    both = P(("row", "col"))
    wide = P(("row", "col"), None)
    placed = (
        wide,
        P("row", "col", None, None),
        P("row", "col", None, None, None, None),
        both,
        both,
        both,
        P(),
        P(),
        wide,
    )
    return jax.shard_map(
        on_device, mesh=mesh, in_specs=placed, out_specs=(wide, wide, P(), P()), check_vma=False
    )
```

```python
import functools
import math

import jax
import jax.numpy as jnp
from jax import lax
from jax.experimental import pallas as pl
from jax.experimental.pallas import tpu as pltpu
from jax.sharding import PartitionSpec as P

F32 = jnp.float32
DEVICES = 128
BF16 = jnp.bfloat16
MESH = pl.DeviceIdType.MESH
VMEM_LIMIT = 60 * 1024 * 1024
ROW_T = (((0,), (0,)), ((), ()))
COL_T = (((1,), (1,)), ((), ()))


def params(**kw):
    return pltpu.CompilerParams(vmem_limit_bytes=VMEM_LIMIT, **kw)


def place():
    r, c = lax.axis_index("row"), lax.axis_index("col")
    return r // 4, r % 4, c // 8, (c // 2) % 4, c % 2


def at_device(xl, y, xh, z, k):
    return (xl * 4 + y, xh * 8 + z * 2 + k)


def device_number():
    return lax.axis_index("row") * 16 + lax.axis_index("col")


def greet():
    barrier, me = pltpu.get_barrier_semaphore(), device_number()

    def one(step, carry):
        peer = (me + step) % DEVICES
        pl.semaphore_signal(barrier, inc=1, device_id=(peer // 16, peer % 16), device_id_type=MESH)
        return carry

    lax.fori_loop(1, DEVICES, one, 0)


def meet():
    pl.semaphore_wait(pltpu.get_barrier_semaphore(), DEVICES - 1)


class Relay:
    def __init__(self, outbox, inbox, sems):
        self.outbox, self.inbox, self.sems = outbox, inbox, sems
        self.width = outbox.shape[2]

    def pack(self, spread_out, data, first):
        def one(i, carry):
            rows = jnp.dot(
                spread_out[pl.ds(pl.multiple_of(i * 128, 128), 128)],
                data[:, pl.ds(first, self.width)],
                preferred_element_type=F32,
            )
            self.outbox[pl.ds(i * 16, 16)] = rows.reshape(16, 8, self.width).astype(BF16)
            return carry

        lax.fori_loop(0, 8, one, 0)

    def whole(self):
        slots = pl.ds(0, DEVICES - 1)
        peer = (device_number() + 1) % DEVICES
        return pltpu.make_async_remote_copy(
            src_ref=self.outbox.at[slots], dst_ref=self.inbox.at[slots], send_sem=self.sems.at[0],
            recv_sem=self.sems.at[1], device_id=(peer // 16, peer % 16), device_id_type=MESH,
        )

    def kept(self):
        me = device_number()
        return pltpu.make_async_copy(self.outbox.at[me], self.inbox.at[me], self.sems.at[2])

    def start(self):
        me = device_number()
        self.kept().start()

        def one(step, carry):
            peer = (me + step) % DEVICES
            pltpu.make_async_remote_copy(
                src_ref=self.outbox.at[peer], dst_ref=self.inbox.at[me], send_sem=self.sems.at[0],
                recv_sem=self.sems.at[1], device_id=(peer // 16, peer % 16), device_id_type=MESH,
            ).start()
            return carry

        lax.fori_loop(1, DEVICES, one, 0)

    def collect(self, flat):
        self.kept().wait()
        self.whole().wait_recv()

        def one(i, carry):
            rows = self.inbox[pl.ds(i * 16, 16)].astype(F32).reshape(128, self.width)
            flat[pl.ds(pl.multiple_of(i * 128, 128), 128), pl.ds(0, self.width)] = rows.astype(BF16)
            return carry

        lax.fori_loop(0, 8, one, 0)

    def finish(self):
        self.whole().wait_send()


def pick_rows(table, flat_row):
    def one(i, carry):
        slot = lax.broadcasted_iota(jnp.int32, (128, table.shape[1]), 0) + i * 128
        table[pl.ds(pl.multiple_of(i * 128, 128), 128)] = jnp.where(slot == flat_row, 1.0, 0.0).astype(BF16)
        return carry

    lax.fori_loop(0, table.shape[0] // 128, one, 0)


def pick_slots(table, flat_col):
    def one(i, carry):
        at = pl.ds(pl.multiple_of(i * 128, 128), 128)
        slot = lax.broadcasted_iota(jnp.int32, (128, table.shape[1]), 1)
        table[at] = jnp.where(slot == flat_col[at], 1.0, 0.0).astype(BF16)
        return carry

    lax.fori_loop(0, table.shape[0] // 128, one, 0)


def upright(row):
    return jnp.broadcast_to(row, (128, row.shape[1])).T


def rank_row(group, order, side):
    count = group.shape[1]
    side[0, pl.ds(0, count)] = upright(group)
    side[1, pl.ds(0, count)] = upright(order)

    def one(i, total):
        at = pl.ds(pl.multiple_of(i * 128, 128), 128)
        before = (side[0, at, pl.ds(0, 1)] == group) & (side[1, at, pl.ds(0, 1)] < order)
        return total + jnp.sum(jnp.where(before, 1, 0), axis=0, keepdims=True)

    return lax.fori_loop(0, count // 128, one, jnp.zeros((1, count), jnp.int32))


def column_tables(cols, tables):
    count = cols.shape[1]
    block = cols // 4
    tile = ((block % 2) * 8 + ((block // 2) % 4) * 2 + block // 8) * 4 + cols % 4
    entry = lax.broadcasted_iota(jnp.int32, (1, count), 1)
    key = tile * count + entry
    rank = jnp.sum(jnp.where(upright(key)[:, :1] < key, 1, 0), axis=0, keepdims=True)
    place_of, tile_of = upright(rank)[:, :1], upright(tile)[:, :1]
    source = lax.broadcasted_iota(jnp.int32, (count, count), 0)
    spot = lax.broadcasted_iota(jnp.int32, (count, count), 1)
    add = lambda values: jnp.sum(values, axis=0, keepdims=True)
    pick = add(jnp.where(place_of == spot, source, 0))
    here = add(jnp.where(place_of == spot, tile_of, 0))
    before = add(jnp.where(place_of == spot - 1, tile_of + 1, 0)) - 1
    tables[0:1] = pick
    tables[1:2] = pick // 8
    tables[2:3] = jnp.where(here == before, 1, 0)
    tables[3:4] = jnp.maximum(add(jnp.where(tile_of <= spot, 1, 0)) - 1, 0)
    tables[4:5] = jnp.minimum(add(jnp.where(tile_of == spot, 1, 0)), 1)
    tables[5:8] = jnp.zeros((3, count), jnp.int32)


def each_block(count, body):
    def one(i, carry):
        body(i, pl.ds(pl.multiple_of(i * 128, 128), 128))
        return carry

    lax.fori_loop(0, count, one, 0)


class Copies:
    def __init__(self, send, recv):
        self.send, self.recv, self.used, self.started = send, recv, 0, []

    def remote(self, src, dst, device):
        i, self.used = self.used, self.used + 1
        copy = pltpu.make_async_remote_copy(
            src_ref=src, dst_ref=dst, send_sem=self.send.at[i], recv_sem=self.recv.at[i],
            device_id=device, device_id_type=MESH,
        )
        copy.start()
        self.started.append(copy)
        return copy

    def local(self, src, dst):
        i, self.used = self.used, self.used + 1
        copy = pltpu.make_async_copy(src, dst, self.recv.at[i])
        copy.start()
        return copy

    def finish(self):
        for copy in self.started:
            copy.wait_send()


FAR_FIRST = (2, 1, 3)
NEXT = (1, 3)


class Gather:
    def __init__(self, copies, source, held, slot, ring, place_in_ring, across):
        self.copies, self.source, self.held, self.slot = copies, source, held, slot
        self.ring, self.place, self.across = ring, place_in_ring, across
        self.first, self.last = {}, []

    def tiles(self, side, step, first=0, count=4):
        return self.held.at[pl.ds(self.slot(side, (self.place + step) % 4) * 4 + first, count)]

    def over(self):
        mine = self.tiles(0, 0)
        self.kept = self.copies.local(self.source, mine)
        self.crossing = self.copies.remote(self.source, mine, self.across)

    def own(self):
        self.first[0] = [self.copies.remote(self.source, self.tiles(0, 0), self.ring(d)) for d in NEXT]

    def onward(self):
        self.crossing.wait_recv()
        block = self.tiles(1, 0)
        self.first[1] = [self.copies.remote(block, block, self.ring(d)) for d in NEXT]

    def pass_on(self, side):
        for copy, d in zip(self.first[side], NEXT):
            copy.wait_recv()
            half = self.tiles(side, -d, 0 if d == 1 else 2, 2)
            self.last.append(self.copies.remote(half, half, self.ring(d)))

    def wait(self):
        self.kept.wait()
        for copy in self.last:
            copy.wait_recv()


class Sum:
    def __init__(self, copies, part, base, via, near, cross, crossed, ring, place_in_ring, side, across):
        self.copies, self.part, self.base, self.via, self.near = copies, part, base, via, near
        self.cross, self.crossed, self.ring, self.place = cross, crossed, ring, place_in_ring
        self.side, self.across = side, across

    def at(self, step, first=0):
        return self.base + (self.place + step) % 4 * 8 + first

    def far(self):
        self.vias = []
        for d, first in zip(NEXT, (0, 4)):
            self.vias.append(
                self.copies.remote(
                    self.part.at[pl.ds(self.at(2, first), 4)], self.via.at[pl.ds(first, 4)], self.ring(d)
                )
            )

    def hop(self):
        self.nears = []
        for n, (d, first) in enumerate(zip(NEXT, (0, 4))):
            start = self.at(d, first)

            def one(i, carry):
                self.part[start + i] = (self.part[start + i].astype(F32) + self.via[first + i].astype(F32)).astype(BF16)
                return carry

            self.vias[n].wait_recv()
            lax.fori_loop(0, 4, one, 0)
            self.nears.append(
                self.copies.remote(self.part.at[pl.ds(self.at(d), 8)], self.near.at[pl.ds(n * 8, 8)], self.ring(d))
            )

    def total(self, side, i):
        total = (
            self.part[self.at(0, side * 4 + i)].astype(F32)
            + self.near[side * 4 + i].astype(F32)
            + self.near[8 + side * 4 + i].astype(F32)
        )
        return total

    def over(self):
        for copy in self.nears:
            copy.wait_recv()

        def one(i, carry):
            self.cross[i] = self.total(1 - self.side, i).astype(BF16)
            return carry

        lax.fori_loop(0, 4, one, 0)
        self.crossing = self.copies.remote(self.cross, self.crossed, self.across)

    def finish(self, body):
        self.crossing.wait_recv()

        def one(i, carry):
            body(i, self.total(self.side, i) + self.crossed[i].astype(F32))
            return carry

        lax.fori_loop(0, 4, one, 0)


def held_tile(col):
    block = lax.shift_right_logical(col, 2)
    half = (block & 1) * 8 + lax.shift_right_logical(block, 3) * 4 + (lax.shift_right_logical(block, 1) & 3)
    return half * 4 + (col & 3)


def forward_kernel(
    cols_ref, cols_row, nodes, position, degree, features, cotangent, mask_hbm,
    out_ref, x_ref, node_extra, own_col, node_row, tables, mask, *rest
):
    held, part, near, cross, crossed, (send, recv) = (
        rest[0:4], rest[4:8], rest[8:12], rest[12:16], rest[16:20], rest[20:22]
    )
    xl, y, xh, z, k = place()
    copies = Copies(send, recv)
    mask_copy = copies.local(mask_hbm, mask)
    packing, unpacking, flat, flat_extra = rest[22:26]
    relays = [Relay(rest[26], rest[27], rest[28]), Relay(rest[29], rest[30], rest[31])]
    extra_relay = Relay(rest[32], rest[33], rest[34])
    extra, side, node_col = rest[35:38]
    width = features.shape[1]
    greet()
    lane = lax.broadcasted_iota(jnp.int32, nodes.shape, 1)
    dest = nodes[...] // width
    own_row = dest * 8 + rank_row(dest, lane, side)
    pick_rows(packing, own_row)
    relays[0].pack(packing, features, 0)
    meet()
    relays[0].start()
    relays[1].pack(packing, features, 256)
    relays[1].start()
    source = position[...] // width
    node_slot = source * 8 + rank_row(source, position[...], side)
    node_row[...] = node_slot
    node_col[...] = upright(node_slot)[:, :1]
    pick_slots(unpacking, node_col)
    own_col[...] = upright(own_row)[:, :1]
    column_tables(cols_row[...], tables)
    extra[:, pl.ds(0, width)] = cotangent[...]
    extra[:, pl.ds(width, 128)] = upright(degree[...]).astype(F32).astype(BF16)
    extra_relay.pack(packing, extra, 0)

    def unpack(c):
        if c % 2 == 0:
            relays[c // 2].collect(flat)

        def one(i, at):
            rows = jnp.dot(unpacking[at], flat[:, pl.ds(c % 2 * 128, 128)], preferred_element_type=F32)
            x_ref[c, i] = rows.astype(BF16)

        each_block(4, one)

    def unpack_extra():
        extra_relay.collect(flat_extra)

        def one(i, at):
            node_extra[at] = jnp.dot(unpacking[at], flat_extra[...], preferred_element_type=F32).astype(BF16)

        each_block(4, one)

    tiles = lambda slot: pl.ds(slot * 4, 4)
    mine, pair = k * 8 + xh * 4 + z, k * 8 + (1 - xh) * 4 + z
    gathered, over, swap, row_copies, cross_copy = [[] for _ in range(4)], {}, {}, {}, {}

    def own(c):
        gathered[c].append(copies.local(x_ref.at[c], held[c].at[tiles(mine)]))
        over[c] = copies.remote(x_ref.at[c], held[c].at[tiles(mine)], at_device(xl, y, 1 - xh, z, k))
        for d in FAR_FIRST:
            to = at_device(xl, y, xh, (z + d) % 4, k)
            gathered[c].append(copies.remote(x_ref.at[c], held[c].at[tiles(mine)], to))

    def onward(c):
        over[c].wait_recv()
        for d in FAR_FIRST:
            to = at_device(xl, y, xh, (z + d) % 4, k)
            gathered[c].append(copies.remote(held[c].at[tiles(pair)], held[c].at[tiles(pair)], to))

    def swap_cores(c):
        gathered[c][0].wait()
        for copy in gathered[c][1:]:
            copy.wait_recv()
        half = held[c].at[pl.ds(k * 32, 32)]
        swap[c] = copies.remote(half, half, at_device(xl, y, xh, z, 1 - k))

    def product(c):
        swap[c].wait_recv()
        row_copies[c] = []
        for d in FAR_FIRST + (0,):
            to_y = (y + d) % 4

            def one(q, carry):
                t = (q // 4) * 16 + to_y * 4 + q % 4
                left = jnp.concatenate([mask[t * 8 + j] for j in range(8)], axis=1)
                right = jnp.concatenate([held[c][held_tile(cols_ref[t * 8 + j])] for j in range(8)], axis=0)
                part[c][to_y * 8 + q] = jnp.dot(left, right, preferred_element_type=F32).astype(BF16)
                return carry

            lax.fori_loop(0, 8, one, 0)
            if d:
                i = FAR_FIRST.index(d)
                row_copies[c].append(
                    copies.remote(
                        part[c].at[pl.ds(to_y * 8, 8)], near[c].at[pl.ds(i * 8, 8)], at_device(xl, to_y, xh, z, k)
                    )
                )

    def row_sum(c, side, i):
        total = part[c][y * 8 + side * 4 + i].astype(F32)
        for n in range(3):
            total = total + near[c][n * 8 + side * 4 + i].astype(F32)
        return total

    def sum_rows(c):
        for copy in row_copies[c]:
            copy.wait_recv()

        def one(i, carry):
            cross[c][i] = row_sum(c, 1 - xl, i).astype(BF16)
            return carry

        lax.fori_loop(0, 4, one, 0)
        cross_copy[c] = copies.remote(cross[c], crossed[c], at_device(1 - xl, y, xh, z, k))

    def sum_cross(c):
        cross_copy[c].wait_recv()

        def one(i, carry):
            out_ref[c, i] = row_sum(c, xl, i) + crossed[c][i].astype(F32)
            return carry

        lax.fori_loop(0, 4, one, 0)

    unpack(0)
    own(0)
    unpack(1)
    onward(0)
    own(1)
    unpack(2)
    onward(1)
    swap_cores(0)
    own(2)
    unpack(3)
    mask_copy.wait()
    product(0)
    onward(2)
    swap_cores(1)
    own(3)
    product(1)
    onward(3)
    swap_cores(2)
    extra_relay.start()
    sum_rows(0)
    product(2)
    swap_cores(3)
    sum_rows(1)
    sum_cross(0)
    product(3)
    sum_rows(2)
    sum_cross(1)
    unpack_extra()
    sum_rows(3)
    sum_cross(2)
    sum_cross(3)
    copies.finish()
    for relay in relays + [extra_relay]:
        relay.finish()


def remote_params(ident):
    return params(collective_id=ident, has_side_effects=True)


SMEM_SPEC = pl.BlockSpec(memory_space=pltpu.SMEM)
VMEM_SPEC = pl.BlockSpec(memory_space=pltpu.VMEM)
ANY_SPEC = pl.BlockSpec(memory_space=pl.ANY)


def tile_buffer(count):
    return pltpu.VMEM((count, 128, 128), BF16)


def boxes(width):
    return [
        pltpu.VMEM((DEVICES, 8, width), BF16),
        pltpu.VMEM((DEVICES, 8, width), BF16),
        pltpu.SemaphoreType.DMA((3,)),
    ]


def forward_exchange(cols, nodes, position, degree, features, cotangent, masks):
    rows, width = features.shape
    slots, wide = DEVICES * 8, width + 128
    tiled = (4, 4, 128, 128)
    count = cols.shape[0]
    as_row = lambda values: values.reshape(1, -1)
    return pl.pallas_call(
        forward_kernel,
        in_specs=[SMEM_SPEC] + [VMEM_SPEC] * 6 + [ANY_SPEC],
        out_specs=[VMEM_SPEC] * 6,
        out_shape=[
            jax.ShapeDtypeStruct(tiled, F32),
            jax.ShapeDtypeStruct(tiled, BF16),
            jax.ShapeDtypeStruct((rows, wide), BF16),
            jax.ShapeDtypeStruct((rows, 1), jnp.int32),
            jax.ShapeDtypeStruct((1, rows), jnp.int32),
            jax.ShapeDtypeStruct((8, count), jnp.int32),
        ],
        scratch_shapes=[tile_buffer(256)]
        + [tile_buffer(64)] * 4
        + [tile_buffer(32)] * 4
        + [tile_buffer(24)] * 4
        + [tile_buffer(4)] * 8
        + [pltpu.SemaphoreType.DMA((64,)), pltpu.SemaphoreType.DMA((64,))]
        + [pltpu.VMEM((slots, rows), BF16), pltpu.VMEM((rows, slots), BF16)]
        + [pltpu.VMEM((slots, width // 2), BF16), pltpu.VMEM((slots, wide), BF16)]
        + boxes(width // 2) * 2
        + boxes(wide)
        + [pltpu.VMEM((rows, wide), BF16), pltpu.VMEM((2, rows, 128), jnp.int32), pltpu.VMEM((rows, 1), jnp.int32)],
        compiler_params=remote_params(0),
        name="forward_exchange",
    )(cols, as_row(cols), as_row(nodes), as_row(position), as_row(degree), features, cotangent, masks)


def backward_kernel(
    scale, tables, node_row, own_col, hidden, own_back, s_ref, g_ref, mask_hbm,
    hidden_out, grad_out, sum_ref, mask, chain, *rest
):
    held, block, traded, via, near, cross, crossed = [rest[i : i + 4] for i in range(0, 28, 4)]
    send, recv = rest[28:30]
    rest = rest[4:]
    g_core, g_traded, g_half, g_quarter, g_part, g_eighth, g_piece = rest[26:33]
    xl, y, xh, z, k = place()
    copies = Copies(send, recv)
    mask_copy = copies.local(mask_hbm, mask)
    packing, unpacking, flat, joined = rest[33:37]
    hidden_relay = Relay(rest[37], rest[38], rest[39])
    relays = [Relay(rest[i], rest[i + 1], rest[i + 2]) for i in (40, 43, 46)]
    greet()
    pick_rows(packing, node_row[...])
    pick_slots(unpacking, own_col)
    hidden_relay.pack(packing, hidden, 0)
    meet()
    ring_z = lambda d: at_device(xl, y, xh, (z + d) % 4, k)
    ring_y = lambda d: at_device(xl, (y + d) % 4, xh, z, k)
    slot = lambda side, at: (xl + side) % 2 * 4 + at
    gather = [
        Gather(copies, s_ref.at[c], held[c], slot, ring_y, y, at_device(1 - xl, y, xh, z, k)) for c in range(4)
    ]
    cols = [
        Sum(
            copies, block[c], k * 32, via[c], near[c], cross[c], crossed[c], ring_z, z, xh,
            at_device(xl, y, 1 - xh, z, k),
        )
        for c in range(4)
    ]
    trade = {}

    def product(c, *between):
        gather[c].wait()

        def one(g, total):
            for u in range(8):
                e = g * 8 + u
                piece = jnp.dot(held[c][tables[1, e]], mask[tables[0, e]], preferred_element_type=F32)
                total = total * tables[2, e].astype(F32) + piece
                chain[e] = total.astype(BF16)
            return total

        total = jnp.zeros((128, 128), F32)
        for n in range(4):
            total = lax.fori_loop(n * 8, n * 8 + 8, one, total)
            for action in between[n : n + 1]:
                action()

        def settle(p, carry):
            block[c][p] = (chain[tables[3, p]].astype(F32) * tables[4, p].astype(F32)).astype(BF16)
            return carry

        lax.fori_loop(0, 64, settle, 0)
        trade[c] = copies.remote(
            block[c].at[pl.ds((1 - k) * 32, 32)], traded[c], at_device(xl, y, xh, z, 1 - k)
        )

    def sum_cores(c):
        trade[c].wait_recv()

        def one(i, carry):
            block[c][k * 32 + i] = (block[c][k * 32 + i].astype(F32) + traded[c][i].astype(F32)).astype(BF16)
            return carry

        lax.fori_loop(0, 32, one, 0)
        cols[c].far()

    def finish(c):
        def body(i, total):
            at = (pl.ds(pl.multiple_of(i * 128, 128), 128), pl.ds(c * 128, 128))
            joined[at] = (own_back[at] + total.T).astype(BF16)

        cols[c].finish(body)

    width = g_ref.shape[1]
    quarter_at = k * 512 + z * 128
    x_index = xl * 2 + xh
    x_others = [((xl + a) % 2, (xh + b) % 2) for a, b in ((1, 1), (0, 1), (1, 0))]
    level = {}

    def blocks(count, size, body):
        def one(i, carry):
            body(pl.ds(pl.multiple_of(i * size, size), size), i * size)
            return carry

        lax.fori_loop(0, count, one, 0)

    def rows_of(base, offset, size):
        return pl.ds(pl.multiple_of(base + offset, size), size)

    def grad_core():
        def body(at, offset):
            g_core[at] = g_ref[rows_of((1 - k) * 512, offset, 64)].astype(BF16)

        blocks(8, 64, body)
        level["core"] = copies.remote(g_core, g_traded, at_device(xl, y, xh, z, 1 - k))

    def grad_z():
        level["core"].wait_recv()

        def body(at, offset):
            g_half[at] = (g_ref[rows_of(k * 512, offset, 64)] + g_traded[at].astype(F32)).astype(BF16)

        blocks(8, 64, body)
        level["z"] = []
        for i, d in enumerate(FAR_FIRST):
            to_z = (z + d) % 4
            level["z"].append(
                copies.remote(g_half.at[rows_of(0, to_z * 128, 128)], g_quarter.at[i], at_device(xl, y, xh, to_z, k))
            )

    def grad_y():
        for copy in level["z"]:
            copy.wait_recv()

        def body(at, offset):
            total = g_ref[rows_of(quarter_at, offset, 32)] + g_traded[rows_of(z * 128, offset, 32)].astype(F32)
            for i in range(3):
                total = total + g_quarter[i, at].astype(F32)
            g_part[0, at] = total

        blocks(4, 32, body)
        level["y"] = []
        for i, d in enumerate(FAR_FIRST):
            to_y = (y + d) % 4
            level["y"].append(
                copies.remote(g_part.at[0, rows_of(0, to_y * 32, 32)], g_eighth.at[i], at_device(xl, to_y, xh, z, k))
            )

    def grad_x():
        for copy in level["y"]:
            copy.wait_recv()
        total = g_part[0, rows_of(0, y * 32, 32)]
        for i in range(3):
            total = total + g_eighth[i]
        g_eighth_sum = g_piece.at[0]
        g_eighth_sum[...] = total
        level["x"] = []
        for i, (a, b) in enumerate(x_others):
            at = rows_of(0, (a * 2 + b) * 8, 8)
            level["x"].append(copies.remote(g_eighth_sum.at[at], g_piece.at[1, pl.ds(i * 8, 8)], at_device(a, y, b, z, k)))

    def grad_total():
        for copy in level["x"]:
            copy.wait_recv()
        total = g_piece[0, rows_of(0, x_index * 8, 8)]
        for i in range(3):
            total = total + g_piece[1, pl.ds(i * 8, 8)]
        at = (k, z, y, rows_of(0, x_index * 8, 8))
        sum_ref[at] = total * scale
        level["to_x"] = [copies.remote(sum_ref.at[at], sum_ref.at[at], at_device(a, y, b, z, k)) for a, b in x_others]

    def grad_to_z():
        for copy in level["to_x"]:
            copy.wait_recv()
        at = sum_ref.at[k, z, y]
        level["to_z"] = [copies.remote(at, at, at_device(xl, y, xh, (z + d) % 4, k)) for d in FAR_FIRST]

    def grad_to_y():
        for copy in level["to_z"]:
            copy.wait_recv()
        at = sum_ref.at[k, :, y]
        level["to_y"] = [copies.remote(at, at, at_device(xl, (y + d) % 4, xh, z, k)) for d in FAR_FIRST]

    def grad_to_core():
        for copy in level["to_y"]:
            copy.wait_recv()
        level["to_core"] = copies.remote(sum_ref.at[k], sum_ref.at[k], at_device(xl, y, xh, z, 1 - k))

    def take(relay, out, first):
        relay.collect(flat)

        def one(i, at):
            rows = jnp.dot(unpacking[at], flat[:, pl.ds(0, relay.width)], preferred_element_type=F32)
            out[at, pl.ds(first, relay.width)] = rows.astype(BF16)

        each_block(4, one)

    def send(relay, first):
        relay.pack(packing, joined, first)
        relay.start()

    def steps(*actions):
        def run():
            for action in actions:
                action()

        return run

    def passing(c, side):
        return lambda: gather[c].pass_on(side)

    def paired(c):
        return lambda: sum_cores(c)

    for c in range(4):
        gather[c].over()
    gather[0].own()
    grad_core()
    gather[0].onward()
    gather[0].pass_on(0)
    gather[0].pass_on(1)
    gather[1].own()
    gather[1].onward()
    grad_z()
    mask_copy.wait()
    product(
        0,
        passing(1, 0),
        steps(passing(1, 1), gather[2].own),
        steps(gather[2].onward, grad_y),
    )
    product(
        1,
        steps(paired(0), passing(2, 0)),
        steps(passing(2, 1), gather[3].own, gather[3].onward),
        steps(cols[0].hop, grad_x),
    )
    product(
        2,
        steps(paired(1), passing(3, 0)),
        steps(passing(3, 1), cols[0].over, hidden_relay.start),
        steps(cols[1].hop, grad_total),
    )
    product(
        3,
        steps(paired(2), lambda: finish(0)),
        steps(cols[1].over, grad_to_z),
        steps(cols[2].hop, lambda: finish(1), lambda: send(relays[0], 0)),
    )
    sum_cores(3)
    grad_to_y()
    cols[2].over()
    cols[3].hop()
    take(hidden_relay, hidden_out, 0)
    finish(2)
    send(relays[1], 256)
    cols[3].over()
    grad_to_core()
    finish(3)
    send(relays[2], 384)
    take(relays[0], grad_out, 0)
    take(relays[1], grad_out, 256)
    take(relays[2], grad_out, 384)
    level["to_core"].wait_recv()
    copies.finish()
    for relay in relays + [hidden_relay]:
        relay.finish()


def backward_exchange(tables, node_row, own_col, hidden, own_back, s, grads, masks, scale):
    rows, width = hidden.shape
    slots = DEVICES * 8
    return pl.pallas_call(
        functools.partial(backward_kernel, scale),
        in_specs=[SMEM_SPEC] + [VMEM_SPEC] * 6 + [ANY_SPEC],
        out_specs=[VMEM_SPEC] * 3,
        out_shape=[
            jax.ShapeDtypeStruct((rows, width), BF16),
            jax.ShapeDtypeStruct((rows, width), BF16),
            jax.ShapeDtypeStruct((2, 4, 4, 32, width), F32),
        ],
        scratch_shapes=[tile_buffer(256), tile_buffer(256)]
        + [tile_buffer(32)] * 4
        + [tile_buffer(64)] * 4
        + [tile_buffer(32)] * 4
        + [tile_buffer(8)] * 4
        + [tile_buffer(16)] * 4
        + [tile_buffer(4)] * 8
        + [pltpu.SemaphoreType.DMA((128,)), pltpu.SemaphoreType.DMA((128,))]
        + [pltpu.VMEM((512, 512), BF16)] * 3
        + [pltpu.VMEM((3, 128, 512), BF16), pltpu.VMEM((1, 128, 512), F32)]
        + [pltpu.VMEM((3, 32, 512), F32), pltpu.VMEM((2, 32, 512), F32)]
        + [pltpu.VMEM((slots, rows), BF16), pltpu.VMEM((rows, slots), BF16)]
        + [pltpu.VMEM((slots, width), BF16), pltpu.VMEM((rows, width), BF16)]
        + boxes(width)
        + boxes(width // 2)
        + boxes(width // 4) * 2,
        compiler_params=remote_params(1),
        name="backward_exchange",
    )(tables, node_row, own_col, hidden, own_back, s, grads, masks)


def dense_kernel(
    sum_ref, x_ref, extra_ref, ws_ref, wn_ref, hidden_ref, own_ref, spread_ref, grads_ref
):
    step = pl.program_id(0)
    width = hidden_ref.shape[1]
    parts = x_ref.shape[1]
    whole = lambda ref: jnp.concatenate([ref[c].reshape(parts * 128, 128) for c in range(4)], axis=1)
    x = whole(x_ref)
    degrees = extra_ref[:, pl.ds(width, 1)].astype(F32)
    cot = extra_ref[:, pl.ds(0, width)].astype(F32)
    summed = whole(sum_ref)
    aggregate = (summed / degrees).astype(BF16)
    preact = jnp.dot(x, ws_ref[...], preferred_element_type=F32) + jnp.dot(
        aggregate, wn_ref[...], preferred_element_type=F32
    )
    gate = jax.nn.sigmoid(preact)
    hidden_ref[...] = (preact * gate).astype(BF16)
    slopes = (cot * gate * (1.0 + preact * (1.0 - gate))).astype(BF16)
    gs = lax.dot_general(x, slopes, ROW_T, preferred_element_type=F32)
    gn = lax.dot_general(aggregate, slopes, ROW_T, preferred_element_type=F32)

    @pl.when(step == 0)
    def _():
        grads_ref[pl.ds(0, width)] = gs
        grads_ref[pl.ds(width, width)] = gn

    @pl.when(step > 0)
    def _():
        grads_ref[pl.ds(0, width)] += gs
        grads_ref[pl.ds(width, width)] += gn

    own_ref[...] = lax.dot_general(slopes, ws_ref[...], COL_T, preferred_element_type=F32)
    spread = lax.dot_general(slopes, wn_ref[...], COL_T, preferred_element_type=F32) / degrees
    for c in range(4):
        for i in range(parts):
            spread_ref[c, i] = spread[i * 128 : (i + 1) * 128, c * 128 : (c + 1) * 128].T.astype(BF16)


def dense(summed, x, extra, ws, wn):
    rows, width = extra.shape[0], ws.shape[0]
    step = 256
    whole = lambda i: (0, 0)
    rowwise = lambda i: (i, 0)
    tiled = pl.BlockSpec((4, step // 128, 128, 128), lambda i: (0, i, 0, 0))
    return pl.pallas_call(
        dense_kernel,
        grid=(rows // step,),
        in_specs=[
            tiled,
            tiled,
            pl.BlockSpec((step, extra.shape[1]), rowwise),
            pl.BlockSpec((width, width), whole),
            pl.BlockSpec((width, width), whole),
        ],
        out_specs=[
            pl.BlockSpec((step, width), rowwise),
            pl.BlockSpec((step, width), rowwise),
            tiled,
            pl.BlockSpec((2 * width, width), whole),
        ],
        out_shape=[
            jax.ShapeDtypeStruct((rows, width), BF16),
            jax.ShapeDtypeStruct((rows, width), F32),
            jax.ShapeDtypeStruct(x.shape, BF16),
            jax.ShapeDtypeStruct((2 * width, width), F32),
        ],
        compiler_params=params(),
        name="dense",
    )(summed, x, extra, ws, wn)


def on_device(
    features, tile_cols, tile_masks, degree, owner_nodes, owner_position, self_weight, neigh_weight, cotangent
):
    rows, width = features.shape
    masks = tile_masks.reshape(-1, *tile_masks.shape[-2:])
    summed, node_x, node_extra, own_col, node_row, tables = forward_exchange(
        tile_cols.reshape(-1), owner_nodes, owner_position, degree, features, cotangent, masks
    )
    hidden, own_back, spread, grads = dense(summed, node_x, node_extra, self_weight, neigh_weight)
    grad_scale = 1.0 / math.sqrt(rows * DEVICES)
    hidden_out, grad_out, sums = backward_exchange(
        tables, node_row, own_col, hidden, own_back, spread, grads, masks, grad_scale
    )
    sums = sums.reshape(2, width, width)
    return hidden_out, grad_out, sums[0], sums[1]


def solution(mesh):
    both = P(("row", "col"))
    wide = P(("row", "col"), None)
    placed = (
        wide,
        P("row", "col", None, None),
        P("row", "col", None, None, None, None),
        both,
        both,
        both,
        P(),
        P(),
        wide,
    )
    return jax.shard_map(
        on_device, mesh=mesh, in_specs=placed, out_specs=(wide, wide, P(), P()), check_vma=False
    )
```

```python
import functools
import math

import jax
import jax.numpy as jnp
from jax import lax
from jax.experimental import pallas as pl
from jax.experimental.pallas import tpu as pltpu
from jax.sharding import PartitionSpec as P

F32 = jnp.float32
DEVICES = 128
BF16 = jnp.bfloat16
MESH = pl.DeviceIdType.MESH
VMEM_LIMIT = 60 * 1024 * 1024
ROW_T = (((0,), (0,)), ((), ()))
COL_T = (((1,), (1,)), ((), ()))


def params(**kw):
    return pltpu.CompilerParams(vmem_limit_bytes=VMEM_LIMIT, **kw)


def place():
    r, c = lax.axis_index("row"), lax.axis_index("col")
    return r // 4, r % 4, c // 8, (c // 2) % 4, c % 2


def at_device(xl, y, xh, z, k):
    return (xl * 4 + y, xh * 8 + z * 2 + k)


def device_number():
    return lax.axis_index("row") * 16 + lax.axis_index("col")


def greet():
    barrier, me = pltpu.get_barrier_semaphore(), device_number()

    def one(step, carry):
        peer = (me + step) % DEVICES
        pl.semaphore_signal(barrier, inc=1, device_id=(peer // 16, peer % 16), device_id_type=MESH)
        return carry

    lax.fori_loop(1, DEVICES, one, 0)


def meet():
    pl.semaphore_wait(pltpu.get_barrier_semaphore(), DEVICES - 1)


class Relay:
    def __init__(self, outbox, inbox, sems):
        self.outbox, self.inbox, self.sems = outbox, inbox, sems
        self.width = outbox.shape[2]

    def pack(self, spread_out, data, first):
        def one(i, carry):
            rows = jnp.dot(
                spread_out[pl.ds(pl.multiple_of(i * 128, 128), 128)],
                data[:, pl.ds(first, self.width)],
                preferred_element_type=F32,
            )
            self.outbox[pl.ds(i * 16, 16)] = rows.reshape(16, 8, self.width).astype(BF16)
            return carry

        lax.fori_loop(0, 8, one, 0)

    def whole(self):
        slots = pl.ds(0, DEVICES - 1)
        peer = (device_number() + 1) % DEVICES
        return pltpu.make_async_remote_copy(
            src_ref=self.outbox.at[slots], dst_ref=self.inbox.at[slots], send_sem=self.sems.at[0],
            recv_sem=self.sems.at[1], device_id=(peer // 16, peer % 16), device_id_type=MESH,
        )

    def kept(self):
        me = device_number()
        return pltpu.make_async_copy(self.outbox.at[me], self.inbox.at[me], self.sems.at[2])

    def start(self):
        me = device_number()
        self.kept().start()

        def one(step, carry):
            peer = (me + step) % DEVICES
            pltpu.make_async_remote_copy(
                src_ref=self.outbox.at[peer], dst_ref=self.inbox.at[me], send_sem=self.sems.at[0],
                recv_sem=self.sems.at[1], device_id=(peer // 16, peer % 16), device_id_type=MESH,
            ).start()
            return carry

        lax.fori_loop(1, DEVICES, one, 0)

    def collect(self, flat):
        self.kept().wait()
        self.whole().wait_recv()

        def one(i, carry):
            rows = self.inbox[pl.ds(i * 16, 16)].astype(F32).reshape(128, self.width)
            flat[pl.ds(pl.multiple_of(i * 128, 128), 128), pl.ds(0, self.width)] = rows.astype(BF16)
            return carry

        lax.fori_loop(0, 8, one, 0)

    def finish(self):
        self.whole().wait_send()


def pick_rows(table, flat_row):
    def one(i, carry):
        slot = lax.broadcasted_iota(jnp.int32, (128, table.shape[1]), 0) + i * 128
        table[pl.ds(pl.multiple_of(i * 128, 128), 128)] = jnp.where(slot == flat_row, 1.0, 0.0).astype(BF16)
        return carry

    lax.fori_loop(0, table.shape[0] // 128, one, 0)


def pick_slots(table, flat_col):
    def one(i, carry):
        at = pl.ds(pl.multiple_of(i * 128, 128), 128)
        slot = lax.broadcasted_iota(jnp.int32, (128, table.shape[1]), 1)
        table[at] = jnp.where(slot == flat_col[at], 1.0, 0.0).astype(BF16)
        return carry

    lax.fori_loop(0, table.shape[0] // 128, one, 0)


def upright(row):
    return jnp.broadcast_to(row, (128, row.shape[1])).T


def rank_row(group, order, side):
    count = group.shape[1]
    side[0, pl.ds(0, count)] = upright(group)
    side[1, pl.ds(0, count)] = upright(order)

    def one(i, total):
        at = pl.ds(pl.multiple_of(i * 128, 128), 128)
        before = (side[0, at, pl.ds(0, 1)] == group) & (side[1, at, pl.ds(0, 1)] < order)
        return total + jnp.sum(jnp.where(before, 1, 0), axis=0, keepdims=True)

    return lax.fori_loop(0, count // 128, one, jnp.zeros((1, count), jnp.int32))


def column_tables(cols, tables):
    count = cols.shape[1]
    block = cols // 4
    tile = ((block % 2) * 8 + ((block // 2) % 4) * 2 + block // 8) * 4 + cols % 4
    entry = lax.broadcasted_iota(jnp.int32, (1, count), 1)
    key = tile * count + entry
    rank = jnp.sum(jnp.where(upright(key)[:, :1] < key, 1, 0), axis=0, keepdims=True)
    place_of, tile_of = upright(rank)[:, :1], upright(tile)[:, :1]
    source = lax.broadcasted_iota(jnp.int32, (count, count), 0)
    spot = lax.broadcasted_iota(jnp.int32, (count, count), 1)
    add = lambda values: jnp.sum(values, axis=0, keepdims=True)
    pick = add(jnp.where(place_of == spot, source, 0))
    here = add(jnp.where(place_of == spot, tile_of, 0))
    before = add(jnp.where(place_of == spot - 1, tile_of + 1, 0)) - 1
    tables[0:1] = pick
    tables[1:2] = pick // 8
    tables[2:3] = jnp.where(here == before, 1, 0)
    tables[3:4] = jnp.maximum(add(jnp.where(tile_of <= spot, 1, 0)) - 1, 0)
    tables[4:5] = jnp.minimum(add(jnp.where(tile_of == spot, 1, 0)), 1)
    tables[5:8] = jnp.zeros((3, count), jnp.int32)


def each_block(count, body):
    def one(i, carry):
        body(i, pl.ds(pl.multiple_of(i * 128, 128), 128))
        return carry

    lax.fori_loop(0, count, one, 0)


class Copies:
    def __init__(self, send, recv):
        self.send, self.recv, self.used, self.started = send, recv, 0, []

    def remote(self, src, dst, device):
        i, self.used = self.used, self.used + 1
        copy = pltpu.make_async_remote_copy(
            src_ref=src, dst_ref=dst, send_sem=self.send.at[i], recv_sem=self.recv.at[i],
            device_id=device, device_id_type=MESH,
        )
        copy.start()
        self.started.append(copy)
        return copy

    def local(self, src, dst):
        i, self.used = self.used, self.used + 1
        copy = pltpu.make_async_copy(src, dst, self.recv.at[i])
        copy.start()
        return copy

    def finish(self):
        for copy in self.started:
            copy.wait_send()


FAR_FIRST = (2, 1, 3)
NEXT = (1, 3)


class Gather:
    def __init__(self, copies, source, held, slot, ring, place_in_ring, across):
        self.copies, self.source, self.held, self.slot = copies, source, held, slot
        self.ring, self.place, self.across = ring, place_in_ring, across
        self.first, self.last = {}, []

    def tiles(self, side, step, first=0, count=4):
        return self.held.at[pl.ds(self.slot(side, (self.place + step) % 4) * 4 + first, count)]

    def over(self):
        mine = self.tiles(0, 0)
        self.kept = self.copies.local(self.source, mine)
        self.crossing = self.copies.remote(self.source, mine, self.across)

    def own(self):
        self.first[0] = [self.copies.remote(self.source, self.tiles(0, 0), self.ring(d)) for d in NEXT]

    def onward(self):
        self.crossing.wait_recv()
        block = self.tiles(1, 0)
        self.first[1] = [self.copies.remote(block, block, self.ring(d)) for d in NEXT]

    def pass_on(self, side):
        for copy, d in zip(self.first[side], NEXT):
            copy.wait_recv()
            half = self.tiles(side, -d, 0 if d == 1 else 2, 2)
            self.last.append(self.copies.remote(half, half, self.ring(d)))

    def wait(self):
        self.kept.wait()
        for copy in self.last:
            copy.wait_recv()


class Sum:
    def __init__(self, copies, part, base, via, near, cross, crossed, ring, place_in_ring, side, across):
        self.copies, self.part, self.base, self.via, self.near = copies, part, base, via, near
        self.cross, self.crossed, self.ring, self.place = cross, crossed, ring, place_in_ring
        self.side, self.across = side, across

    def at(self, step, first=0):
        return self.base + (self.place + step) % 4 * 8 + first

    def far(self):
        self.vias = []
        for d, first in zip(NEXT, (0, 4)):
            self.vias.append(
                self.copies.remote(
                    self.part.at[pl.ds(self.at(2, first), 4)], self.via.at[pl.ds(first, 4)], self.ring(d)
                )
            )

    def hop(self):
        self.nears = []
        for n, (d, first) in enumerate(zip(NEXT, (0, 4))):
            start = self.at(d, first)

            def one(i, carry):
                self.part[start + i] = (self.part[start + i].astype(F32) + self.via[first + i].astype(F32)).astype(BF16)
                return carry

            self.vias[n].wait_recv()
            lax.fori_loop(0, 4, one, 0)
            self.nears.append(
                self.copies.remote(self.part.at[pl.ds(self.at(d), 8)], self.near.at[pl.ds(n * 8, 8)], self.ring(d))
            )

    def total(self, side, i):
        total = (
            self.part[self.at(0, side * 4 + i)].astype(F32)
            + self.near[side * 4 + i].astype(F32)
            + self.near[8 + side * 4 + i].astype(F32)
        )
        return total

    def over(self):
        for copy in self.nears:
            copy.wait_recv()

        def one(i, carry):
            self.cross[i] = self.total(1 - self.side, i).astype(BF16)
            return carry

        lax.fori_loop(0, 4, one, 0)
        self.crossing = self.copies.remote(self.cross, self.crossed, self.across)

    def finish(self, body):
        self.crossing.wait_recv()

        def one(i, carry):
            body(i, self.total(self.side, i) + self.crossed[i].astype(F32))
            return carry

        lax.fori_loop(0, 4, one, 0)


def held_tile(col):
    block = lax.shift_right_logical(col, 2)
    half = (block & 1) * 8 + lax.shift_right_logical(block, 3) * 4 + (lax.shift_right_logical(block, 1) & 3)
    return half * 4 + (col & 3)


def forward_kernel(
    cols_ref, cols_row, nodes, position, degree, features, cotangent, mask_hbm,
    out_ref, x_ref, node_extra, own_col, node_row, tables, mask, *rest
):
    held, part, near, cross, crossed, (send, recv) = (
        rest[0:4], rest[4:8], rest[8:12], rest[12:16], rest[16:20], rest[20:22]
    )
    xl, y, xh, z, k = place()
    copies = Copies(send, recv)
    mask_copy = copies.local(mask_hbm, mask)
    packing, unpacking, flat, flat_extra = rest[22:26]
    relays = [Relay(rest[26], rest[27], rest[28]), Relay(rest[29], rest[30], rest[31])]
    extra_relay = Relay(rest[32], rest[33], rest[34])
    extra, side, node_col = rest[35:38]
    width = features.shape[1]
    greet()
    lane = lax.broadcasted_iota(jnp.int32, nodes.shape, 1)
    dest = nodes[...] // width
    own_row = dest * 8 + rank_row(dest, lane, side)
    pick_rows(packing, own_row)
    relays[0].pack(packing, features, 0)
    meet()
    relays[0].start()
    relays[1].pack(packing, features, 256)
    relays[1].start()
    source = position[...] // width
    node_slot = source * 8 + rank_row(source, position[...], side)
    node_row[...] = node_slot
    node_col[...] = upright(node_slot)[:, :1]
    pick_slots(unpacking, node_col)
    own_col[...] = upright(own_row)[:, :1]
    column_tables(cols_row[...], tables)
    extra[:, pl.ds(0, width)] = cotangent[...]
    extra[:, pl.ds(width, 128)] = upright(degree[...]).astype(F32).astype(BF16)
    extra_relay.pack(packing, extra, 0)

    def unpack(c):
        if c % 2 == 0:
            relays[c // 2].collect(flat)

        def one(i, at):
            rows = jnp.dot(unpacking[at], flat[:, pl.ds(c % 2 * 128, 128)], preferred_element_type=F32)
            x_ref[c, i] = rows.astype(BF16)

        each_block(4, one)

    def unpack_extra():
        extra_relay.collect(flat_extra)

        def one(i, at):
            node_extra[at] = jnp.dot(unpacking[at], flat_extra[...], preferred_element_type=F32).astype(BF16)

        each_block(4, one)

    tiles = lambda slot: pl.ds(slot * 4, 4)
    mine, pair = k * 8 + xh * 4 + z, k * 8 + (1 - xh) * 4 + z
    gathered, over, swap, row_copies, cross_copy = [[] for _ in range(4)], {}, {}, {}, {}

    def own(c):
        gathered[c].append(copies.local(x_ref.at[c], held[c].at[tiles(mine)]))
        over[c] = copies.remote(x_ref.at[c], held[c].at[tiles(mine)], at_device(xl, y, 1 - xh, z, k))
        for d in FAR_FIRST:
            to = at_device(xl, y, xh, (z + d) % 4, k)
            gathered[c].append(copies.remote(x_ref.at[c], held[c].at[tiles(mine)], to))

    def onward(c):
        over[c].wait_recv()
        for d in FAR_FIRST:
            to = at_device(xl, y, xh, (z + d) % 4, k)
            gathered[c].append(copies.remote(held[c].at[tiles(pair)], held[c].at[tiles(pair)], to))

    def swap_cores(c):
        gathered[c][0].wait()
        for copy in gathered[c][1:]:
            copy.wait_recv()
        half = held[c].at[pl.ds(k * 32, 32)]
        swap[c] = copies.remote(half, half, at_device(xl, y, xh, z, 1 - k))

    def product(c):
        swap[c].wait_recv()
        row_copies[c] = []
        for d in FAR_FIRST + (0,):
            to_y = (y + d) % 4

            def one(q, carry):
                t = (q // 4) * 16 + to_y * 4 + q % 4
                left = jnp.concatenate([mask[t * 8 + j] for j in range(8)], axis=1)
                right = jnp.concatenate([held[c][held_tile(cols_ref[t * 8 + j])] for j in range(8)], axis=0)
                part[c][to_y * 8 + q] = jnp.dot(left, right, preferred_element_type=F32).astype(BF16)
                return carry

            lax.fori_loop(0, 8, one, 0)
            if d:
                i = FAR_FIRST.index(d)
                row_copies[c].append(
                    copies.remote(
                        part[c].at[pl.ds(to_y * 8, 8)], near[c].at[pl.ds(i * 8, 8)], at_device(xl, to_y, xh, z, k)
                    )
                )

    def row_sum(c, side, i):
        total = part[c][y * 8 + side * 4 + i].astype(F32)
        for n in range(3):
            total = total + near[c][n * 8 + side * 4 + i].astype(F32)
        return total

    def sum_rows(c):
        for copy in row_copies[c]:
            copy.wait_recv()

        def one(i, carry):
            cross[c][i] = row_sum(c, 1 - xl, i).astype(BF16)
            return carry

        lax.fori_loop(0, 4, one, 0)
        cross_copy[c] = copies.remote(cross[c], crossed[c], at_device(1 - xl, y, xh, z, k))

    def sum_cross(c):
        cross_copy[c].wait_recv()

        def one(i, carry):
            out_ref[c, i] = row_sum(c, xl, i) + crossed[c][i].astype(F32)
            return carry

        lax.fori_loop(0, 4, one, 0)

    unpack(0)
    own(0)
    unpack(1)
    onward(0)
    own(1)
    unpack(2)
    onward(1)
    swap_cores(0)
    own(2)
    unpack(3)
    mask_copy.wait()
    product(0)
    onward(2)
    swap_cores(1)
    own(3)
    product(1)
    onward(3)
    swap_cores(2)
    extra_relay.start()
    sum_rows(0)
    product(2)
    swap_cores(3)
    sum_rows(1)
    sum_cross(0)
    product(3)
    sum_rows(2)
    sum_cross(1)
    unpack_extra()
    sum_rows(3)
    sum_cross(2)
    sum_cross(3)
    copies.finish()
    for relay in relays + [extra_relay]:
        relay.finish()


def remote_params(ident):
    return params(collective_id=ident, has_side_effects=True)


SMEM_SPEC = pl.BlockSpec(memory_space=pltpu.SMEM)
VMEM_SPEC = pl.BlockSpec(memory_space=pltpu.VMEM)
ANY_SPEC = pl.BlockSpec(memory_space=pl.ANY)


def tile_buffer(count):
    return pltpu.VMEM((count, 128, 128), BF16)


def boxes(width):
    return [
        pltpu.VMEM((DEVICES, 8, width), BF16),
        pltpu.VMEM((DEVICES, 8, width), BF16),
        pltpu.SemaphoreType.DMA((3,)),
    ]


def forward_exchange(cols, nodes, position, degree, features, cotangent, masks):
    rows, width = features.shape
    slots, wide = DEVICES * 8, width + 128
    tiled = (4, 4, 128, 128)
    count = cols.shape[0]
    as_row = lambda values: values.reshape(1, -1)
    return pl.pallas_call(
        forward_kernel,
        in_specs=[SMEM_SPEC] + [VMEM_SPEC] * 6 + [ANY_SPEC],
        out_specs=[VMEM_SPEC] * 6,
        out_shape=[
            jax.ShapeDtypeStruct(tiled, F32),
            jax.ShapeDtypeStruct(tiled, BF16),
            jax.ShapeDtypeStruct((rows, wide), BF16),
            jax.ShapeDtypeStruct((rows, 1), jnp.int32),
            jax.ShapeDtypeStruct((1, rows), jnp.int32),
            jax.ShapeDtypeStruct((8, count), jnp.int32),
        ],
        scratch_shapes=[tile_buffer(256)]
        + [tile_buffer(64)] * 4
        + [tile_buffer(32)] * 4
        + [tile_buffer(24)] * 4
        + [tile_buffer(4)] * 8
        + [pltpu.SemaphoreType.DMA((64,)), pltpu.SemaphoreType.DMA((64,))]
        + [pltpu.VMEM((slots, rows), BF16), pltpu.VMEM((rows, slots), BF16)]
        + [pltpu.VMEM((slots, width // 2), BF16), pltpu.VMEM((slots, wide), BF16)]
        + boxes(width // 2) * 2
        + boxes(wide)
        + [pltpu.VMEM((rows, wide), BF16), pltpu.VMEM((2, rows, 128), jnp.int32), pltpu.VMEM((rows, 1), jnp.int32)],
        compiler_params=remote_params(0),
        name="forward_exchange",
    )(cols, as_row(cols), as_row(nodes), as_row(position), as_row(degree), features, cotangent, masks)


def backward_kernel(
    scale, tables, node_row, own_col, summed, x_ref, extra, self_weight, neigh_weight, mask_hbm,
    hidden_out, grad_out, sum_ref, mask, chain, hidden, own_back, s_ref, g_ref, slopes, aggregate, *rest
):
    held, block, traded, via, near, cross, crossed = [rest[i : i + 4] for i in range(0, 28, 4)]
    send, recv = rest[28:30]
    rest = rest[4:]
    g_core, g_traded, g_half, g_quarter, g_part, g_eighth, g_piece = rest[26:33]
    xl, y, xh, z, k = place()
    copies = Copies(send, recv)
    mask_copy = copies.local(mask_hbm, mask)
    packing, unpacking, flat, joined = rest[33:37]
    hidden_relay = Relay(rest[37], rest[38], rest[39])
    relays = [Relay(rest[i], rest[i + 1], rest[i + 2]) for i in (40, 43, 46)]
    greet()
    each_big = lambda body: lax.fori_loop(0, 2, lambda i, carry: body(i, pl.ds(pl.multiple_of(i * 256, 256), 256)), 0)

    def dense_front(i, at):
        whole = lambda ref: jnp.concatenate([ref[c, pl.ds(i * 2, 2)].reshape(256, 128) for c in range(4)], axis=1)
        degrees = extra[at, pl.ds(512, 1)].astype(F32)
        mean = (whole(summed) / degrees).astype(BF16)
        aggregate[at] = mean
        preact = jnp.dot(whole(x_ref), self_weight[...], preferred_element_type=F32) + jnp.dot(
            mean, neigh_weight[...], preferred_element_type=F32
        )
        gate = jax.nn.sigmoid(preact)
        hidden[at] = (preact * gate).astype(BF16)
        slope = (extra[at, pl.ds(0, 512)].astype(F32) * gate * (1.0 + preact * (1.0 - gate))).astype(BF16)
        slopes[at] = slope
        spread = lax.dot_general(slope, neigh_weight[...], COL_T, preferred_element_type=F32) / degrees
        for c in range(4):
            for n in range(2):
                s_ref[c, i * 2 + n] = spread[n * 128 : (n + 1) * 128, c * 128 : (c + 1) * 128].T.astype(BF16)
        return 0

    def dense_own(i, at):
        own_back[at] = lax.dot_general(slopes[at], self_weight[...], COL_T, preferred_element_type=F32)
        return 0

    def dense_grads(c, at):
        columns = x_ref[c].reshape(512, 128)
        g_ref[at] = lax.dot_general(columns, slopes[...], ROW_T, preferred_element_type=F32)
        means = aggregate[:, pl.ds(pl.multiple_of(c * 128, 128), 128)]
        below = pl.ds(pl.multiple_of(512 + c * 128, 128), 128)
        g_ref[below] = lax.dot_general(means, slopes[...], ROW_T, preferred_element_type=F32)

    each_big(dense_front)
    meet()
    ring_z = lambda d: at_device(xl, y, xh, (z + d) % 4, k)
    ring_y = lambda d: at_device(xl, (y + d) % 4, xh, z, k)
    slot = lambda side, at: (xl + side) % 2 * 4 + at
    gather = [
        Gather(copies, s_ref.at[c], held[c], slot, ring_y, y, at_device(1 - xl, y, xh, z, k)) for c in range(4)
    ]
    cols = [
        Sum(
            copies, block[c], k * 32, via[c], near[c], cross[c], crossed[c], ring_z, z, xh,
            at_device(xl, y, 1 - xh, z, k),
        )
        for c in range(4)
    ]
    trade = {}

    def product(c, *between):
        gather[c].wait()

        def one(g, total):
            for u in range(8):
                e = g * 8 + u
                piece = jnp.dot(held[c][tables[1, e]], mask[tables[0, e]], preferred_element_type=F32)
                total = total * tables[2, e].astype(F32) + piece
                chain[e] = total.astype(BF16)
            return total

        total = jnp.zeros((128, 128), F32)
        for n in range(4):
            total = lax.fori_loop(n * 8, n * 8 + 8, one, total)
            for action in between[n : n + 1]:
                action()

        def settle(p, carry):
            block[c][p] = (chain[tables[3, p]].astype(F32) * tables[4, p].astype(F32)).astype(BF16)
            return carry

        lax.fori_loop(0, 64, settle, 0)
        trade[c] = copies.remote(
            block[c].at[pl.ds((1 - k) * 32, 32)], traded[c], at_device(xl, y, xh, z, 1 - k)
        )

    def sum_cores(c):
        trade[c].wait_recv()

        def one(i, carry):
            block[c][k * 32 + i] = (block[c][k * 32 + i].astype(F32) + traded[c][i].astype(F32)).astype(BF16)
            return carry

        lax.fori_loop(0, 32, one, 0)
        cols[c].far()

    def finish(c):
        def body(i, total):
            at = (pl.ds(pl.multiple_of(i * 128, 128), 128), pl.ds(c * 128, 128))
            joined[at] = (own_back[at] + total.T).astype(BF16)

        cols[c].finish(body)

    width = g_ref.shape[1]
    quarter_at = k * 512 + z * 128
    x_index = xl * 2 + xh
    x_others = [((xl + a) % 2, (xh + b) % 2) for a, b in ((1, 1), (0, 1), (1, 0))]
    level = {}

    def blocks(count, size, body):
        def one(i, carry):
            body(pl.ds(pl.multiple_of(i * size, size), size), i * size)
            return carry

        lax.fori_loop(0, count, one, 0)

    def rows_of(base, offset, size):
        return pl.ds(pl.multiple_of(base + offset, size), size)

    def grad_core():
        def body(at, offset):
            g_core[at] = g_ref[rows_of((1 - k) * 512, offset, 64)].astype(BF16)

        blocks(8, 64, body)
        level["core"] = copies.remote(g_core, g_traded, at_device(xl, y, xh, z, 1 - k))

    def grad_z():
        level["core"].wait_recv()

        def body(at, offset):
            g_half[at] = (g_ref[rows_of(k * 512, offset, 64)] + g_traded[at].astype(F32)).astype(BF16)

        blocks(8, 64, body)
        level["z"] = []
        for i, d in enumerate(FAR_FIRST):
            to_z = (z + d) % 4
            level["z"].append(
                copies.remote(g_half.at[rows_of(0, to_z * 128, 128)], g_quarter.at[i], at_device(xl, y, xh, to_z, k))
            )

    def grad_y():
        for copy in level["z"]:
            copy.wait_recv()

        def body(at, offset):
            total = g_ref[rows_of(quarter_at, offset, 32)] + g_traded[rows_of(z * 128, offset, 32)].astype(F32)
            for i in range(3):
                total = total + g_quarter[i, at].astype(F32)
            g_part[0, at] = total

        blocks(4, 32, body)
        level["y"] = []
        for i, d in enumerate(FAR_FIRST):
            to_y = (y + d) % 4
            level["y"].append(
                copies.remote(g_part.at[0, rows_of(0, to_y * 32, 32)], g_eighth.at[i], at_device(xl, to_y, xh, z, k))
            )

    def grad_x():
        for copy in level["y"]:
            copy.wait_recv()
        total = g_part[0, rows_of(0, y * 32, 32)]
        for i in range(3):
            total = total + g_eighth[i]
        g_eighth_sum = g_piece.at[0]
        g_eighth_sum[...] = total
        level["x"] = []
        for i, (a, b) in enumerate(x_others):
            at = rows_of(0, (a * 2 + b) * 8, 8)
            level["x"].append(copies.remote(g_eighth_sum.at[at], g_piece.at[1, pl.ds(i * 8, 8)], at_device(a, y, b, z, k)))

    def grad_total():
        for copy in level["x"]:
            copy.wait_recv()
        total = g_piece[0, rows_of(0, x_index * 8, 8)]
        for i in range(3):
            total = total + g_piece[1, pl.ds(i * 8, 8)]
        at = (k, z, y, rows_of(0, x_index * 8, 8))
        sum_ref[at] = total * scale
        level["to_x"] = [copies.remote(sum_ref.at[at], sum_ref.at[at], at_device(a, y, b, z, k)) for a, b in x_others]

    def grad_to_z():
        for copy in level["to_x"]:
            copy.wait_recv()
        at = sum_ref.at[k, z, y]
        level["to_z"] = [copies.remote(at, at, at_device(xl, y, xh, (z + d) % 4, k)) for d in FAR_FIRST]

    def grad_to_y():
        for copy in level["to_z"]:
            copy.wait_recv()
        at = sum_ref.at[k, :, y]
        level["to_y"] = [copies.remote(at, at, at_device(xl, (y + d) % 4, xh, z, k)) for d in FAR_FIRST]

    def grad_to_core():
        for copy in level["to_y"]:
            copy.wait_recv()
        level["to_core"] = copies.remote(sum_ref.at[k], sum_ref.at[k], at_device(xl, y, xh, z, 1 - k))

    def take(relay, out, first):
        relay.collect(flat)

        def one(i, at):
            rows = jnp.dot(unpacking[at], flat[:, pl.ds(0, relay.width)], preferred_element_type=F32)
            out[at, pl.ds(first, relay.width)] = rows.astype(BF16)

        each_block(4, one)

    def send(relay, first):
        relay.pack(packing, joined, first)
        relay.start()

    def steps(*actions):
        def run():
            for action in actions:
                action()

        return run

    def passing(c, side):
        return lambda: gather[c].pass_on(side)

    def paired(c):
        return lambda: sum_cores(c)

    for c in range(4):
        gather[c].over()
    gather[0].own()
    pick_rows(packing, node_row[...])
    gather[0].onward()
    hidden_relay.pack(packing, hidden, 0)
    gather[0].pass_on(0)
    gather[0].pass_on(1)
    gather[1].own()
    gather[1].onward()
    each_block(4, dense_grads)
    grad_core()
    each_big(dense_own)
    pick_slots(unpacking, own_col)
    mask_copy.wait()
    product(
        0,
        steps(passing(1, 0), grad_z),
        steps(passing(1, 1), gather[2].own),
        gather[2].onward,
    )
    product(
        1,
        steps(paired(0), passing(2, 0), grad_y),
        steps(passing(2, 1), gather[3].own, gather[3].onward),
        steps(cols[0].hop, grad_x),
    )
    product(
        2,
        steps(paired(1), passing(3, 0)),
        steps(passing(3, 1), cols[0].over, hidden_relay.start),
        steps(cols[1].hop, grad_total),
    )
    product(
        3,
        steps(paired(2), lambda: finish(0)),
        steps(cols[1].over, grad_to_z),
        steps(cols[2].hop, lambda: finish(1), lambda: send(relays[0], 0)),
    )
    sum_cores(3)
    grad_to_y()
    cols[2].over()
    cols[3].hop()
    take(hidden_relay, hidden_out, 0)
    finish(2)
    send(relays[1], 256)
    cols[3].over()
    grad_to_core()
    finish(3)
    send(relays[2], 384)
    take(relays[0], grad_out, 0)
    take(relays[1], grad_out, 256)
    take(relays[2], grad_out, 384)
    level["to_core"].wait_recv()
    copies.finish()
    for relay in relays + [hidden_relay]:
        relay.finish()


def backward_exchange(tables, node_row, own_col, summed, x, extra, self_weight, neigh_weight, masks, scale):
    rows, width = extra.shape[0], self_weight.shape[0]
    slots = DEVICES * 8
    return pl.pallas_call(
        functools.partial(backward_kernel, scale),
        in_specs=[SMEM_SPEC] + [VMEM_SPEC] * 7 + [ANY_SPEC],
        out_specs=[VMEM_SPEC] * 3,
        out_shape=[
            jax.ShapeDtypeStruct((rows, width), BF16),
            jax.ShapeDtypeStruct((rows, width), BF16),
            jax.ShapeDtypeStruct((2, 4, 4, 32, width), F32),
        ],
        scratch_shapes=[tile_buffer(256), tile_buffer(256)]
        + [pltpu.VMEM((rows, width), BF16), pltpu.VMEM((rows, width), F32), pltpu.VMEM(x.shape, BF16)]
        + [pltpu.VMEM((2 * rows, width), F32), pltpu.VMEM((rows, width), BF16), pltpu.VMEM((rows, width), BF16)]
        + [tile_buffer(32)] * 4
        + [tile_buffer(64)] * 4
        + [tile_buffer(32)] * 4
        + [tile_buffer(8)] * 4
        + [tile_buffer(16)] * 4
        + [tile_buffer(4)] * 8
        + [pltpu.SemaphoreType.DMA((128,)), pltpu.SemaphoreType.DMA((128,))]
        + [pltpu.VMEM((512, 512), BF16)] * 3
        + [pltpu.VMEM((3, 128, 512), BF16), pltpu.VMEM((1, 128, 512), F32)]
        + [pltpu.VMEM((3, 32, 512), F32), pltpu.VMEM((2, 32, 512), F32)]
        + [pltpu.VMEM((slots, rows), BF16), pltpu.VMEM((rows, slots), BF16)]
        + [pltpu.VMEM((slots, width), BF16), pltpu.VMEM((rows, width), BF16)]
        + boxes(width)
        + boxes(width // 2)
        + boxes(width // 4) * 2,
        compiler_params=remote_params(1),
        name="backward_exchange",
    )(tables, node_row, own_col, summed, x, extra, self_weight, neigh_weight, masks)


def on_device(
    features, tile_cols, tile_masks, degree, owner_nodes, owner_position, self_weight, neigh_weight, cotangent
):
    rows, width = features.shape
    masks = tile_masks.reshape(-1, *tile_masks.shape[-2:])
    summed, node_x, node_extra, own_col, node_row, tables = forward_exchange(
        tile_cols.reshape(-1), owner_nodes, owner_position, degree, features, cotangent, masks
    )
    grad_scale = 1.0 / math.sqrt(rows * DEVICES)
    hidden_out, grad_out, sums = backward_exchange(
        tables, node_row, own_col, summed, node_x, node_extra, self_weight, neigh_weight, masks, grad_scale
    )
    sums = sums.reshape(2, width, width)
    return hidden_out, grad_out, sums[0], sums[1]


def solution(mesh):
    both = P(("row", "col"))
    wide = P(("row", "col"), None)
    placed = (
        wide,
        P("row", "col", None, None),
        P("row", "col", None, None, None, None),
        both,
        both,
        both,
        P(),
        P(),
        wide,
    )
    return jax.shard_map(
        on_device, mesh=mesh, in_specs=placed, out_specs=(wide, wide, P(), P()), check_vma=False
    )
```

```python
import functools
import math

import jax
import jax.numpy as jnp
from jax import lax
from jax.experimental import pallas as pl
from jax.experimental.pallas import tpu as pltpu
from jax.sharding import PartitionSpec as P

F32 = jnp.float32
DEVICES = 128
UNROLL = 8
BF16 = jnp.bfloat16
MESH = pl.DeviceIdType.MESH
VMEM_LIMIT = 60 * 1024 * 1024
ROW_T = (((0,), (0,)), ((), ()))
COL_T = (((1,), (1,)), ((), ()))


def params(**kw):
    return pltpu.CompilerParams(vmem_limit_bytes=VMEM_LIMIT, **kw)


def place():
    r, c = lax.axis_index("row"), lax.axis_index("col")
    return r // 4, r % 4, c // 8, (c // 2) % 4, c % 2


def at_device(xl, y, xh, z, k):
    return (xl * 4 + y, xh * 8 + z * 2 + k)


def device_number():
    return lax.axis_index("row") * 16 + lax.axis_index("col")


def each_peer(me, body):
    def some(first, count):
        for step in range(count):
            peer = lax.rem(me + first + step, DEVICES)
            body(peer, lax.div(peer, 16), lax.rem(peer, 16))

    def one(i, carry):
        some(i * UNROLL, UNROLL)
        return carry

    some(1, UNROLL - 1)
    lax.fori_loop(1, DEVICES // UNROLL, one, 0)


def greet():
    barrier, me = pltpu.get_barrier_semaphore(), device_number()

    def one(peer, row, col):
        pl.semaphore_signal(barrier, inc=1, device_id=(row, col), device_id_type=MESH)

    each_peer(me, one)


def meet():
    pl.semaphore_wait(pltpu.get_barrier_semaphore(), DEVICES - 1)


class Relay:
    def __init__(self, outbox, inbox, sems):
        self.outbox, self.inbox, self.sems = outbox, inbox, sems
        self.width = outbox.shape[2]

    def pack(self, spread_out, data, first):
        def one(i, carry):
            rows = jnp.dot(
                spread_out[pl.ds(pl.multiple_of(i * 128, 128), 128)],
                data[:, pl.ds(first, self.width)],
                preferred_element_type=F32,
            )
            self.outbox[pl.ds(i * 16, 16)] = rows.reshape(16, 8, self.width).astype(BF16)
            return carry

        lax.fori_loop(0, 8, one, 0)

    def whole(self):
        slots = pl.ds(0, DEVICES - 1)
        peer = (device_number() + 1) % DEVICES
        return pltpu.make_async_remote_copy(
            src_ref=self.outbox.at[slots], dst_ref=self.inbox.at[slots], send_sem=self.sems.at[0],
            recv_sem=self.sems.at[1], device_id=(peer // 16, peer % 16), device_id_type=MESH,
        )

    def kept(self):
        me = device_number()
        return pltpu.make_async_copy(self.outbox.at[me], self.inbox.at[me], self.sems.at[2])

    def start(self):
        me = device_number()
        self.kept().start()

        def one(peer, row, col):
            pltpu.make_async_remote_copy(
                src_ref=self.outbox.at[peer], dst_ref=self.inbox.at[me], send_sem=self.sems.at[0],
                recv_sem=self.sems.at[1], device_id=(row, col), device_id_type=MESH,
            ).start()

        each_peer(me, one)

    def collect(self, flat):
        self.kept().wait()
        self.whole().wait_recv()

        def one(i, carry):
            rows = self.inbox[pl.ds(i * 16, 16)].astype(F32).reshape(128, self.width)
            flat[pl.ds(pl.multiple_of(i * 128, 128), 128), pl.ds(0, self.width)] = rows.astype(BF16)
            return carry

        lax.fori_loop(0, 8, one, 0)

    def finish(self):
        self.whole().wait_send()


def pick_rows(table, flat_row):
    def one(i, carry):
        slot = lax.broadcasted_iota(jnp.int32, (128, table.shape[1]), 0) + i * 128
        table[pl.ds(pl.multiple_of(i * 128, 128), 128)] = jnp.where(slot == flat_row, 1.0, 0.0).astype(BF16)
        return carry

    lax.fori_loop(0, table.shape[0] // 128, one, 0)


def pick_slots(table, flat_col):
    def one(i, carry):
        at = pl.ds(pl.multiple_of(i * 128, 128), 128)
        slot = lax.broadcasted_iota(jnp.int32, (128, table.shape[1]), 1)
        table[at] = jnp.where(slot == flat_col[at], 1.0, 0.0).astype(BF16)
        return carry

    lax.fori_loop(0, table.shape[0] // 128, one, 0)


def upright(row):
    return jnp.broadcast_to(row, (128, row.shape[1])).T


def rank_row(group, order, side):
    count = group.shape[1]
    side[0, pl.ds(0, count)] = upright(group)
    side[1, pl.ds(0, count)] = upright(order)

    def one(i, total):
        at = pl.ds(pl.multiple_of(i * 128, 128), 128)
        before = (side[0, at, pl.ds(0, 1)] == group) & (side[1, at, pl.ds(0, 1)] < order)
        return total + jnp.sum(jnp.where(before, 1, 0), axis=0, keepdims=True)

    return lax.fori_loop(0, count // 128, one, jnp.zeros((1, count), jnp.int32))


def column_tables(cols, tables):
    count = cols.shape[1]
    block = cols // 4
    tile = ((block % 2) * 8 + ((block // 2) % 4) * 2 + block // 8) * 4 + cols % 4
    entry = lax.broadcasted_iota(jnp.int32, (1, count), 1)
    key = tile * count + entry
    rank = jnp.sum(jnp.where(upright(key)[:, :1] < key, 1, 0), axis=0, keepdims=True)
    place_of, tile_of = upright(rank)[:, :1], upright(tile)[:, :1]
    source = lax.broadcasted_iota(jnp.int32, (count, count), 0)
    spot = lax.broadcasted_iota(jnp.int32, (count, count), 1)
    add = lambda values: jnp.sum(values, axis=0, keepdims=True)
    pick = add(jnp.where(place_of == spot, source, 0))
    here = add(jnp.where(place_of == spot, tile_of, 0))
    before = add(jnp.where(place_of == spot - 1, tile_of + 1, 0)) - 1
    tables[0:1] = pick
    tables[1:2] = pick // 8
    tables[2:3] = jnp.where(here == before, 1, 0)
    tables[3:4] = jnp.maximum(add(jnp.where(tile_of <= spot, 1, 0)) - 1, 0)
    tables[4:5] = jnp.minimum(add(jnp.where(tile_of == spot, 1, 0)), 1)
    tables[5:8] = jnp.zeros((3, count), jnp.int32)


def each_block(count, body):
    def one(i, carry):
        body(i, pl.ds(pl.multiple_of(i * 128, 128), 128))
        return carry

    lax.fori_loop(0, count, one, 0)


class Copies:
    def __init__(self, send, recv):
        self.send, self.recv, self.used, self.started = send, recv, 0, []

    def remote(self, src, dst, device):
        i, self.used = self.used, self.used + 1
        copy = pltpu.make_async_remote_copy(
            src_ref=src, dst_ref=dst, send_sem=self.send.at[i], recv_sem=self.recv.at[i],
            device_id=device, device_id_type=MESH,
        )
        copy.start()
        self.started.append(copy)
        return copy

    def local(self, src, dst):
        i, self.used = self.used, self.used + 1
        copy = pltpu.make_async_copy(src, dst, self.recv.at[i])
        copy.start()
        return copy

    def finish(self):
        for copy in self.started:
            copy.wait_send()


FAR_FIRST = (2, 1, 3)
NEXT = (1, 3)


class Gather:
    def __init__(self, copies, source, held, slot, ring, place_in_ring, across):
        self.copies, self.source, self.held, self.slot = copies, source, held, slot
        self.ring, self.place, self.across = ring, place_in_ring, across
        self.first, self.last = {}, []

    def tiles(self, side, step, first=0, count=4):
        return self.held.at[pl.ds(self.slot(side, (self.place + step) % 4) * 4 + first, count)]

    def over(self):
        mine = self.tiles(0, 0)
        self.kept = self.copies.local(self.source, mine)
        self.crossing = self.copies.remote(self.source, mine, self.across)

    def own(self):
        self.first[0] = [self.copies.remote(self.source, self.tiles(0, 0), self.ring(d)) for d in NEXT]

    def onward(self):
        self.crossing.wait_recv()
        block = self.tiles(1, 0)
        self.first[1] = [self.copies.remote(block, block, self.ring(d)) for d in NEXT]

    def pass_on(self, side):
        for copy, d in zip(self.first[side], NEXT):
            copy.wait_recv()
            half = self.tiles(side, -d, 0 if d == 1 else 2, 2)
            self.last.append(self.copies.remote(half, half, self.ring(d)))

    def wait(self):
        self.kept.wait()
        for copy in self.last:
            copy.wait_recv()


class Sum:
    def __init__(self, copies, part, base, via, near, cross, crossed, ring, place_in_ring, side, across):
        self.copies, self.part, self.base, self.via, self.near = copies, part, base, via, near
        self.cross, self.crossed, self.ring, self.place = cross, crossed, ring, place_in_ring
        self.side, self.across = side, across

    def at(self, step, first=0):
        return self.base + (self.place + step) % 4 * 8 + first

    def far(self):
        self.vias = []
        for d, first in zip(NEXT, (0, 4)):
            self.vias.append(
                self.copies.remote(
                    self.part.at[pl.ds(self.at(2, first), 4)], self.via.at[pl.ds(first, 4)], self.ring(d)
                )
            )

    def hop(self):
        self.nears = []
        for n, (d, first) in enumerate(zip(NEXT, (0, 4))):
            start = self.at(d, first)

            def one(i, carry):
                self.part[start + i] = (self.part[start + i].astype(F32) + self.via[first + i].astype(F32)).astype(BF16)
                return carry

            self.vias[n].wait_recv()
            lax.fori_loop(0, 4, one, 0)
            self.nears.append(
                self.copies.remote(self.part.at[pl.ds(self.at(d), 8)], self.near.at[pl.ds(n * 8, 8)], self.ring(d))
            )

    def total(self, side, i):
        total = (
            self.part[self.at(0, side * 4 + i)].astype(F32)
            + self.near[side * 4 + i].astype(F32)
            + self.near[8 + side * 4 + i].astype(F32)
        )
        return total

    def over(self):
        for copy in self.nears:
            copy.wait_recv()

        def one(i, carry):
            self.cross[i] = self.total(1 - self.side, i).astype(BF16)
            return carry

        lax.fori_loop(0, 4, one, 0)
        self.crossing = self.copies.remote(self.cross, self.crossed, self.across)

    def finish(self, body):
        self.crossing.wait_recv()

        def one(i, carry):
            body(i, self.total(self.side, i) + self.crossed[i].astype(F32))
            return carry

        lax.fori_loop(0, 4, one, 0)


def held_tile(col):
    block = lax.shift_right_logical(col, 2)
    half = (block & 1) * 8 + lax.shift_right_logical(block, 3) * 4 + (lax.shift_right_logical(block, 1) & 3)
    return half * 4 + (col & 3)


def forward_kernel(
    cols_ref, cols_row, nodes, position, degree, features, cotangent, mask_hbm,
    out_ref, x_ref, node_extra, own_col, node_row, tables, mask, *rest
):
    held, part, near, cross, crossed, (send, recv) = (
        rest[0:4], rest[4:8], rest[8:12], rest[12:16], rest[16:20], rest[20:22]
    )
    xl, y, xh, z, k = place()
    copies = Copies(send, recv)
    mask_copy = copies.local(mask_hbm, mask)
    packing, unpacking, flat, flat_extra = rest[22:26]
    relays = [Relay(rest[26], rest[27], rest[28]), Relay(rest[29], rest[30], rest[31])]
    extra_relay = Relay(rest[32], rest[33], rest[34])
    extra, side, node_col = rest[35:38]
    width = features.shape[1]
    greet()
    lane = lax.broadcasted_iota(jnp.int32, nodes.shape, 1)
    dest = nodes[...] // width
    own_row = dest * 8 + rank_row(dest, lane, side)
    pick_rows(packing, own_row)
    relays[0].pack(packing, features, 0)
    meet()
    relays[0].start()
    relays[1].pack(packing, features, 256)
    relays[1].start()
    source = position[...] // width
    node_slot = source * 8 + rank_row(source, position[...], side)
    node_row[...] = node_slot
    node_col[...] = upright(node_slot)[:, :1]
    pick_slots(unpacking, node_col)
    own_col[...] = upright(own_row)[:, :1]
    column_tables(cols_row[...], tables)
    extra[:, pl.ds(0, width)] = cotangent[...]
    extra[:, pl.ds(width, 128)] = upright(degree[...]).astype(F32).astype(BF16)
    extra_relay.pack(packing, extra, 0)

    def unpack(c):
        if c % 2 == 0:
            relays[c // 2].collect(flat)

        def one(i, at):
            rows = jnp.dot(unpacking[at], flat[:, pl.ds(c % 2 * 128, 128)], preferred_element_type=F32)
            x_ref[c, i] = rows.astype(BF16)

        each_block(4, one)

    def unpack_extra():
        extra_relay.collect(flat_extra)

        def one(i, at):
            node_extra[at] = jnp.dot(unpacking[at], flat_extra[...], preferred_element_type=F32).astype(BF16)

        each_block(4, one)

    tiles = lambda slot: pl.ds(slot * 4, 4)
    mine, pair = k * 8 + xh * 4 + z, k * 8 + (1 - xh) * 4 + z
    gathered, over, swap, row_copies, cross_copy = [[] for _ in range(4)], {}, {}, {}, {}

    def own(c):
        gathered[c].append(copies.local(x_ref.at[c], held[c].at[tiles(mine)]))
        over[c] = copies.remote(x_ref.at[c], held[c].at[tiles(mine)], at_device(xl, y, 1 - xh, z, k))
        for d in FAR_FIRST:
            to = at_device(xl, y, xh, (z + d) % 4, k)
            gathered[c].append(copies.remote(x_ref.at[c], held[c].at[tiles(mine)], to))

    def onward(c):
        over[c].wait_recv()
        for d in FAR_FIRST:
            to = at_device(xl, y, xh, (z + d) % 4, k)
            gathered[c].append(copies.remote(held[c].at[tiles(pair)], held[c].at[tiles(pair)], to))

    def swap_cores(c):
        gathered[c][0].wait()
        for copy in gathered[c][1:]:
            copy.wait_recv()
        half = held[c].at[pl.ds(k * 32, 32)]
        swap[c] = copies.remote(half, half, at_device(xl, y, xh, z, 1 - k))

    def product(c):
        swap[c].wait_recv()
        row_copies[c] = []
        for d in FAR_FIRST + (0,):
            to_y = (y + d) % 4

            def one(q, carry):
                t = (q // 4) * 16 + to_y * 4 + q % 4
                left = jnp.concatenate([mask[t * 8 + j] for j in range(8)], axis=1)
                right = jnp.concatenate([held[c][held_tile(cols_ref[t * 8 + j])] for j in range(8)], axis=0)
                part[c][to_y * 8 + q] = jnp.dot(left, right, preferred_element_type=F32).astype(BF16)
                return carry

            lax.fori_loop(0, 8, one, 0)
            if d:
                i = FAR_FIRST.index(d)
                row_copies[c].append(
                    copies.remote(
                        part[c].at[pl.ds(to_y * 8, 8)], near[c].at[pl.ds(i * 8, 8)], at_device(xl, to_y, xh, z, k)
                    )
                )

    def row_sum(c, side, i):
        total = part[c][y * 8 + side * 4 + i].astype(F32)
        for n in range(3):
            total = total + near[c][n * 8 + side * 4 + i].astype(F32)
        return total

    def sum_rows(c):
        for copy in row_copies[c]:
            copy.wait_recv()

        def one(i, carry):
            cross[c][i] = row_sum(c, 1 - xl, i).astype(BF16)
            return carry

        lax.fori_loop(0, 4, one, 0)
        cross_copy[c] = copies.remote(cross[c], crossed[c], at_device(1 - xl, y, xh, z, k))

    def sum_cross(c):
        cross_copy[c].wait_recv()

        def one(i, carry):
            out_ref[c, i] = row_sum(c, xl, i) + crossed[c][i].astype(F32)
            return carry

        lax.fori_loop(0, 4, one, 0)

    unpack(0)
    own(0)
    unpack(1)
    onward(0)
    own(1)
    unpack(2)
    onward(1)
    swap_cores(0)
    own(2)
    unpack(3)
    mask_copy.wait()
    product(0)
    onward(2)
    swap_cores(1)
    own(3)
    product(1)
    onward(3)
    swap_cores(2)
    extra_relay.start()
    sum_rows(0)
    product(2)
    swap_cores(3)
    sum_rows(1)
    sum_cross(0)
    product(3)
    sum_rows(2)
    sum_cross(1)
    unpack_extra()
    sum_rows(3)
    sum_cross(2)
    sum_cross(3)
    copies.finish()
    for relay in relays + [extra_relay]:
        relay.finish()


def remote_params(ident):
    return params(collective_id=ident, has_side_effects=True)


SMEM_SPEC = pl.BlockSpec(memory_space=pltpu.SMEM)
VMEM_SPEC = pl.BlockSpec(memory_space=pltpu.VMEM)
ANY_SPEC = pl.BlockSpec(memory_space=pl.ANY)


def tile_buffer(count):
    return pltpu.VMEM((count, 128, 128), BF16)


def boxes(width):
    return [
        pltpu.VMEM((DEVICES, 8, width), BF16),
        pltpu.VMEM((DEVICES, 8, width), BF16),
        pltpu.SemaphoreType.DMA((3,)),
    ]


def forward_exchange(cols, nodes, position, degree, features, cotangent, masks):
    rows, width = features.shape
    slots, wide = DEVICES * 8, width + 128
    tiled = (4, 4, 128, 128)
    count = cols.shape[0]
    as_row = lambda values: values.reshape(1, -1)
    return pl.pallas_call(
        forward_kernel,
        in_specs=[SMEM_SPEC] + [VMEM_SPEC] * 6 + [ANY_SPEC],
        out_specs=[VMEM_SPEC] * 6,
        out_shape=[
            jax.ShapeDtypeStruct(tiled, F32),
            jax.ShapeDtypeStruct(tiled, BF16),
            jax.ShapeDtypeStruct((rows, wide), BF16),
            jax.ShapeDtypeStruct((rows, 1), jnp.int32),
            jax.ShapeDtypeStruct((1, rows), jnp.int32),
            jax.ShapeDtypeStruct((8, count), jnp.int32),
        ],
        scratch_shapes=[tile_buffer(256)]
        + [tile_buffer(64)] * 4
        + [tile_buffer(32)] * 4
        + [tile_buffer(24)] * 4
        + [tile_buffer(4)] * 8
        + [pltpu.SemaphoreType.DMA((64,)), pltpu.SemaphoreType.DMA((64,))]
        + [pltpu.VMEM((slots, rows), BF16), pltpu.VMEM((rows, slots), BF16)]
        + [pltpu.VMEM((slots, width // 2), BF16), pltpu.VMEM((slots, wide), BF16)]
        + boxes(width // 2) * 2
        + boxes(wide)
        + [pltpu.VMEM((rows, wide), BF16), pltpu.VMEM((2, rows, 128), jnp.int32), pltpu.VMEM((rows, 1), jnp.int32)],
        compiler_params=remote_params(0),
        name="forward_exchange",
    )(cols, as_row(cols), as_row(nodes), as_row(position), as_row(degree), features, cotangent, masks)


def backward_kernel(
    scale, tables, node_row, own_col, summed, x_ref, extra, self_weight, neigh_weight, mask_hbm,
    hidden_out, grad_out, sum_ref, mask, chain, hidden, own_back, s_ref, g_ref, slopes, aggregate, *rest
):
    held, block, traded, via, near, cross, crossed = [rest[i : i + 4] for i in range(0, 28, 4)]
    send, recv = rest[28:30]
    rest = rest[4:]
    g_core, g_traded, g_half, g_quarter, g_part, g_eighth, g_piece = rest[26:33]
    xl, y, xh, z, k = place()
    copies = Copies(send, recv)
    mask_copy = copies.local(mask_hbm, mask)
    packing, unpacking, flat, joined = rest[33:37]
    hidden_relay = Relay(rest[37], rest[38], rest[39])
    relays = [Relay(rest[i], rest[i + 1], rest[i + 2]) for i in (40, 43, 46)]
    greet()
    each_big = lambda body: lax.fori_loop(0, 2, lambda i, carry: body(i, pl.ds(pl.multiple_of(i * 256, 256), 256)), 0)

    def dense_front(i, at):
        whole = lambda ref: jnp.concatenate([ref[c, pl.ds(i * 2, 2)].reshape(256, 128) for c in range(4)], axis=1)
        degrees = extra[at, pl.ds(512, 1)].astype(F32)
        mean = (whole(summed) / degrees).astype(BF16)
        aggregate[at] = mean
        preact = jnp.dot(whole(x_ref), self_weight[...], preferred_element_type=F32) + jnp.dot(
            mean, neigh_weight[...], preferred_element_type=F32
        )
        gate = jax.nn.sigmoid(preact)
        hidden[at] = (preact * gate).astype(BF16)
        slope = (extra[at, pl.ds(0, 512)].astype(F32) * gate * (1.0 + preact * (1.0 - gate))).astype(BF16)
        slopes[at] = slope
        spread = lax.dot_general(slope, neigh_weight[...], COL_T, preferred_element_type=F32) / degrees
        for c in range(4):
            for n in range(2):
                s_ref[c, i * 2 + n] = spread[n * 128 : (n + 1) * 128, c * 128 : (c + 1) * 128].T.astype(BF16)
        return 0

    def dense_own(i, at):
        own_back[at] = lax.dot_general(slopes[at], self_weight[...], COL_T, preferred_element_type=F32)
        return 0

    def dense_grads(c, at):
        columns = x_ref[c].reshape(512, 128)
        g_ref[at] = lax.dot_general(columns, slopes[...], ROW_T, preferred_element_type=F32)
        means = aggregate[:, pl.ds(pl.multiple_of(c * 128, 128), 128)]
        below = pl.ds(pl.multiple_of(512 + c * 128, 128), 128)
        g_ref[below] = lax.dot_general(means, slopes[...], ROW_T, preferred_element_type=F32)

    each_big(dense_front)
    meet()
    ring_z = lambda d: at_device(xl, y, xh, (z + d) % 4, k)
    ring_y = lambda d: at_device(xl, (y + d) % 4, xh, z, k)
    slot = lambda side, at: (xl + side) % 2 * 4 + at
    gather = [
        Gather(copies, s_ref.at[c], held[c], slot, ring_y, y, at_device(1 - xl, y, xh, z, k)) for c in range(4)
    ]
    cols = [
        Sum(
            copies, block[c], k * 32, via[c], near[c], cross[c], crossed[c], ring_z, z, xh,
            at_device(xl, y, 1 - xh, z, k),
        )
        for c in range(4)
    ]
    trade = {}

    def product(c, *between):
        gather[c].wait()

        def one(g, total):
            for u in range(8):
                e = g * 8 + u
                piece = jnp.dot(held[c][tables[1, e]], mask[tables[0, e]], preferred_element_type=F32)
                total = total * tables[2, e].astype(F32) + piece
                chain[e] = total.astype(BF16)
            return total

        total = jnp.zeros((128, 128), F32)
        for n in range(4):
            total = lax.fori_loop(n * 8, n * 8 + 8, one, total)
            for action in between[n : n + 1]:
                action()

        def settle(p, carry):
            block[c][p] = (chain[tables[3, p]].astype(F32) * tables[4, p].astype(F32)).astype(BF16)
            return carry

        lax.fori_loop(0, 64, settle, 0)
        trade[c] = copies.remote(
            block[c].at[pl.ds((1 - k) * 32, 32)], traded[c], at_device(xl, y, xh, z, 1 - k)
        )

    def sum_cores(c):
        trade[c].wait_recv()

        def one(i, carry):
            block[c][k * 32 + i] = (block[c][k * 32 + i].astype(F32) + traded[c][i].astype(F32)).astype(BF16)
            return carry

        lax.fori_loop(0, 32, one, 0)
        cols[c].far()

    def finish(c):
        def body(i, total):
            at = (pl.ds(pl.multiple_of(i * 128, 128), 128), pl.ds(c * 128, 128))
            joined[at] = (own_back[at] + total.T).astype(BF16)

        cols[c].finish(body)

    width = g_ref.shape[1]
    quarter_at = k * 512 + z * 128
    x_index = xl * 2 + xh
    x_others = [((xl + a) % 2, (xh + b) % 2) for a, b in ((1, 1), (0, 1), (1, 0))]
    level = {}

    def blocks(count, size, body):
        def one(i, carry):
            body(pl.ds(pl.multiple_of(i * size, size), size), i * size)
            return carry

        lax.fori_loop(0, count, one, 0)

    def rows_of(base, offset, size):
        return pl.ds(pl.multiple_of(base + offset, size), size)

    def grad_core():
        def body(at, offset):
            g_core[at] = g_ref[rows_of((1 - k) * 512, offset, 64)].astype(BF16)

        blocks(8, 64, body)
        level["core"] = copies.remote(g_core, g_traded, at_device(xl, y, xh, z, 1 - k))

    def grad_z():
        level["core"].wait_recv()

        def body(at, offset):
            g_half[at] = (g_ref[rows_of(k * 512, offset, 64)] + g_traded[at].astype(F32)).astype(BF16)

        blocks(8, 64, body)
        level["z"] = []
        for i, d in enumerate(FAR_FIRST):
            to_z = (z + d) % 4
            level["z"].append(
                copies.remote(g_half.at[rows_of(0, to_z * 128, 128)], g_quarter.at[i], at_device(xl, y, xh, to_z, k))
            )

    def grad_y():
        for copy in level["z"]:
            copy.wait_recv()

        def body(at, offset):
            total = g_ref[rows_of(quarter_at, offset, 32)] + g_traded[rows_of(z * 128, offset, 32)].astype(F32)
            for i in range(3):
                total = total + g_quarter[i, at].astype(F32)
            g_part[0, at] = total

        blocks(4, 32, body)
        level["y"] = []
        for i, d in enumerate(FAR_FIRST):
            to_y = (y + d) % 4
            level["y"].append(
                copies.remote(g_part.at[0, rows_of(0, to_y * 32, 32)], g_eighth.at[i], at_device(xl, to_y, xh, z, k))
            )

    def grad_x():
        for copy in level["y"]:
            copy.wait_recv()
        total = g_part[0, rows_of(0, y * 32, 32)]
        for i in range(3):
            total = total + g_eighth[i]
        g_eighth_sum = g_piece.at[0]
        g_eighth_sum[...] = total
        level["x"] = []
        for i, (a, b) in enumerate(x_others):
            at = rows_of(0, (a * 2 + b) * 8, 8)
            level["x"].append(copies.remote(g_eighth_sum.at[at], g_piece.at[1, pl.ds(i * 8, 8)], at_device(a, y, b, z, k)))

    def grad_total():
        for copy in level["x"]:
            copy.wait_recv()
        total = g_piece[0, rows_of(0, x_index * 8, 8)]
        for i in range(3):
            total = total + g_piece[1, pl.ds(i * 8, 8)]
        at = (k, z, y, rows_of(0, x_index * 8, 8))
        sum_ref[at] = total * scale
        level["to_x"] = [copies.remote(sum_ref.at[at], sum_ref.at[at], at_device(a, y, b, z, k)) for a, b in x_others]

    def grad_to_z():
        for copy in level["to_x"]:
            copy.wait_recv()
        at = sum_ref.at[k, z, y]
        level["to_z"] = [copies.remote(at, at, at_device(xl, y, xh, (z + d) % 4, k)) for d in FAR_FIRST]

    def grad_to_y():
        for copy in level["to_z"]:
            copy.wait_recv()
        at = sum_ref.at[k, :, y]
        level["to_y"] = [copies.remote(at, at, at_device(xl, (y + d) % 4, xh, z, k)) for d in FAR_FIRST]

    def grad_to_core():
        for copy in level["to_y"]:
            copy.wait_recv()
        level["to_core"] = copies.remote(sum_ref.at[k], sum_ref.at[k], at_device(xl, y, xh, z, 1 - k))

    def take(relay, out, first):
        relay.collect(flat)

        def one(i, at):
            rows = jnp.dot(unpacking[at], flat[:, pl.ds(0, relay.width)], preferred_element_type=F32)
            out[at, pl.ds(first, relay.width)] = rows.astype(BF16)

        each_block(4, one)

    def send(relay, first):
        relay.pack(packing, joined, first)
        relay.start()

    def steps(*actions):
        def run():
            for action in actions:
                action()

        return run

    def passing(c, side):
        return lambda: gather[c].pass_on(side)

    def paired(c):
        return lambda: sum_cores(c)

    for c in range(4):
        gather[c].over()
    gather[0].own()
    pick_rows(packing, node_row[...])
    gather[0].onward()
    hidden_relay.pack(packing, hidden, 0)
    gather[0].pass_on(0)
    gather[0].pass_on(1)
    gather[1].own()
    gather[1].onward()
    each_block(4, dense_grads)
    grad_core()
    each_big(dense_own)
    pick_slots(unpacking, own_col)
    mask_copy.wait()
    product(
        0,
        steps(passing(1, 0), grad_z),
        steps(passing(1, 1), gather[2].own),
        gather[2].onward,
    )
    product(
        1,
        steps(paired(0), passing(2, 0), grad_y),
        steps(passing(2, 1), gather[3].own, gather[3].onward),
        steps(cols[0].hop, grad_x),
    )
    product(
        2,
        steps(paired(1), passing(3, 0)),
        steps(passing(3, 1), cols[0].over, hidden_relay.start),
        steps(cols[1].hop, grad_total),
    )
    product(
        3,
        steps(paired(2), lambda: finish(0)),
        steps(cols[1].over, grad_to_z),
        steps(cols[2].hop, lambda: finish(1), lambda: send(relays[0], 0)),
    )
    sum_cores(3)
    grad_to_y()
    cols[2].over()
    cols[3].hop()
    take(hidden_relay, hidden_out, 0)
    finish(2)
    send(relays[1], 256)
    cols[3].over()
    grad_to_core()
    finish(3)
    send(relays[2], 384)
    take(relays[0], grad_out, 0)
    take(relays[1], grad_out, 256)
    take(relays[2], grad_out, 384)
    level["to_core"].wait_recv()
    copies.finish()
    for relay in relays + [hidden_relay]:
        relay.finish()


def backward_exchange(tables, node_row, own_col, summed, x, extra, self_weight, neigh_weight, masks, scale):
    rows, width = extra.shape[0], self_weight.shape[0]
    slots = DEVICES * 8
    return pl.pallas_call(
        functools.partial(backward_kernel, scale),
        in_specs=[SMEM_SPEC] + [VMEM_SPEC] * 7 + [ANY_SPEC],
        out_specs=[VMEM_SPEC] * 3,
        out_shape=[
            jax.ShapeDtypeStruct((rows, width), BF16),
            jax.ShapeDtypeStruct((rows, width), BF16),
            jax.ShapeDtypeStruct((2, 4, 4, 32, width), F32),
        ],
        scratch_shapes=[tile_buffer(256), tile_buffer(256)]
        + [pltpu.VMEM((rows, width), BF16), pltpu.VMEM((rows, width), F32), pltpu.VMEM(x.shape, BF16)]
        + [pltpu.VMEM((2 * rows, width), F32), pltpu.VMEM((rows, width), BF16), pltpu.VMEM((rows, width), BF16)]
        + [tile_buffer(32)] * 4
        + [tile_buffer(64)] * 4
        + [tile_buffer(32)] * 4
        + [tile_buffer(8)] * 4
        + [tile_buffer(16)] * 4
        + [tile_buffer(4)] * 8
        + [pltpu.SemaphoreType.DMA((128,)), pltpu.SemaphoreType.DMA((128,))]
        + [pltpu.VMEM((512, 512), BF16)] * 3
        + [pltpu.VMEM((3, 128, 512), BF16), pltpu.VMEM((1, 128, 512), F32)]
        + [pltpu.VMEM((3, 32, 512), F32), pltpu.VMEM((2, 32, 512), F32)]
        + [pltpu.VMEM((slots, rows), BF16), pltpu.VMEM((rows, slots), BF16)]
        + [pltpu.VMEM((slots, width), BF16), pltpu.VMEM((rows, width), BF16)]
        + boxes(width)
        + boxes(width // 2)
        + boxes(width // 4) * 2,
        compiler_params=remote_params(1),
        name="backward_exchange",
    )(tables, node_row, own_col, summed, x, extra, self_weight, neigh_weight, masks)


def on_device(
    features, tile_cols, tile_masks, degree, owner_nodes, owner_position, self_weight, neigh_weight, cotangent
):
    rows, width = features.shape
    masks = tile_masks.reshape(-1, *tile_masks.shape[-2:])
    summed, node_x, node_extra, own_col, node_row, tables = forward_exchange(
        tile_cols.reshape(-1), owner_nodes, owner_position, degree, features, cotangent, masks
    )
    grad_scale = 1.0 / math.sqrt(rows * DEVICES)
    hidden_out, grad_out, sums = backward_exchange(
        tables, node_row, own_col, summed, node_x, node_extra, self_weight, neigh_weight, masks, grad_scale
    )
    sums = sums.reshape(2, width, width)
    return hidden_out, grad_out, sums[0], sums[1]


def solution(mesh):
    both = P(("row", "col"))
    wide = P(("row", "col"), None)
    placed = (
        wide,
        P("row", "col", None, None),
        P("row", "col", None, None, None, None),
        both,
        both,
        both,
        P(),
        P(),
        wide,
    )
    return jax.shard_map(
        on_device, mesh=mesh, in_specs=placed, out_specs=(wide, wide, P(), P()), check_vma=False
    )
```

```python
import functools
import math

import jax
import jax.numpy as jnp
from jax import lax
from jax.experimental import pallas as pl
from jax.experimental.pallas import tpu as pltpu
from jax.sharding import PartitionSpec as P

F32 = jnp.float32
DEVICES = 128
UNROLL = 8
STRIDE = 53
BF16 = jnp.bfloat16
MESH = pl.DeviceIdType.MESH
VMEM_LIMIT = 60 * 1024 * 1024
ROW_T = (((0,), (0,)), ((), ()))
COL_T = (((1,), (1,)), ((), ()))


def params(**kw):
    return pltpu.CompilerParams(vmem_limit_bytes=VMEM_LIMIT, **kw)


def place():
    r, c = lax.axis_index("row"), lax.axis_index("col")
    return r // 4, r % 4, c // 8, (c // 2) % 4, c % 2


def at_device(xl, y, xh, z, k):
    return (xl * 4 + y, xh * 8 + z * 2 + k)


def device_number():
    return lax.axis_index("row") * 16 + lax.axis_index("col")


def each_peer(me, body):
    def some(first, count):
        for step in range(count):
            peer = lax.rem(me + (first + step) * STRIDE, DEVICES)
            body(peer, lax.div(peer, 16), lax.rem(peer, 16))

    def one(i, carry):
        some(i * UNROLL, UNROLL)
        return carry

    some(1, UNROLL - 1)
    lax.fori_loop(1, DEVICES // UNROLL, one, 0)


def greet():
    barrier, me = pltpu.get_barrier_semaphore(), device_number()

    def one(peer, row, col):
        pl.semaphore_signal(barrier, inc=1, device_id=(row, col), device_id_type=MESH)

    each_peer(me, one)


def meet():
    pl.semaphore_wait(pltpu.get_barrier_semaphore(), DEVICES - 1)


class Relay:
    def __init__(self, outbox, inbox, sems):
        self.outbox, self.inbox, self.sems = outbox, inbox, sems
        self.width = outbox.shape[2]

    def pack(self, spread_out, data, first):
        def one(i, carry):
            rows = jnp.dot(
                spread_out[pl.ds(pl.multiple_of(i * 128, 128), 128)],
                data[:, pl.ds(first, self.width)],
                preferred_element_type=F32,
            )
            self.outbox[pl.ds(i * 16, 16)] = rows.reshape(16, 8, self.width).astype(BF16)
            return carry

        lax.fori_loop(0, 8, one, 0)

    def whole(self):
        slots = pl.ds(0, DEVICES - 1)
        peer = (device_number() + 1) % DEVICES
        return pltpu.make_async_remote_copy(
            src_ref=self.outbox.at[slots], dst_ref=self.inbox.at[slots], send_sem=self.sems.at[0],
            recv_sem=self.sems.at[1], device_id=(peer // 16, peer % 16), device_id_type=MESH,
        )

    def kept(self):
        me = device_number()
        return pltpu.make_async_copy(self.outbox.at[me], self.inbox.at[me], self.sems.at[2])

    def start(self):
        me = device_number()
        self.kept().start()

        def one(peer, row, col):
            pltpu.make_async_remote_copy(
                src_ref=self.outbox.at[peer], dst_ref=self.inbox.at[me], send_sem=self.sems.at[0],
                recv_sem=self.sems.at[1], device_id=(row, col), device_id_type=MESH,
            ).start()

        each_peer(me, one)

    def collect(self, flat):
        self.kept().wait()
        self.whole().wait_recv()

        def one(i, carry):
            rows = self.inbox[pl.ds(i * 16, 16)].astype(F32).reshape(128, self.width)
            flat[pl.ds(pl.multiple_of(i * 128, 128), 128), pl.ds(0, self.width)] = rows.astype(BF16)
            return carry

        lax.fori_loop(0, 8, one, 0)

    def finish(self):
        self.whole().wait_send()


def pick_rows(table, flat_row):
    def one(i, carry):
        slot = lax.broadcasted_iota(jnp.int32, (128, table.shape[1]), 0) + i * 128
        table[pl.ds(pl.multiple_of(i * 128, 128), 128)] = jnp.where(slot == flat_row, 1.0, 0.0).astype(BF16)
        return carry

    lax.fori_loop(0, table.shape[0] // 128, one, 0)


def pick_slots(table, flat_col):
    def one(i, carry):
        at = pl.ds(pl.multiple_of(i * 128, 128), 128)
        slot = lax.broadcasted_iota(jnp.int32, (128, table.shape[1]), 1)
        table[at] = jnp.where(slot == flat_col[at], 1.0, 0.0).astype(BF16)
        return carry

    lax.fori_loop(0, table.shape[0] // 128, one, 0)


def upright(row):
    return jnp.broadcast_to(row, (128, row.shape[1])).T


def rank_row(group, order, side):
    count = group.shape[1]
    side[0, pl.ds(0, count)] = upright(group)
    side[1, pl.ds(0, count)] = upright(order)

    def one(i, total):
        at = pl.ds(pl.multiple_of(i * 128, 128), 128)
        before = (side[0, at, pl.ds(0, 1)] == group) & (side[1, at, pl.ds(0, 1)] < order)
        return total + jnp.sum(jnp.where(before, 1, 0), axis=0, keepdims=True)

    return lax.fori_loop(0, count // 128, one, jnp.zeros((1, count), jnp.int32))


def column_tables(cols, tables):
    count = cols.shape[1]
    block = cols // 4
    tile = ((block % 2) * 8 + ((block // 2) % 4) * 2 + block // 8) * 4 + cols % 4
    entry = lax.broadcasted_iota(jnp.int32, (1, count), 1)
    key = tile * count + entry
    rank = jnp.sum(jnp.where(upright(key)[:, :1] < key, 1, 0), axis=0, keepdims=True)
    place_of, tile_of = upright(rank)[:, :1], upright(tile)[:, :1]
    source = lax.broadcasted_iota(jnp.int32, (count, count), 0)
    spot = lax.broadcasted_iota(jnp.int32, (count, count), 1)
    add = lambda values: jnp.sum(values, axis=0, keepdims=True)
    pick = add(jnp.where(place_of == spot, source, 0))
    here = add(jnp.where(place_of == spot, tile_of, 0))
    before = add(jnp.where(place_of == spot - 1, tile_of + 1, 0)) - 1
    tables[0:1] = pick
    tables[1:2] = pick // 8
    tables[2:3] = jnp.where(here == before, 1, 0)
    tables[3:4] = jnp.maximum(add(jnp.where(tile_of <= spot, 1, 0)) - 1, 0)
    tables[4:5] = jnp.minimum(add(jnp.where(tile_of == spot, 1, 0)), 1)
    tables[5:8] = jnp.zeros((3, count), jnp.int32)


def each_block(count, body):
    def one(i, carry):
        body(i, pl.ds(pl.multiple_of(i * 128, 128), 128))
        return carry

    lax.fori_loop(0, count, one, 0)


class Copies:
    def __init__(self, send, recv):
        self.send, self.recv, self.used, self.started = send, recv, 0, []

    def remote(self, src, dst, device):
        i, self.used = self.used, self.used + 1
        copy = pltpu.make_async_remote_copy(
            src_ref=src, dst_ref=dst, send_sem=self.send.at[i], recv_sem=self.recv.at[i],
            device_id=device, device_id_type=MESH,
        )
        copy.start()
        self.started.append(copy)
        return copy

    def local(self, src, dst):
        i, self.used = self.used, self.used + 1
        copy = pltpu.make_async_copy(src, dst, self.recv.at[i])
        copy.start()
        return copy

    def finish(self):
        for copy in self.started:
            copy.wait_send()


FAR_FIRST = (2, 1, 3)
NEXT = (1, 3)


class Gather:
    def __init__(self, copies, source, held, slot, ring, place_in_ring, across):
        self.copies, self.source, self.held, self.slot = copies, source, held, slot
        self.ring, self.place, self.across = ring, place_in_ring, across
        self.first, self.last = {}, []

    def tiles(self, side, step, first=0, count=4):
        return self.held.at[pl.ds(self.slot(side, (self.place + step) % 4) * 4 + first, count)]

    def over(self):
        mine = self.tiles(0, 0)
        self.kept = self.copies.local(self.source, mine)
        self.crossing = self.copies.remote(self.source, mine, self.across)

    def own(self):
        self.first[0] = [self.copies.remote(self.source, self.tiles(0, 0), self.ring(d)) for d in NEXT]

    def onward(self):
        self.crossing.wait_recv()
        block = self.tiles(1, 0)
        self.first[1] = [self.copies.remote(block, block, self.ring(d)) for d in NEXT]

    def pass_on(self, side):
        for copy, d in zip(self.first[side], NEXT):
            copy.wait_recv()
            half = self.tiles(side, -d, 0 if d == 1 else 2, 2)
            self.last.append(self.copies.remote(half, half, self.ring(d)))

    def wait(self):
        self.kept.wait()
        for copy in self.last:
            copy.wait_recv()


class Sum:
    def __init__(self, copies, part, base, via, near, cross, crossed, ring, place_in_ring, side, across):
        self.copies, self.part, self.base, self.via, self.near = copies, part, base, via, near
        self.cross, self.crossed, self.ring, self.place = cross, crossed, ring, place_in_ring
        self.side, self.across = side, across

    def at(self, step, first=0):
        return self.base + (self.place + step) % 4 * 8 + first

    def far(self):
        self.vias = []
        for d, first in zip(NEXT, (0, 4)):
            self.vias.append(
                self.copies.remote(
                    self.part.at[pl.ds(self.at(2, first), 4)], self.via.at[pl.ds(first, 4)], self.ring(d)
                )
            )

    def hop(self):
        self.nears = []
        for n, (d, first) in enumerate(zip(NEXT, (0, 4))):
            start = self.at(d, first)

            def one(i, carry):
                self.part[start + i] = (self.part[start + i].astype(F32) + self.via[first + i].astype(F32)).astype(BF16)
                return carry

            self.vias[n].wait_recv()
            lax.fori_loop(0, 4, one, 0)
            self.nears.append(
                self.copies.remote(self.part.at[pl.ds(self.at(d), 8)], self.near.at[pl.ds(n * 8, 8)], self.ring(d))
            )

    def total(self, side, i):
        total = (
            self.part[self.at(0, side * 4 + i)].astype(F32)
            + self.near[side * 4 + i].astype(F32)
            + self.near[8 + side * 4 + i].astype(F32)
        )
        return total

    def over(self):
        for copy in self.nears:
            copy.wait_recv()

        def one(i, carry):
            self.cross[i] = self.total(1 - self.side, i).astype(BF16)
            return carry

        lax.fori_loop(0, 4, one, 0)
        self.crossing = self.copies.remote(self.cross, self.crossed, self.across)

    def finish(self, body):
        self.crossing.wait_recv()

        def one(i, carry):
            body(i, self.total(self.side, i) + self.crossed[i].astype(F32))
            return carry

        lax.fori_loop(0, 4, one, 0)


def held_tile(col):
    block = lax.shift_right_logical(col, 2)
    half = (block & 1) * 8 + lax.shift_right_logical(block, 3) * 4 + (lax.shift_right_logical(block, 1) & 3)
    return half * 4 + (col & 3)


def forward_kernel(
    cols_ref, cols_row, nodes, position, degree, features, cotangent, mask_hbm,
    out_ref, x_ref, node_extra, own_col, node_row, tables, mask, *rest
):
    held, part, near, cross, crossed, (send, recv) = (
        rest[0:4], rest[4:8], rest[8:12], rest[12:16], rest[16:20], rest[20:22]
    )
    xl, y, xh, z, k = place()
    copies = Copies(send, recv)
    mask_copy = copies.local(mask_hbm, mask)
    packing, unpacking, flat, flat_extra = rest[22:26]
    relays = [Relay(rest[26], rest[27], rest[28]), Relay(rest[29], rest[30], rest[31])]
    extra_relay = Relay(rest[32], rest[33], rest[34])
    extra, side, node_col = rest[35:38]
    width = features.shape[1]
    greet()
    lane = lax.broadcasted_iota(jnp.int32, nodes.shape, 1)
    dest = nodes[...] // width
    own_row = dest * 8 + rank_row(dest, lane, side)
    pick_rows(packing, own_row)
    relays[0].pack(packing, features, 0)
    meet()
    relays[0].start()
    relays[1].pack(packing, features, 256)
    relays[1].start()
    source = position[...] // width
    node_slot = source * 8 + rank_row(source, position[...], side)
    node_row[...] = node_slot
    node_col[...] = upright(node_slot)[:, :1]
    pick_slots(unpacking, node_col)
    own_col[...] = upright(own_row)[:, :1]
    column_tables(cols_row[...], tables)
    extra[:, pl.ds(0, width)] = cotangent[...]
    extra[:, pl.ds(width, 128)] = upright(degree[...]).astype(F32).astype(BF16)
    extra_relay.pack(packing, extra, 0)

    def unpack(c):
        if c % 2 == 0:
            relays[c // 2].collect(flat)

        def one(i, at):
            rows = jnp.dot(unpacking[at], flat[:, pl.ds(c % 2 * 128, 128)], preferred_element_type=F32)
            x_ref[c, i] = rows.astype(BF16)

        each_block(4, one)

    def unpack_extra():
        extra_relay.collect(flat_extra)

        def one(i, at):
            node_extra[at] = jnp.dot(unpacking[at], flat_extra[...], preferred_element_type=F32).astype(BF16)

        each_block(4, one)

    tiles = lambda slot: pl.ds(slot * 4, 4)
    mine, pair = k * 8 + xh * 4 + z, k * 8 + (1 - xh) * 4 + z
    gathered, over, swap, row_copies, cross_copy = [[] for _ in range(4)], {}, {}, {}, {}

    def own(c):
        gathered[c].append(copies.local(x_ref.at[c], held[c].at[tiles(mine)]))
        over[c] = copies.remote(x_ref.at[c], held[c].at[tiles(mine)], at_device(xl, y, 1 - xh, z, k))
        for d in FAR_FIRST:
            to = at_device(xl, y, xh, (z + d) % 4, k)
            gathered[c].append(copies.remote(x_ref.at[c], held[c].at[tiles(mine)], to))

    def onward(c):
        over[c].wait_recv()
        for d in FAR_FIRST:
            to = at_device(xl, y, xh, (z + d) % 4, k)
            gathered[c].append(copies.remote(held[c].at[tiles(pair)], held[c].at[tiles(pair)], to))

    def swap_cores(c):
        gathered[c][0].wait()
        for copy in gathered[c][1:]:
            copy.wait_recv()
        half = held[c].at[pl.ds(k * 32, 32)]
        swap[c] = copies.remote(half, half, at_device(xl, y, xh, z, 1 - k))

    def product(c):
        swap[c].wait_recv()
        row_copies[c] = []
        for d in FAR_FIRST + (0,):
            to_y = (y + d) % 4

            def one(q, carry):
                t = (q // 4) * 16 + to_y * 4 + q % 4
                left = jnp.concatenate([mask[t * 8 + j] for j in range(8)], axis=1)
                right = jnp.concatenate([held[c][held_tile(cols_ref[t * 8 + j])] for j in range(8)], axis=0)
                part[c][to_y * 8 + q] = jnp.dot(left, right, preferred_element_type=F32).astype(BF16)
                return carry

            lax.fori_loop(0, 8, one, 0)
            if d:
                i = FAR_FIRST.index(d)
                row_copies[c].append(
                    copies.remote(
                        part[c].at[pl.ds(to_y * 8, 8)], near[c].at[pl.ds(i * 8, 8)], at_device(xl, to_y, xh, z, k)
                    )
                )

    def row_sum(c, side, i):
        total = part[c][y * 8 + side * 4 + i].astype(F32)
        for n in range(3):
            total = total + near[c][n * 8 + side * 4 + i].astype(F32)
        return total

    def sum_rows(c):
        for copy in row_copies[c]:
            copy.wait_recv()

        def one(i, carry):
            cross[c][i] = row_sum(c, 1 - xl, i).astype(BF16)
            return carry

        lax.fori_loop(0, 4, one, 0)
        cross_copy[c] = copies.remote(cross[c], crossed[c], at_device(1 - xl, y, xh, z, k))

    def sum_cross(c):
        cross_copy[c].wait_recv()

        def one(i, carry):
            out_ref[c, i] = row_sum(c, xl, i) + crossed[c][i].astype(F32)
            return carry

        lax.fori_loop(0, 4, one, 0)

    unpack(0)
    own(0)
    unpack(1)
    onward(0)
    own(1)
    unpack(2)
    onward(1)
    swap_cores(0)
    own(2)
    unpack(3)
    mask_copy.wait()
    product(0)
    onward(2)
    swap_cores(1)
    own(3)
    product(1)
    onward(3)
    swap_cores(2)
    extra_relay.start()
    sum_rows(0)
    product(2)
    swap_cores(3)
    sum_rows(1)
    sum_cross(0)
    product(3)
    sum_rows(2)
    sum_cross(1)
    unpack_extra()
    sum_rows(3)
    sum_cross(2)
    sum_cross(3)
    copies.finish()
    for relay in relays + [extra_relay]:
        relay.finish()


def remote_params(ident):
    return params(collective_id=ident, has_side_effects=True)


SMEM_SPEC = pl.BlockSpec(memory_space=pltpu.SMEM)
VMEM_SPEC = pl.BlockSpec(memory_space=pltpu.VMEM)
ANY_SPEC = pl.BlockSpec(memory_space=pl.ANY)


def tile_buffer(count):
    return pltpu.VMEM((count, 128, 128), BF16)


def boxes(width):
    return [
        pltpu.VMEM((DEVICES, 8, width), BF16),
        pltpu.VMEM((DEVICES, 8, width), BF16),
        pltpu.SemaphoreType.DMA((3,)),
    ]


def forward_exchange(cols, nodes, position, degree, features, cotangent, masks):
    rows, width = features.shape
    slots, wide = DEVICES * 8, width + 128
    tiled = (4, 4, 128, 128)
    count = cols.shape[0]
    as_row = lambda values: values.reshape(1, -1)
    return pl.pallas_call(
        forward_kernel,
        in_specs=[SMEM_SPEC] + [VMEM_SPEC] * 6 + [ANY_SPEC],
        out_specs=[VMEM_SPEC] * 6,
        out_shape=[
            jax.ShapeDtypeStruct(tiled, F32),
            jax.ShapeDtypeStruct(tiled, BF16),
            jax.ShapeDtypeStruct((rows, wide), BF16),
            jax.ShapeDtypeStruct((rows, 1), jnp.int32),
            jax.ShapeDtypeStruct((1, rows), jnp.int32),
            jax.ShapeDtypeStruct((8, count), jnp.int32),
        ],
        scratch_shapes=[tile_buffer(256)]
        + [tile_buffer(64)] * 4
        + [tile_buffer(32)] * 4
        + [tile_buffer(24)] * 4
        + [tile_buffer(4)] * 8
        + [pltpu.SemaphoreType.DMA((64,)), pltpu.SemaphoreType.DMA((64,))]
        + [pltpu.VMEM((slots, rows), BF16), pltpu.VMEM((rows, slots), BF16)]
        + [pltpu.VMEM((slots, width // 2), BF16), pltpu.VMEM((slots, wide), BF16)]
        + boxes(width // 2) * 2
        + boxes(wide)
        + [pltpu.VMEM((rows, wide), BF16), pltpu.VMEM((2, rows, 128), jnp.int32), pltpu.VMEM((rows, 1), jnp.int32)],
        compiler_params=remote_params(0),
        name="forward_exchange",
    )(cols, as_row(cols), as_row(nodes), as_row(position), as_row(degree), features, cotangent, masks)


def backward_kernel(
    scale, tables, node_row, own_col, summed, x_ref, extra, self_weight, neigh_weight, mask_hbm,
    hidden_out, grad_out, sum_ref, mask, chain, hidden, own_back, s_ref, g_ref, slopes, aggregate, *rest
):
    held, block, traded, via, near, cross, crossed = [rest[i : i + 4] for i in range(0, 28, 4)]
    send, recv = rest[28:30]
    rest = rest[4:]
    g_core, g_traded, g_half, g_quarter, g_part, g_eighth, g_piece = rest[26:33]
    xl, y, xh, z, k = place()
    copies = Copies(send, recv)
    mask_copy = copies.local(mask_hbm, mask)
    packing, unpacking, flat, joined = rest[33:37]
    hidden_relay = Relay(rest[37], rest[38], rest[39])
    relays = [Relay(rest[i], rest[i + 1], rest[i + 2]) for i in (40, 43)]
    greet()
    each_big = lambda body: lax.fori_loop(0, 2, lambda i, carry: body(i, pl.ds(pl.multiple_of(i * 256, 256), 256)), 0)

    def dense_front(i, at):
        whole = lambda ref: jnp.concatenate([ref[c, pl.ds(i * 2, 2)].reshape(256, 128) for c in range(4)], axis=1)
        degrees = extra[at, pl.ds(512, 1)].astype(F32)
        mean = (whole(summed) / degrees).astype(BF16)
        aggregate[at] = mean
        preact = jnp.dot(whole(x_ref), self_weight[...], preferred_element_type=F32) + jnp.dot(
            mean, neigh_weight[...], preferred_element_type=F32
        )
        gate = jax.nn.sigmoid(preact)
        hidden[at] = (preact * gate).astype(BF16)
        slope = (extra[at, pl.ds(0, 512)].astype(F32) * gate * (1.0 + preact * (1.0 - gate))).astype(BF16)
        slopes[at] = slope
        spread = lax.dot_general(slope, neigh_weight[...], COL_T, preferred_element_type=F32) / degrees
        for c in range(4):
            for n in range(2):
                s_ref[c, i * 2 + n] = spread[n * 128 : (n + 1) * 128, c * 128 : (c + 1) * 128].T.astype(BF16)
        return 0

    def dense_own(i, at):
        own_back[at] = lax.dot_general(slopes[at], self_weight[...], COL_T, preferred_element_type=F32)
        return 0

    def dense_grads(c, at):
        columns = x_ref[c].reshape(512, 128)
        g_ref[at] = lax.dot_general(columns, slopes[...], ROW_T, preferred_element_type=F32)
        means = aggregate[:, pl.ds(pl.multiple_of(c * 128, 128), 128)]
        below = pl.ds(pl.multiple_of(512 + c * 128, 128), 128)
        g_ref[below] = lax.dot_general(means, slopes[...], ROW_T, preferred_element_type=F32)

    each_big(dense_front)
    meet()
    ring_z = lambda d: at_device(xl, y, xh, (z + d) % 4, k)
    ring_y = lambda d: at_device(xl, (y + d) % 4, xh, z, k)
    slot = lambda side, at: (xl + side) % 2 * 4 + at
    gather = [
        Gather(copies, s_ref.at[c], held[c], slot, ring_y, y, at_device(1 - xl, y, xh, z, k)) for c in range(4)
    ]
    cols = [
        Sum(
            copies, block[c], k * 32, via[c], near[c], cross[c], crossed[c], ring_z, z, xh,
            at_device(xl, y, 1 - xh, z, k),
        )
        for c in range(4)
    ]
    trade = {}

    def product(c, *between):
        gather[c].wait()

        def one(g, total):
            for u in range(8):
                e = g * 8 + u
                piece = jnp.dot(held[c][tables[1, e]], mask[tables[0, e]], preferred_element_type=F32)
                total = total * tables[2, e].astype(F32) + piece
                chain[e] = total.astype(BF16)
            return total

        total = jnp.zeros((128, 128), F32)
        for n in range(4):
            total = lax.fori_loop(n * 8, n * 8 + 8, one, total)
            for action in between[n : n + 1]:
                action()

        def settle(p, carry):
            block[c][p] = (chain[tables[3, p]].astype(F32) * tables[4, p].astype(F32)).astype(BF16)
            return carry

        lax.fori_loop(0, 64, settle, 0)
        trade[c] = copies.remote(
            block[c].at[pl.ds((1 - k) * 32, 32)], traded[c], at_device(xl, y, xh, z, 1 - k)
        )

    def sum_cores(c):
        trade[c].wait_recv()

        def one(i, carry):
            block[c][k * 32 + i] = (block[c][k * 32 + i].astype(F32) + traded[c][i].astype(F32)).astype(BF16)
            return carry

        lax.fori_loop(0, 32, one, 0)
        cols[c].far()

    def finish(c):
        def body(i, total):
            at = (pl.ds(pl.multiple_of(i * 128, 128), 128), pl.ds(c * 128, 128))
            joined[at] = (own_back[at] + total.T).astype(BF16)

        cols[c].finish(body)

    width = g_ref.shape[1]
    quarter_at = k * 512 + z * 128
    x_index = xl * 2 + xh
    x_others = [((xl + a) % 2, (xh + b) % 2) for a, b in ((1, 1), (0, 1), (1, 0))]
    level = {}

    def blocks(count, size, body):
        def one(i, carry):
            body(pl.ds(pl.multiple_of(i * size, size), size), i * size)
            return carry

        lax.fori_loop(0, count, one, 0)

    def rows_of(base, offset, size):
        return pl.ds(pl.multiple_of(base + offset, size), size)

    def grad_core():
        def body(at, offset):
            g_core[at] = g_ref[rows_of((1 - k) * 512, offset, 64)].astype(BF16)

        blocks(8, 64, body)
        level["core"] = copies.remote(g_core, g_traded, at_device(xl, y, xh, z, 1 - k))

    def grad_z():
        level["core"].wait_recv()

        def body(at, offset):
            g_half[at] = (g_ref[rows_of(k * 512, offset, 64)] + g_traded[at].astype(F32)).astype(BF16)

        blocks(8, 64, body)
        level["z"] = []
        for i, d in enumerate(FAR_FIRST):
            to_z = (z + d) % 4
            level["z"].append(
                copies.remote(g_half.at[rows_of(0, to_z * 128, 128)], g_quarter.at[i], at_device(xl, y, xh, to_z, k))
            )

    def grad_y():
        for copy in level["z"]:
            copy.wait_recv()

        def body(at, offset):
            total = g_ref[rows_of(quarter_at, offset, 32)] + g_traded[rows_of(z * 128, offset, 32)].astype(F32)
            for i in range(3):
                total = total + g_quarter[i, at].astype(F32)
            g_part[0, at] = total

        blocks(4, 32, body)
        level["y"] = []
        for i, d in enumerate(FAR_FIRST):
            to_y = (y + d) % 4
            level["y"].append(
                copies.remote(g_part.at[0, rows_of(0, to_y * 32, 32)], g_eighth.at[i], at_device(xl, to_y, xh, z, k))
            )

    def grad_x():
        for copy in level["y"]:
            copy.wait_recv()
        total = g_part[0, rows_of(0, y * 32, 32)]
        for i in range(3):
            total = total + g_eighth[i]
        g_eighth_sum = g_piece.at[0]
        g_eighth_sum[...] = total
        level["x"] = []
        for i, (a, b) in enumerate(x_others):
            at = rows_of(0, (a * 2 + b) * 8, 8)
            level["x"].append(copies.remote(g_eighth_sum.at[at], g_piece.at[1, pl.ds(i * 8, 8)], at_device(a, y, b, z, k)))

    def grad_total():
        for copy in level["x"]:
            copy.wait_recv()
        total = g_piece[0, rows_of(0, x_index * 8, 8)]
        for i in range(3):
            total = total + g_piece[1, pl.ds(i * 8, 8)]
        at = (k, z, y, rows_of(0, x_index * 8, 8))
        sum_ref[at] = total * scale
        level["to_x"] = [copies.remote(sum_ref.at[at], sum_ref.at[at], at_device(a, y, b, z, k)) for a, b in x_others]

    def grad_to_z():
        for copy in level["to_x"]:
            copy.wait_recv()
        at = sum_ref.at[k, z, y]
        level["to_z"] = [copies.remote(at, at, at_device(xl, y, xh, (z + d) % 4, k)) for d in FAR_FIRST]

    def grad_to_y():
        for copy in level["to_z"]:
            copy.wait_recv()
        at = sum_ref.at[k, :, y]
        level["to_y"] = [copies.remote(at, at, at_device(xl, (y + d) % 4, xh, z, k)) for d in FAR_FIRST]

    def grad_to_core():
        for copy in level["to_y"]:
            copy.wait_recv()
        level["to_core"] = copies.remote(sum_ref.at[k], sum_ref.at[k], at_device(xl, y, xh, z, 1 - k))

    def take(relay, out, first):
        relay.collect(flat)

        def one(i, at):
            rows = jnp.dot(unpacking[at], flat[:, pl.ds(0, relay.width)], preferred_element_type=F32)
            out[at, pl.ds(first, relay.width)] = rows.astype(BF16)

        each_block(4, one)

    def send(relay, first):
        relay.pack(packing, joined, first)
        relay.start()

    def steps(*actions):
        def run():
            for action in actions:
                action()

        return run

    def passing(c, side):
        return lambda: gather[c].pass_on(side)

    def paired(c):
        return lambda: sum_cores(c)

    for c in range(4):
        gather[c].over()
    gather[0].own()
    pick_rows(packing, node_row[...])
    gather[0].onward()
    hidden_relay.pack(packing, hidden, 0)
    gather[0].pass_on(0)
    gather[0].pass_on(1)
    gather[1].own()
    gather[1].onward()
    each_block(4, dense_grads)
    grad_core()
    each_big(dense_own)
    pick_slots(unpacking, own_col)
    mask_copy.wait()
    product(
        0,
        steps(passing(1, 0), grad_z),
        steps(passing(1, 1), gather[2].own),
        gather[2].onward,
    )
    product(
        1,
        steps(paired(0), passing(2, 0), grad_y),
        steps(passing(2, 1), gather[3].own, gather[3].onward),
        steps(cols[0].hop, grad_x),
    )
    product(
        2,
        steps(paired(1), passing(3, 0)),
        steps(passing(3, 1), cols[0].over, hidden_relay.start),
        steps(cols[1].hop, grad_total),
    )
    product(
        3,
        steps(paired(2), lambda: finish(0)),
        steps(cols[1].over, grad_to_z),
        steps(cols[2].hop, lambda: finish(1), lambda: send(relays[0], 0)),
    )
    sum_cores(3)
    grad_to_y()
    cols[2].over()
    cols[3].hop()
    take(hidden_relay, hidden_out, 0)
    finish(2)
    cols[3].over()
    grad_to_core()
    finish(3)
    send(relays[1], 256)
    take(relays[0], grad_out, 0)
    take(relays[1], grad_out, 256)
    level["to_core"].wait_recv()
    copies.finish()
    for relay in relays + [hidden_relay]:
        relay.finish()


def backward_exchange(tables, node_row, own_col, summed, x, extra, self_weight, neigh_weight, masks, scale):
    rows, width = extra.shape[0], self_weight.shape[0]
    slots = DEVICES * 8
    return pl.pallas_call(
        functools.partial(backward_kernel, scale),
        in_specs=[SMEM_SPEC] + [VMEM_SPEC] * 7 + [ANY_SPEC],
        out_specs=[VMEM_SPEC] * 3,
        out_shape=[
            jax.ShapeDtypeStruct((rows, width), BF16),
            jax.ShapeDtypeStruct((rows, width), BF16),
            jax.ShapeDtypeStruct((2, 4, 4, 32, width), F32),
        ],
        scratch_shapes=[tile_buffer(256), tile_buffer(256)]
        + [pltpu.VMEM((rows, width), BF16), pltpu.VMEM((rows, width), F32), pltpu.VMEM(x.shape, BF16)]
        + [pltpu.VMEM((2 * rows, width), F32), pltpu.VMEM((rows, width), BF16), pltpu.VMEM((rows, width), BF16)]
        + [tile_buffer(32)] * 4
        + [tile_buffer(64)] * 4
        + [tile_buffer(32)] * 4
        + [tile_buffer(8)] * 4
        + [tile_buffer(16)] * 4
        + [tile_buffer(4)] * 8
        + [pltpu.SemaphoreType.DMA((128,)), pltpu.SemaphoreType.DMA((128,))]
        + [pltpu.VMEM((512, 512), BF16)] * 3
        + [pltpu.VMEM((3, 128, 512), BF16), pltpu.VMEM((1, 128, 512), F32)]
        + [pltpu.VMEM((3, 32, 512), F32), pltpu.VMEM((2, 32, 512), F32)]
        + [pltpu.VMEM((slots, rows), BF16), pltpu.VMEM((rows, slots), BF16)]
        + [pltpu.VMEM((slots, width), BF16), pltpu.VMEM((rows, width), BF16)]
        + boxes(width)
        + boxes(width // 2) * 2,
        compiler_params=remote_params(1),
        name="backward_exchange",
    )(tables, node_row, own_col, summed, x, extra, self_weight, neigh_weight, masks)


def on_device(
    features, tile_cols, tile_masks, degree, owner_nodes, owner_position, self_weight, neigh_weight, cotangent
):
    rows, width = features.shape
    masks = tile_masks.reshape(-1, *tile_masks.shape[-2:])
    summed, node_x, node_extra, own_col, node_row, tables = forward_exchange(
        tile_cols.reshape(-1), owner_nodes, owner_position, degree, features, cotangent, masks
    )
    grad_scale = 1.0 / math.sqrt(rows * DEVICES)
    hidden_out, grad_out, sums = backward_exchange(
        tables, node_row, own_col, summed, node_x, node_extra, self_weight, neigh_weight, masks, grad_scale
    )
    sums = sums.reshape(2, width, width)
    return hidden_out, grad_out, sums[0], sums[1]


def solution(mesh):
    both = P(("row", "col"))
    wide = P(("row", "col"), None)
    placed = (
        wide,
        P("row", "col", None, None),
        P("row", "col", None, None, None, None),
        both,
        both,
        both,
        P(),
        P(),
        wide,
    )
    return jax.shard_map(
        on_device, mesh=mesh, in_specs=placed, out_specs=(wide, wide, P(), P()), check_vma=False
    )
```
